32 devices in a mesh: tm: 2 (over x), row: 4 (over z), col: 4 (over y, core).
Axes of the slice: x: 2, y: 2, z: 4, core: 2. Of those that a mesh axis runs over, the one named last changes fastest.
Arguments:
- features: bfloat16 [4, 60, 104, 128], P('tm', 'row', 'col'), may hold values from -13 to 13
- cotangent: bfloat16 [4, 60, 104, 128], P('tm', 'row', 'col'), may hold values from -7 to 7
- conv_one: bfloat16 [27, 128, 128], replicated, may hold values from -0.109375 to 0.109375
- conv_two: bfloat16 [27, 128, 128], replicated, may hold values from -0.109375 to 0.109375
- gain_one: float32 [128], replicated, may hold values from 0.25 to 1.75
- shift_one: float32 [128], replicated, may hold values from -0.6 to 0.6
- gain_two: float32 [128], replicated, may hold values from 0.25 to 1.75
- shift_two: float32 [128], replicated, may hold values from -0.6 to 0.6
Outputs:
- block_out: bfloat16 [4, 60, 104, 128], P('tm', 'row', 'col')
- grad_input: bfloat16 [4, 60, 104, 128], P('tm', 'row', 'col')
- grad_conv_one: float32 [27, 128, 128], replicated
- grad_conv_two: float32 [27, 128, 128], replicated
The draws below stay inside these ranges and needn't reach their ends.
All inputs are finite; a program needn't handle non-finite values.
Results may differ from the reference program's by a relative error of at most 0.0034.
Values may be sent and summed in bfloat16 or wider, within the bound.
A program may use at most 128 MiB of HBM per device.

```python
import jax
import jax.numpy as jnp
from jax import lax

C = 128
GROUPS = 32
TAPS = 27
FRAMES = 4
HEIGHT = 60
WIDTH = 104


def spatial_ramps():
    frame_pos = jnp.arange(FRAMES, dtype=jnp.float32) / max(FRAMES - 1, 1)
    row_pos = jnp.arange(HEIGHT, dtype=jnp.float32) / max(HEIGHT - 1, 1)
    col_pos = jnp.arange(WIDTH, dtype=jnp.float32) / max(WIDTH - 1, 1)
    return (frame_pos, row_pos, col_pos)


def draw_features(key, part):
    key_base, key_offset = jax.random.split(jax.random.fold_in(key, 11), 2)
    shape_full = (FRAMES, HEIGHT, WIDTH, C)
    frame_pos, row_pos, col_pos = spatial_ramps()
    frame_factor = 1.0 + 2.0 * frame_pos
    row_factor = 0.4 + 0.6 * row_pos
    col_factor = 1.0 - 0.6 * col_pos
    factor = frame_factor[:, None, None] * row_factor[None, :, None] * col_factor[None, None, :]
    place_offset = 0.5 * (col_pos[None, :] - row_pos[:, None])
    offset = 0.5 * jax.random.uniform(key_offset, (C,), jnp.float32, -1.0, 1.0)
    base = jnp.clip(jax.random.normal(key_base, shape_full, jnp.float32), -4.0, 4.0)
    values = base * factor[:, :, :, None] + place_offset[None, :, :, None] + offset
    return values.astype(jnp.bfloat16)


def draw_cotangent(key, part):
    key_noise, key_offset = jax.random.split(jax.random.fold_in(key, 23), 2)
    shape_full = (FRAMES, HEIGHT, WIDTH, C)
    frame_pos, row_pos, col_pos = spatial_ramps()
    reach = 0.25 + 0.5 * (frame_pos[:, None, None] + row_pos[None, :, None] + col_pos[None, None, :])
    offset = jax.random.uniform(key_offset, (C,), jnp.float32, -1.0, 1.0)
    noise = jnp.clip(jax.random.normal(key_noise, shape_full, jnp.float32), -5.0, 5.0)
    values = noise + reach[:, :, :, None] * offset
    return values.astype(jnp.bfloat16)


def centred(own_key, dims, scale, most, held_as=jnp.bfloat16):
    result = jax.random.normal(own_key, dims, jnp.float32) * scale
    return jnp.minimum(jnp.maximum(result, -most), most).astype(held_as)


def setup_inputs(seed: int = 0) -> dict:
    splits = jax.random.split(jax.random.key(seed), 9)
    features = draw_features(jax.random.fold_in(splits[8], 71), 0)
    cotangent = draw_cotangent(jax.random.fold_in(splits[8], 71), 0)
    conv_one = centred(splits[2], (TAPS, C, C), (TAPS * C) ** -0.5, 0.109375)
    conv_two = centred(splits[3], (TAPS, C, C), (TAPS * C) ** -0.5, 0.109375)
    gain_one = jnp.clip(1.0 + 0.15 * jax.random.normal(splits[4], (C,), jnp.float32), 0.25, 1.75)
    shift_one = jnp.clip(jax.random.uniform(splits[5], (C,), jnp.float32, -0.6, 0.6), -0.6, 0.6)
    gain_two = jnp.clip(1.0 + 0.15 * jax.random.normal(splits[6], (C,), jnp.float32), 0.25, 1.75)
    shift_two = jnp.clip(jax.random.uniform(splits[7], (C,), jnp.float32, -0.6, 0.6), -0.6, 0.6)
    return dict(features=features, cotangent=cotangent, conv_one=conv_one, conv_two=conv_two, gain_one=gain_one, shift_one=shift_one, gain_two=gain_two, shift_two=shift_two)


epsilon = 1e-05

def unfold_taps(padded, frames, height, width):
    pieces = []
    for frame_off in range(3):
        for row_off in range(3):
            for col_off in range(3):
                pieces.append(padded[frame_off:frame_off + frames, row_off:row_off + height, col_off:col_off + width])
    stacked = jnp.concatenate(pieces, axis=3)
    return stacked.reshape(frames * height * width, stacked.shape[3])

def statistics(values):
    per_group = C // GROUPS
    members = FRAMES * HEIGHT * WIDTH * per_group
    grouped = values.reshape(-1, GROUPS, per_group)
    average = lax.optimization_barrier(jnp.sum(grouped, axis=(0, 2))) / members
    centered = grouped - average[None, :, None]
    variance = lax.optimization_barrier(jnp.sum(centered * centered, axis=(0, 2))) / members
    return (jnp.repeat(average, per_group), jnp.repeat(lax.rsqrt(variance + epsilon), per_group))

def group_means(first, second):
    per_group = C // GROUPS
    members = FRAMES * HEIGHT * WIDTH * per_group
    mean_first = lax.optimization_barrier(jnp.sum(first.reshape(-1, GROUPS, per_group), axis=(0, 2))) / members
    mean_second = lax.optimization_barrier(jnp.sum(second.reshape(-1, GROUPS, per_group), axis=(0, 2))) / members
    return (jnp.repeat(mean_first, per_group), jnp.repeat(mean_second, per_group))

def silu_slope(normed):
    sigm = jax.nn.sigmoid(normed)
    return sigm * (1.0 + normed * (1.0 - sigm))

def conv_frames(padded, kernel_flat):
    kernel_wide = kernel_flat.astype(jnp.float32)

    def one_frame(start):
        window = lax.dynamic_slice_in_dim(padded, start, 3, 0)
        columns = unfold_taps(window, 1, HEIGHT, WIDTH).astype(jnp.float32)
        return jnp.dot(columns, kernel_wide, precision=lax.Precision.HIGHEST)
    rows_out = lax.map(one_frame, jnp.arange(FRAMES, dtype=jnp.int32))
    return rows_out.reshape(FRAMES, HEIGHT, WIDTH, C)

def kernel_grad(padded, grad):

    def one_frame(carry, start):
        window = lax.dynamic_slice_in_dim(padded, start, 3, 0)
        columns = unfold_taps(window, 1, HEIGHT, WIDTH).astype(jnp.float32)
        frame_grad = lax.dynamic_index_in_dim(grad, start, 0, keepdims=False).reshape(HEIGHT * WIDTH, C).astype(jnp.float32)
        term = lax.dot_general(columns, frame_grad, (((0,), (0,)), ((), ())), precision=lax.Precision.HIGHEST)
        return (carry + term, None)
    summed, unused = lax.scan(one_frame, jnp.zeros((TAPS * C, C), jnp.float32), jnp.arange(FRAMES, dtype=jnp.int32))
    return summed.reshape(TAPS, C, C)

def pad_past(values):
    return jnp.pad(values, ((2, 0), (1, 1), (1, 1), (0, 0)))

def pad_future(values):
    return jnp.pad(values, ((0, 2), (1, 1), (1, 1), (0, 0)))

def flipped(kernel):
    return jnp.flip(kernel, 0).transpose(0, 2, 1).reshape(TAPS * C, C)

def reference(features, cotangent, conv_one, conv_two, gain_one, shift_one, gain_two, shift_two):
    inputs_wide = features.astype(jnp.float32)
    average_one, scale_one = statistics(inputs_wide)
    unit_one = (inputs_wide - average_one) * scale_one
    normed_one = unit_one * gain_one + shift_one
    acted_one = jax.nn.silu(normed_one).astype(jnp.bfloat16)
    padded_one = pad_past(acted_one)
    hidden = conv_frames(padded_one, conv_one.reshape(TAPS * C, C))
    average_two, scale_two = statistics(hidden)
    unit_two = (hidden - average_two) * scale_two
    normed_two = unit_two * gain_two + shift_two
    acted_two = jax.nn.silu(normed_two).astype(jnp.bfloat16)
    padded_two = pad_past(acted_two)
    block_out = (inputs_wide + conv_frames(padded_two, conv_two.reshape(TAPS * C, C))).astype(jnp.bfloat16)
    grad_conv_two = kernel_grad(padded_two, cotangent)
    back_two = conv_frames(pad_future(cotangent), flipped(conv_two))
    lifted_two = back_two * silu_slope(normed_two) * gain_two
    mean_first, mean_second = group_means(lifted_two, lifted_two * unit_two)
    grad_hidden = (scale_two * (lifted_two - mean_first - unit_two * mean_second)).astype(jnp.bfloat16)
    grad_conv_one = kernel_grad(padded_one, grad_hidden)
    back_one = conv_frames(pad_future(grad_hidden), flipped(conv_one))
    lifted_one = back_one * silu_slope(normed_one) * gain_one
    mean_first, mean_second = group_means(lifted_one, lifted_one * unit_one)
    grad_input = (cotangent.astype(jnp.float32) + scale_one * (lifted_one - mean_first - unit_one * mean_second)).astype(jnp.bfloat16)
    return (block_out, grad_input, grad_conv_one, grad_conv_two)
```

```python
import functools

import jax
import jax.numpy as jnp
from jax import lax
from jax.experimental import pallas as pl
from jax.experimental.pallas import tpu as pltpu
from jax.sharding import PartitionSpec as P

GROUPS = 32
EPSILON = 1e-05
MESH = pl.DeviceIdType.MESH
F32 = jnp.float32
BF16 = jnp.bfloat16
AXES = ("tm", "row", "col")


class Plan:
    def __init__(self, f, h, w, c, sizes):
        self.f, self.h, self.w, self.c = f, h, w, c
        self.wp = 16
        while self.wp < w + 2:
            self.wp *= 2
        self.n = f * h * self.wp
        self.hp = h + 2
        self.np = (f + 2) * self.hp * self.wp
        self.cb = -(-(f * h) // 16) * 16
        self.rb = 2 * self.wp
        self.ntm, self.nrow, self.ncol = sizes
        self.na = self.nrow
        self.nb = self.ntm * self.ncol
        self.taps_rows = 27 * c
        unit = 16 * self.ntm * self.nrow * self.ncol
        units = -(-self.taps_rows // unit)
        first = -(-units // 2)
        self.sum_rows = units * unit
        self.parts = [(0, first * unit)]
        if units > first:
            self.parts.append((first * unit, (units - first) * unit))

    def stages(self, order):
        near = 2 if self.ncol % 2 == 0 else 1
        known = dict(
            near=("col", 1, near, True),
            col=("col", near, self.ncol // near, False),
            tm=("tm", 1, self.ntm, False),
            row=("row", 1, self.nrow, False),
        )
        return [known[name] for name in order if known[name][2] > 1]


class Link:
    def __init__(self, src, dst, sems, index, device, sends, receives):
        self.make = lambda: pltpu.make_async_remote_copy(
            src_ref=src,
            dst_ref=dst,
            send_sem=sems[0].at[index],
            recv_sem=sems[1].at[index],
            device_id=device,
            device_id_type=MESH,
        )
        self.sends, self.receives = sends, receives

    def start(self):
        if self.sends is None:
            self.make().start()
            return

        @pl.when(self.sends)
        def _():
            self.make().start()

    def wait_send(self):
        if self.sends is None:
            self.make().wait_send()
            return

        @pl.when(self.sends)
        def _():
            self.make().wait_send()

    def wait_recv(self):
        if self.receives is None:
            self.make().wait_recv()
            return

        @pl.when(self.receives)
        def _():
            self.make().wait_recv()


class Place:
    def __init__(self, plan):
        self.t, self.r, self.c = (lax.axis_index(a) for a in AXES)
        self.has = dict(
            left=self.c > 0,
            right=self.c < plan.ncol - 1,
            up=self.r > 0,
            down=self.r < plan.nrow - 1,
            past=self.t > 0,
            future=self.t < plan.ntm - 1,
        )
        self.dev = dict(
            left={"col": self.c - 1},
            right={"col": self.c + 1},
            up={"row": self.r - 1},
            down={"row": self.r + 1},
            past={"tm": self.t - 1},
            future={"tm": self.t + 1},
        )

    def partners(self, plan):
        rows = [{"row": lax.rem(self.r + d, plan.na)} for d in range(1, plan.na)]
        index = self.t * plan.ncol + self.c
        others = []
        for d in range(1, plan.nb):
            to = lax.rem(index + d, plan.nb)
            others.append({"tm": lax.div(to, plan.ncol), "col": lax.rem(to, plan.ncol)})
        return rows, others


class Reduce:
    def __init__(self, plan, place, refs, sems, base):
        self.own, self.slots_a, self.mid, self.slots_b = refs
        rows, others = place.partners(plan)
        self.a = [
            Link(self.own, self.slots_a.at[d], sems, base + d, dev, None, None)
            for d, dev in enumerate(rows)
        ]
        self.b = [
            Link(self.mid, self.slots_b.at[d], sems, base + len(rows) + d, dev, None, None)
            for d, dev in enumerate(others)
        ]

    def start(self, first, second):
        self.own[...] = jnp.zeros_like(self.own)
        self.own[0:1] = first
        self.own[1:2] = second
        for link in self.a:
            link.start()

    def middle(self):
        for link in self.a:
            link.wait_recv()
        total = self.own[...]
        for d in range(len(self.a)):
            total = total + self.slots_a[d]
        self.mid[...] = total
        for link in self.b:
            link.start()

    def finish(self):
        for link in self.b:
            link.wait_recv()
        total = self.mid[...]
        for d in range(len(self.b)):
            total = total + self.slots_b[d]
        return total

    def drain(self):
        for link in self.a + self.b:
            link.wait_send()


class KernelSum:
    def __init__(self, plan, place, stages, span, acc, done, outs, ins, sems, base):
        self.acc, self.done, self.outs, self.ins = acc, done, outs, ins
        self.stages = stages
        at, count = span
        self.spans, self.reduce, self.gather = [], [], []
        for k, (axis, stride, ways, wide) in enumerate(stages):
            here = dict(tm=place.t, row=place.r, col=place.c)[axis]
            mine = lax.rem(lax.div(here, stride), ways)
            piece = count // ways
            aligned = lambda v: pl.multiple_of(v, 16)
            kept = aligned(at + mine * piece)
            links, sources = [], []
            for d in range(1, ways):
                other = lax.rem(mine + d, ways)
                dev = {axis: here + (other - mine) * stride}
                sent = aligned(at + other * piece)
                if wide:
                    src = acc.at[pl.ds(sent, piece)]
                else:
                    src = outs[k].at[d - 1]
                    sources.append((d - 1, sent))
                links.append((Link(src, ins[k].at[d - 1], sems, base, dev, None, None), dev))
                base += 1
            self.reduce.append([link for link, _ in links])
            gathers = []
            for _, dev in links:
                part = done.at[pl.ds(kept, piece)]
                gathers.append(Link(part, part, sems, base, dev, None, None))
                base += 1
            self.gather.append(gathers)
            self.spans.append((kept, piece, sources))
            at, count = kept, piece
        self.base = base

    def steps(self):
        out = []
        last = len(self.stages) - 1
        for k in range(len(self.stages)):
            out.append(functools.partial(self.reduce_step, k))
        for k in range(last, -1, -1):
            out.append(functools.partial(self.gather_step, k))
        out.append(self.last_step)
        return out

    def reduce_step(self, k):
        if k:
            self.settle(k - 1)
        kept, piece, sources = self.spans[k]
        for slot, sent in sources:
            self.outs[k][slot] = self.acc[pl.ds(sent, piece)].astype(BF16)
        for link in self.reduce[k]:
            link.start()

    def settle(self, k):
        kept, piece, _ = self.spans[k]
        for link in self.reduce[k]:
            link.wait_recv()
        total = self.acc[pl.ds(kept, piece)]
        for d in range(len(self.reduce[k])):
            total = total + self.ins[k][d].astype(F32)
        if k == len(self.stages) - 1:
            self.done[pl.ds(kept, piece)] = total.astype(BF16)
        else:
            self.acc[pl.ds(kept, piece)] = total

    def gather_step(self, k):
        if k == len(self.stages) - 1:
            self.settle(k)
        else:
            for link in self.gather[k + 1]:
                link.wait_recv()
        for link in self.gather[k]:
            link.start()

    def last_step(self):
        for link in self.gather[0]:
            link.wait_recv()

    def drain(self):
        for links in self.reduce + self.gather:
            for link in links:
                link.wait_send()


ORDERS = (("near", "col", "tm", "row"), ("near", "tm", "col", "row"))


def sum_scratch(plan):
    shapes, counts = [], []
    for order, (_, count) in zip(ORDERS, plan.parts):
        outs, ins = [], []
        for axis, stride, ways, wide in plan.stages(order):
            piece = count // ways
            shape = (ways - 1, piece, plan.c)
            outs.append(pltpu.VMEM((1, 16, plan.c) if wide else shape, BF16))
            ins.append(pltpu.VMEM(shape, F32 if wide else BF16))
            count = piece
        counts.append(len(outs))
        shapes += outs + ins
    return shapes, counts


def sum_sems(plan):
    return 2 * sum(
        stage[2] - 1 for order, _ in zip(ORDERS, plan.parts) for stage in plan.stages(order)
    )


EX_SEMS = 10


class Exchange:
    def __init__(self, plan, place, refs, sems, base, directions):
        self.plan, self.place, self.directions = plan, place, directions
        self.own, self.cols_out, self.cols_in, self.rows_out, self.rows_in = refs[:5]
        has, dev = place.has, place.dev
        cb, half = plan.cb, plan.f * plan.wp
        self.cols = [
            Link(self.cols_out.at[pl.ds(0, cb)], self.cols_in.at[pl.ds(0, cb)], sems, base,
                 dev["left"], has["left"], has["right"]),
            Link(self.cols_out.at[pl.ds(cb, cb)], self.cols_in.at[pl.ds(cb, cb)], sems, base + 1,
                 dev["right"], has["right"], has["left"]),
        ]
        self.rows = [
            Link(self.rows_out.at[pl.ds(0, half)], self.rows_in.at[pl.ds(half, half)], sems,
                 base + 2, dev["up"], has["up"], has["down"]),
            Link(self.rows_out.at[pl.ds(half, half)], self.rows_in.at[pl.ds(0, half)], sems,
                 base + 3, dev["down"], has["down"], has["up"]),
        ]
        self.tm = {}
        for k, source in enumerate(directions):
            block, cols, rows = refs[5 + 3 * k : 8 + 3 * k]
            target = "future" if source == "past" else "past"
            links = [
                Link(src, dst, sems, base + 4 + 3 * k + j, dev[target], has[target], has[source])
                for j, (src, dst) in enumerate(
                    [(self.own, block), (self.cols_in, cols), (self.rows_in, rows)]
                )
            ]
            self.tm[source] = ((block, cols, rows), links)

    def clear(self):
        cb, half = self.plan.cb, self.plan.f * self.plan.wp
        has = self.place.has

        def zero(ref, part, cond):
            @pl.when(jnp.logical_not(cond))
            def _():
                ref[part] = jnp.zeros(ref.at[part].shape, ref.dtype)

        zero(self.cols_in, pl.ds(0, cb), has["right"])
        zero(self.cols_in, pl.ds(cb, cb), has["left"])
        zero(self.rows_in, pl.ds(0, half), has["up"])
        zero(self.rows_in, pl.ds(half, half), has["down"])
        for source, (refs, _) in self.tm.items():
            for ref in refs:
                zero(ref, pl.ds(0, ref.shape[0]), has[source])

    def start(self, wide, pick):
        self.own[...] = wide[...].astype(BF16)
        for source in self.directions:
            self.tm[source][1][0].start()
        self.cols_out[...] = jnp.dot(pick[...], self.own[...], preferred_element_type=F32).astype(BF16)
        for link in self.cols:
            link.start()

    def middle(self, wide, spread):
        plan = self.plan
        for link in self.cols:
            link.wait_recv()
        for source in self.directions:
            self.tm[source][1][1].start()
        ends = spread_cols(self.cols_in, spread)
        size = plan.h * plan.wp
        for f in range(plan.f):
            for k, at in enumerate((f * size, (f + 1) * size - plan.wp)):
                self.rows_out[pl.ds((k * plan.f + f) * plan.wp, plan.wp)] = (
                    wide[pl.ds(at, plan.wp)] + ends[at : at + plan.wp]
                ).astype(BF16)
        for link in self.rows:
            link.start()

    def later(self):
        for link in self.rows:
            link.wait_recv()
        for source in self.directions:
            self.tm[source][1][2].start()

    def finish(self):
        for source in self.directions:
            for link in self.tm[source][1]:
                link.wait_recv()

    def drain(self):
        for link in self.cols + self.rows:
            link.wait_send()
        for source in self.directions:
            for link in self.tm[source][1]:
                link.wait_send()

    def pieces(self, wide, spread, source):
        plan = self.plan
        size = plan.h * plan.wp
        (block, cols, rows), _ = self.tm[source]

        def of(value, border, side):
            out = []
            for f in range(plan.f):
                top = border[pl.ds(f * plan.wp, plan.wp)].astype(F32)
                low = border[pl.ds((plan.f + f) * plan.wp, plan.wp)].astype(F32)
                out.append((side, top, value[f * size : (f + 1) * size], low))
            return out

        inner = of(wide[...] + spread_cols(self.cols_in, spread), self.rows_in, None)
        outer = of(block[...].astype(F32) + spread_cols(cols, spread), rows, source)
        if source == "past":
            return outer[plan.f - 2 :] + inner
        return inner + outer[:2]


def spread_cols(cols, spread):
    return jnp.dot(spread[...], cols[...], preferred_element_type=F32)


def silu(v):
    return v / (1.0 + jnp.exp(-v))


def slope(v):
    sigm = 1.0 / (1.0 + jnp.exp(-v))
    return sigm * (1.0 + v * (1.0 - sigm))


def valid(plan, place, count, side, border):
    has = place.has
    w = lax.broadcasted_iota(jnp.int32, (count, plan.c), 0) & (plan.wp - 1)
    one = lambda cond: cond.astype(jnp.int32)
    mask = jnp.where(
        w < plan.w,
        1,
        jnp.where(
            w == plan.w,
            one(has["right"]),
            jnp.where(w == plan.wp - 1, one(has["left"]), 0),
        ),
    )
    for name in (side, border):
        if name is not None:
            mask = mask * one(has[name])
    return mask > 0


def store_shifted(plan, ref, at, value):
    count = value.shape[0]
    rows = value.reshape(count // plan.wp, plan.wp, plan.c)
    before = pltpu.roll(rows, 1, axis=1).reshape(value.shape)
    after = pltpu.roll(rows, plan.wp - 1, axis=1).reshape(value.shape)
    c = plan.c
    ref[pl.ds(at, count), 0:c] = before.astype(BF16)
    ref[pl.ds(at, count), c : 2 * c] = value.astype(BF16)
    ref[pl.ds(at, count), 2 * c : 3 * c] = after.astype(BF16)


def build(plan, ref, frames):
    for k, (top, rows, low) in enumerate(frames):
        at = k * plan.hp * plan.wp
        store_shifted(plan, ref, at, top)
        store_shifted(plan, ref, at + plan.wp, rows)
        store_shifted(plan, ref, at + (plan.h + 1) * plan.wp, low)


def convolve(plan, ref, kernel, out):
    size = plan.h * plan.wp

    def frame(f, carry):
        pieces = []
        for p in range(3):
            for q in range(3):
                at = pl.multiple_of(((f + p) * plan.hp + q) * plan.wp, plan.wp)
                pieces.append(ref[pl.ds(at, size), :])
        wide = jnp.dot(jnp.concatenate(pieces, axis=1), kernel[...], preferred_element_type=F32)
        w = lax.broadcasted_iota(jnp.int32, wide.shape, 0) & (plan.wp - 1)
        out[pl.ds(pl.multiple_of(f * size, size), size), :] = jnp.where(w < plan.w, wide, 0.0)
        return carry

    lax.fori_loop(0, plan.f, frame, 0)


def kernel_term(plan, ref, turned, part, low, high):
    size = plan.h * plan.wp

    def tap(pq, carry):
        p, q = lax.div(pq, 3), lax.rem(pq, 3)
        pieces = []
        for f in range(plan.f):
            at = pl.multiple_of(((f + p) * plan.hp + q) * plan.wp, plan.wp)
            pieces.append(ref[pl.ds(at, size), :])
        term = jnp.dot(turned, jnp.concatenate(pieces, axis=0), preferred_element_type=F32)
        part[pl.ds(pl.multiple_of(pq * 3 * plan.c, 3 * plan.c), 3 * plan.c), :] = term.T
        return carry

    lax.fori_loop(low, high, tap, 0)


def turn_kernel(plan, kernel, out):
    taps, c = 27, plan.c

    def tap(k, carry):
        source = kernel[pl.ds(pl.multiple_of((taps - 1 - k) * c, c), c), :]
        out[pl.ds(pl.multiple_of(k * c, c), c), :] = source.astype(F32).T.astype(BF16)
        return carry

    lax.fori_loop(0, taps, tap, 0)


def spaced(plan, ref, wide):
    wide[...] = jnp.zeros_like(wide)
    for f in range(plan.f):
        for y in range(plan.h):
            wide[pl.ds((f * plan.h + y) * plan.wp, plan.w)] = ref[f, y].astype(F32)


def unspaced(plan, value, ref):
    for f in range(plan.f):
        for y in range(plan.h):
            at = (f * plan.h + y) * plan.wp
            ref[f, y] = value[at : at + plan.w].astype(BF16)


def column_sum(value):
    return jnp.sum(value, axis=0, keepdims=True)


def body(plan, n_ex, *refs):
    refs = list(refs)
    take = lambda k: [refs.pop(0) for _ in range(k)]
    features, cotangent, kernel_one, kernel_two, *norms = take(8)
    block_out, grad_input, part_one, part_two = take(4)
    wide_x, wide_g, wide_h, wide_l, wide_b = take(5)
    pick, spread, turned_one, turned_two = take(4)
    x3_one, x3_two, x3_g, x3_h = take(4)
    exchange_refs = [take(k) for k in n_ex]
    reduce_refs = [take(4) for _ in range(4)]
    acc_one, acc_two, done_one, done_two = take(4)
    sum_refs = []
    for _ in range(2):
        for count in sum_scratch(plan)[1]:
            sum_refs.append((take(count), take(count)))
    sems = take(2)

    place = Place(plan)
    rows, others = place.partners(plan)
    per_reduce = len(rows) + len(others)
    exchanges = [
        Exchange(plan, place, r, sems, EX_SEMS * k, d)
        for k, (r, d) in enumerate(
            zip(exchange_refs, (("past",), ("future",), ("past", "future"), ("future",)))
        )
    ]
    ex_x, ex_g, ex_h, ex_l = exchanges
    reduces = [
        Reduce(plan, place, r, sems, EX_SEMS * 4 + per_reduce * k)
        for k, r in enumerate(reduce_refs)
    ]
    sums = []
    base = EX_SEMS * 4 + per_reduce * 4
    for acc, done in ((acc_two, done_two), (acc_one, done_one)):
        for order, span in zip(ORDERS, plan.parts):
            outs, ins = sum_refs[len(sums)]
            sums.append(
                KernelSum(plan, place, plan.stages(order), span, acc, done, outs, ins, sems, base)
            )
            base = sums[-1].base
        acc[pl.ds(plan.taps_rows, plan.sum_rows - plan.taps_rows)] = jnp.zeros(
            (plan.sum_rows - plan.taps_rows, plan.c), F32
        )
    sums_two, sums_one = sums[: len(plan.parts)], sums[len(plan.parts) :]
    steps_two = [list(group) for group in zip(*[item.steps() for item in sums_two])]

    def advance():
        if steps_two:
            for step in steps_two.pop(0):
                step()

    for ex in exchanges:
        ex.clear()

    barrier = pltpu.get_barrier_semaphore()
    for dev in rows + others:
        pl.semaphore_signal(barrier, inc=1, device_id=dev, device_id_type=MESH)

    c = plan.c
    per_group = c // GROUPS
    members = float(plan.f * plan.h * plan.w * plan.ntm * plan.nrow * plan.ncol * per_group)
    lane_i = lax.broadcasted_iota(jnp.int32, (c, c), 0)
    lane_j = lax.broadcasted_iota(jnp.int32, (c, c), 1)
    same = (lax.div(lane_i, per_group) == lax.div(lane_j, per_group)).astype(F32)

    def group_means(total):
        sums = jnp.dot(
            total, same, preferred_element_type=F32, precision=lax.Precision.HIGHEST
        )
        return sums[0:1] / members, sums[1:2] / members

    def moments(total):
        average, square = group_means(total)
        return average, lax.rsqrt(square - average * average + EPSILON)

    spaced(plan, features, wide_x)
    j = lax.broadcasted_iota(jnp.int32, (2 * plan.cb, plan.n), 0)
    at = lax.broadcasted_iota(jnp.int32, (2 * plan.cb, plan.n), 1)
    first = j < plan.cb
    pick[...] = (
        at == jnp.where(first, j * plan.wp, (j - plan.cb) * plan.wp + plan.w - 1)
    ).astype(F32).astype(BF16)
    at = lax.broadcasted_iota(jnp.int32, (plan.n, 2 * plan.cb), 0)
    j = lax.broadcasted_iota(jnp.int32, (plan.n, 2 * plan.cb), 1)
    first = j < plan.cb
    spread[...] = (
        at == jnp.where(first, j * plan.wp + plan.w, (j - plan.cb) * plan.wp + plan.wp - 1)
    ).astype(F32).astype(BF16)

    pl.semaphore_wait(barrier, per_reduce)
    gain_one, shift_one, gain_two, shift_two = (ref[...] for ref in norms)

    x = wide_x[...]
    reduces[0].start(column_sum(x), column_sum(x * x))
    ex_x.start(wide_x, pick)
    spaced(plan, cotangent, wide_g)
    ex_g.start(wide_g, pick)
    reduces[0].middle()
    ex_x.middle(wide_x, spread)
    ex_g.middle(wide_g, spread)
    turn_kernel(plan, kernel_two, turned_two)
    ex_x.later()
    ex_g.later()
    turn_kernel(plan, kernel_one, turned_one)
    mean_one, scale_one = moments(reduces[0].finish())
    ex_x.finish()

    def unit_one(v):
        return (v - mean_one) * scale_one

    def frames_of(pieces, fn):
        out = []
        for side, top, rows_, low in pieces:
            keep = lambda v, border: jnp.where(
                valid(plan, place, v.shape[0], side, border), fn(v), 0.0
            )
            out.append((keep(top, "up"), keep(rows_, None), keep(low, "down")))
        return out

    build(
        plan,
        x3_one,
        frames_of(
            ex_x.pieces(wide_x, spread, "past"),
            lambda v: silu(unit_one(v) * gain_one + shift_one),
        ),
    )
    convolve(plan, x3_one, kernel_one, wide_h)
    hidden = wide_h[...]
    reduces[1].start(column_sum(hidden), column_sum(hidden * hidden))
    ex_h.start(wide_h, pick)
    reduces[1].middle()
    ex_h.middle(wide_h, spread)
    ex_g.finish()
    build(plan, x3_g, [p[1:] for p in ex_g.pieces(wide_g, spread, "future")])
    ex_h.later()
    convolve(plan, x3_g, turned_two, wide_b)
    mean_two, scale_two = moments(reduces[1].finish())

    def unit_two(v):
        return (v - mean_two) * scale_two

    unit = unit_two(wide_h[...])
    lifted = wide_b[...] * slope(unit * gain_two + shift_two) * gain_two
    wide_l[...] = lifted
    reduces[2].start(column_sum(lifted), column_sum(lifted * unit))
    ex_l.start(wide_l, pick)
    reduces[2].middle()
    ex_l.middle(wide_l, spread)
    ex_h.finish()
    build(
        plan,
        x3_two,
        frames_of(
            ex_h.pieces(wide_h, spread, "past"),
            lambda v: silu(unit_two(v) * gain_two + shift_two),
        ),
    )
    ex_l.later()
    kernel_term(plan, x3_two, wide_g[...].T.astype(BF16), acc_two, 0, 9)
    a_two, b_two = group_means(reduces[2].finish())
    advance()
    ex_l.finish()
    frames = []
    for (side, *lifts), (_, *hids) in zip(
        ex_l.pieces(wide_l, spread, "future"), ex_h.pieces(wide_h, spread, "future")
    ):
        out = []
        for border, lift, hid in zip(("up", None, "down"), lifts, hids):
            value = scale_two * (lift - a_two - unit_two(hid) * b_two)
            out.append(jnp.where(valid(plan, place, lift.shape[0], side, border), value, 0.0))
        frames.append(tuple(out))
    build(plan, x3_h, frames)
    advance()
    w = lax.broadcasted_iota(jnp.int32, (plan.h * plan.wp, c), 0) & (plan.wp - 1)
    own = jnp.concatenate(
        [jnp.where(w < plan.w, frames[f][1], 0.0) for f in range(plan.f)], axis=0
    )
    turned = own.T.astype(BF16)
    ready = min(9, -(-plan.parts[0][1] // (3 * c)))
    kernel_term(plan, x3_one, turned, acc_one, 0, ready)
    steps_one = [item.steps() for item in sums_one]
    steps_one[0].pop(0)()
    advance()
    kernel_term(plan, x3_one, turned, acc_one, ready, 9)
    for steps in steps_one[1:]:
        steps.pop(0)()

    def advance_one():
        for steps in steps_one:
            steps.pop(0)()

    convolve(plan, x3_h, turned_one, wide_b)
    unit = unit_one(wide_x[...])
    lifted = wide_b[...] * slope(unit * gain_one + shift_one) * gain_one
    reduces[3].start(column_sum(lifted), column_sum(lifted * unit))
    wide_l[...] = lifted
    advance_one()
    advance()
    reduces[3].middle()
    convolve(plan, x3_two, kernel_two, wide_b)
    advance_one()
    advance()
    unspaced(plan, wide_x[...] + wide_b[...], block_out)
    a_one, b_one = group_means(reduces[3].finish())
    advance_one()
    advance()
    unit = unit_one(wide_x[...])
    unspaced(
        plan,
        wide_g[...] + scale_one * (wide_l[...] - a_one - unit * b_one),
        grad_input,
    )
    while steps_one[0]:
        advance_one()
        advance()
    part_two[...] = done_two[pl.ds(0, plan.taps_rows)]
    part_one[...] = done_one[pl.ds(0, plan.taps_rows)]
    for item in exchanges + reduces + sums:
        item.drain()


def block_kernel(plan, features, cotangent, kernel_one, kernel_two, *norms):
    c, n = plan.c, plan.n
    half = plan.f * plan.wp
    exchange = []
    n_ex = []
    for count in (1, 1, 2, 1):
        shapes = [(n, c), (2 * plan.cb, c), (2 * plan.cb, c), (2 * half, c), (2 * half, c)]
        shapes += [(n, c), (2 * plan.cb, c), (2 * half, c)] * count
        n_ex.append(len(shapes))
        exchange += [pltpu.VMEM(s, BF16) for s in shapes]
    reduce = [
        pltpu.VMEM((8, c), F32),
        pltpu.VMEM((max(1, plan.na - 1), 8, c), F32),
        pltpu.VMEM((8, c), F32),
        pltpu.VMEM((max(1, plan.nb - 1), 8, c), F32),
    ] * 4
    sems = 4 * EX_SEMS + 4 * (plan.na + plan.nb - 2) + 2 * sum_sems(plan)
    vmem = pl.BlockSpec(memory_space=pltpu.VMEM)
    taps = kernel_one.shape[0]
    return pl.pallas_call(
        functools.partial(body, plan, n_ex),
        out_shape=(
            jax.ShapeDtypeStruct(features.shape, BF16),
            jax.ShapeDtypeStruct(features.shape, BF16),
            jax.ShapeDtypeStruct((taps, c), BF16),
            jax.ShapeDtypeStruct((taps, c), BF16),
        ),
        in_specs=[vmem] * 8,
        out_specs=(vmem,) * 4,
        scratch_shapes=[pltpu.VMEM((n, c), F32)] * 5
        + [pltpu.VMEM((2 * plan.cb, n), BF16), pltpu.VMEM((n, 2 * plan.cb), BF16)]
        + [pltpu.VMEM((taps, c), BF16)] * 2
        + [pltpu.VMEM((plan.np, 3 * c), BF16)] * 4
        + exchange
        + reduce
        + [pltpu.VMEM((plan.sum_rows, c), F32)] * 2
        + [pltpu.VMEM((plan.sum_rows, c), BF16)] * 2
        + sum_scratch(plan)[0] * 2
        + [pltpu.SemaphoreType.DMA((sems,))] * 2,
        compiler_params=pltpu.CompilerParams(
            collective_id=0, has_side_effects=True, vmem_limit_bytes=52 * 2**20
        ),
    )(features, cotangent, kernel_one, kernel_two, *norms)


SLOT = 16
MANY = 224


class Split:
    def __init__(self, f, h, w, c, sizes):
        self.f, self.h, self.w, self.c = f, h, w, c
        self.ntm, self.nrow, self.ncol = sizes
        self.frames = f * self.ntm
        self.half = w // 2
        self.fn = h * SLOT
        self.pn = (h + 2) * SLOT
        self.n = self.frames * self.fn
        self.hs = -(-h // 16) * 16
        self.ext = self.frames * self.hs
        self.wide = 2 * SLOT
        self.gn = -(-self.fn // 128) * 128
        self.taps_rows = 27 * c
        self.nxy = self.ntm * (self.ncol // 2)
        unit = 16 * self.nxy * self.nrow
        units = -(-self.taps_rows // (2 * unit))
        first = max(1, (5 * units) // 7)
        self.core_rows = units * unit
        self.sum_rows = 2 * self.core_rows
        self.part_rows = [first * unit, (units - first) * unit]

    @staticmethod
    def fits(f, h, w, c, sizes):
        ntm, nrow, ncol = sizes
        return (
            ntm == 2
            and ncol % 2 == 0
            and w % 2 == 0
            and SLOT < w <= 2 * SLOT
            and w // 2 + 2 <= SLOT
            and w - SLOT <= w // 2 - 1
            and h <= 16
            and f * ntm * 16 <= 64
            and f * ntm >= 3
        )


class Spot:
    def __init__(self, plan):
        self.t, self.r, self.c = (lax.axis_index(a) for a in AXES)
        self.k = 2 * self.c + self.t
        self.left = self.k > 0
        self.right = self.k < 2 * plan.ncol - 1
        self.up = self.r > 0
        self.down = self.r < plan.nrow - 1
        self.core = lax.rem(self.c, 2)
        self.y = lax.div(self.c, 2)

    def peers(self, plan):
        offsets = [
            (dt, dr, dc)
            for dt in range(plan.ntm)
            for dr in range(plan.nrow)
            for dc in range(plan.ncol)
            if (dt, dr, dc) != (0, 0, 0)
        ]
        offsets.sort(key=lambda o: -(o[0] + min(1, o[2]) + 2 * (o[1] == plan.nrow // 2) + (o[1] > 0)))
        out = []
        for dt, dr, dc in offsets:
            out.append(
                {
                    "tm": lax.rem(self.t + dt, plan.ntm),
                    "row": lax.rem(self.r + dr, plan.nrow),
                    "col": lax.rem(self.c + dc, plan.ncol),
                }
            )
        return out

    def plane(self, plan):
        me = self.t * (plan.ncol // 2) + self.y
        out = []
        for d in range(1, plan.nxy):
            o = lax.rem(me + d, plan.nxy)
            dev = {
                "tm": lax.div(o, plan.ncol // 2),
                "col": 2 * lax.rem(o, plan.ncol // 2) + self.core,
            }
            out.append((o, dev))
        return me, out

    def line(self, plan):
        out = []
        for d in range(1, plan.nrow):
            o = lax.rem(self.r + d, plan.nrow)
            out.append((o, {"row": o}))
        return self.r, out


class Counter:
    def __init__(self):
        self.at = 0

    def take(self):
        self.at += 1
        return self.at - 1


class Total:
    def __init__(self, peers, own, slots, sems, counter):
        self.own, self.slots, self.peers, self.sems = own, slots, peers, sems
        self.index = counter.take()

    def start(self, first, second):
        self.own[0:1] = first
        self.own[1:2] = second
        for d, dev in enumerate(self.peers):
            pltpu.make_async_remote_copy(
                src_ref=self.own.at[pl.ds(0, 2)],
                dst_ref=self.slots.at[d, pl.ds(0, 2)],
                send_sem=self.sems[0].at[self.index],
                recv_sem=self.sems[1].at[self.index],
                device_id=dev,
                device_id_type=MESH,
            ).start()

    def whole(self, k):
        part = self.slots.at[pl.ds(0, len(self.peers)), pl.ds(0, 2)]
        return pltpu.make_async_copy(part, part, self.sems[k].at[self.index])

    def finish(self):
        self.whole(1).wait()
        total = self.own[0:2]
        for d in range(len(self.peers)):
            total = total + self.slots[d, 0:2]
        return total

    def drain(self):
        self.whole(0).wait()


class Halo:
    def __init__(self, plan, spot, refs, sems, counter):
        self.plan, self.spot = plan, spot
        self.block, self.edge, self.top, self.bot, self.ch = refs
        self.sems, self.counter = sems, counter
        self.links = []

    def link(self, src, dst, dev, sends, receives):
        item = Link(src, dst, self.sems, self.counter.take(), dev, sends, receives)
        self.links.append(item)
        return item

    def rows(self):
        s = self.spot
        return ((1, s.r + 1, s.down, s.up), (2, s.r - 1, s.up, s.down))

    def lines(self):
        s = self.spot
        return ((0, None, None, None),) + self.rows()

    def clear(self):
        for ref in (self.top, self.bot, self.ch):
            ref[...] = jnp.zeros(ref.shape, BF16)

    def wait(self):
        for link in self.links:
            link.wait_recv()

    def drain(self):
        for link in self.links:
            link.wait_send()


def both(*conds):
    out = None
    for cond in conds:
        if cond is not None:
            out = cond if out is None else jnp.logical_and(out, cond)
    return out


class Reshard(Halo):
    def __init__(self, plan, spot, pair, refs, sems, counter):
        super().__init__(plan, spot, refs, sems, counter)
        self.pair = pair
        t, r, c, f = spot.t, spot.r, spot.c, plan.f
        n = plan.ncol
        for which, row, sends, receives in self.rows():
            src_at = plan.fn - SLOT if which == 1 else 0
            dst = (self.top if which == 1 else self.bot).at[pl.ds(f * t, f)]
            for d in range(2):
                to = t if d == 0 else 1 - t
                self.link(pair.at[to, :, pl.ds(src_at, SLOT)], dst, {"tm": to, "row": row}, sends, receives)
        rows = f * plan.hs
        for which, row, sends, receives in self.lines():
            for d in range(2):
                dev = {"tm": t - d, "col": c + 1}
                if row is not None:
                    dev["row"] = row
                self.link(
                    self.edge.at[1], self.ch.at[which, pl.ds(rows * d, rows)], dev,
                    both(t == d, c < n - 1, sends), both(t == 0, c > 0, receives),
                )
                dev = {"tm": t - d + 1, "col": c - 1}
                if row is not None:
                    dev["row"] = row
                self.link(
                    self.edge.at[0], self.ch.at[which, pl.ds(plan.ext + rows * d, rows)], dev,
                    both(t == d, c > 0, sends), both(t == 1, c < n - 1, receives),
                )
        self.link(pair.at[1 - t], self.block.at[pl.ds(f * t, f)], {"tm": 1 - t}, None, None)

    def start(self, source, w32):
        plan, t = self.plan, self.spot.t
        w32[...] = jnp.zeros(w32.shape, F32)
        for f in range(plan.f):
            for y in range(plan.h):
                w32[pl.ds((f * plan.h + y) * plan.wide, plan.w)] = source[f, y].astype(F32)
        slot = lax.broadcasted_iota(jnp.int32, (plan.h, SLOT, plan.c), 1)
        for f in range(plan.f):
            v = w32[pl.ds(f * plan.h * plan.wide, plan.h * plan.wide)]
            v = v.reshape(plan.h, plan.wide, plan.c)
            low, high = v[:, :SLOT], v[:, SLOT:]
            second = jnp.where(slot >= plan.half - 1, low, high)
            self.pair[0, f] = low.reshape(plan.fn, plan.c).astype(BF16)
            self.pair[1, f] = second.reshape(plan.fn, plan.c).astype(BF16)
            for side, x in ((0, 0), (1, plan.w - 1)):
                at = f * plan.h * plan.wide + x
                self.edge[side, pl.ds(f * plan.hs, plan.hs)] = w32[
                    pl.ds(at, plan.hs, plan.wide)
                ].astype(BF16)

    def send(self):
        for link in self.links:
            link.start()

    def keep(self):
        self.block[pl.ds(self.plan.f * self.spot.t, self.plan.f)] = self.pair[self.spot.t]


class Border(Halo):
    def __init__(self, plan, spot, refs, sems, counter):
        super().__init__(plan, spot, refs, sems, counter)
        t, c = spot.t, spot.c
        for which, row, sends, receives in self.rows():
            at = plan.fn - SLOT if which == 1 else 0
            dst = self.top if which == 1 else self.bot
            self.link(self.block.at[:, pl.ds(at, SLOT)], dst, {"row": row}, sends, receives)
        for which, row, sends, receives in self.lines():
            dev = {"tm": 1 - t, "col": c - 1 + t}
            if row is not None:
                dev["row"] = row
            self.link(
                self.edge.at[0], self.ch.at[which, pl.ds(plan.ext, plan.ext)], dev,
                both(spot.left, sends), both(spot.right, receives),
            )
            dev = {"tm": 1 - t, "col": c + t}
            if row is not None:
                dev["row"] = row
            self.link(
                self.edge.at[1], self.ch.at[which, pl.ds(0, plan.ext)], dev,
                both(spot.right, sends), both(spot.left, receives),
            )

    def start(self, wide):
        plan, t = self.plan, self.spot.t
        for f in range(plan.frames):
            self.block[f] = wide[pl.ds(f * plan.fn, plan.fn)].astype(BF16)
            for side, offset in ((0, 0), (1, plan.half - 1)):
                values = [
                    wide[pl.ds(f * plan.fn + (plan.half * k + offset) % SLOT, plan.hs, SLOT)]
                    for k in range(2)
                ]
                self.edge[side, pl.ds(f * plan.hs, plan.hs)] = jnp.where(
                    t == 0, values[0], values[1]
                ).astype(BF16)
        for link in self.links:
            link.start()


class KernelTotal:
    def __init__(self, plan, spot, acc, done, refs, sems, counter):
        self.plan, self.spot, self.acc, self.done = plan, spot, acc, done
        self.core_in, *parts = refs
        link = lambda src, dst, dev: Link(src, dst, sems, counter.take(), dev, None, None)
        aligned = lambda v: pl.multiple_of(v, 16)
        mine = aligned(spot.core * plan.core_rows)
        other = aligned((1 - spot.core) * plan.core_rows)
        sibling = {"col": spot.c + 1 - 2 * spot.core}
        self.mine = mine
        self.core = []
        self.parts = []
        at = 0
        for j, count in enumerate(plan.part_rows):
            if not count:
                continue
            self.core.append(
                link(acc.at[pl.ds(aligned(other + at), count)], self.core_in.at[pl.ds(at, count)], sibling)
            )
            stages = (spot.plane(plan), spot.line(plan))
            if j:
                stages = stages[::-1]
            (one, ones), (two, twos) = stages
            out1, in1, out2, in2 = parts[4 * j : 4 * j + 4]
            big = count // (len(ones) + 1)
            small = big // (len(twos) + 1)
            base = aligned(mine + at)
            own1 = aligned(base + one * big)
            own2 = aligned(own1 + two * small)
            part = dict(at=at, count=count, base=base, big=big, small=small, own1=own1, own2=own2)
            part["own1_in"] = aligned(at + one * big)
            part["send1"] = [
                (aligned(base + o * big), aligned(at + o * big), out1.at[d], link(out1.at[d], in1.at[d], dev))
                for d, (o, dev) in enumerate(ones)
            ]
            part["send2"] = [
                (two_at, out2.at[d], link(out2.at[d], in2.at[d], dev))
                for d, (two_at, dev) in enumerate((aligned(own1 + o * small), dev) for o, dev in twos)
            ]
            part["in1"], part["in2"] = in1, in2
            piece2 = done.at[pl.ds(own2, small)]
            part["gather2"] = [link(piece2, piece2, dev) for _, dev in twos]
            piece1 = done.at[pl.ds(own1, big)]
            part["gather1"] = [link(piece1, piece1, dev) for _, dev in ones]
            forward = [link(piece1, piece1, sibling)]
            for d in range(len(ones)):
                o, _ = ones[len(ones) - 1 - d]
                ref = done.at[pl.ds(aligned(base + o * big), big)]
                forward.append(link(ref, ref, sibling))
            part["forward"] = forward
            self.parts.append(part)
            at += count

    def start(self):
        for link in self.core:
            link.start()

    def first(self):
        acc = self.acc
        for part, core in zip(self.parts, self.core):
            core.wait_recv()
            big = part["big"]
            for at, inside, out, link in part["send1"]:
                out[...] = (acc[pl.ds(at, big)] + self.core_in[pl.ds(inside, big)]).astype(BF16)
                link.start()

    def second(self):
        acc = self.acc
        for part in self.parts:
            big, small, own1 = part["big"], part["small"], part["own1"]
            total = acc[pl.ds(own1, big)] + self.core_in[pl.ds(part["own1_in"], big)]
            for d, (_, _, _, link) in enumerate(part["send1"]):
                link.wait_recv()
                total = total + part["in1"][d].astype(F32)
            acc[pl.ds(own1, big)] = total
            for at, out, link in part["send2"]:
                out[...] = acc[pl.ds(at, small)].astype(BF16)
                link.start()

    def third(self):
        for part in self.parts:
            own2, small = part["own2"], part["small"]
            total = self.acc[pl.ds(own2, small)]
            for d, (_, _, link) in enumerate(part["send2"]):
                link.wait_recv()
                total = total + part["in2"][d].astype(F32)
            self.done[pl.ds(own2, small)] = total.astype(BF16)
            for link in part["gather2"]:
                link.start()

    def fourth(self):
        for part in self.parts:
            for link in part["gather2"]:
                link.wait_recv()
            for link in part["gather1"]:
                link.start()
            part["forward"][0].start()

    def fifth(self):
        for part in self.parts:
            for d, link in enumerate(part["gather1"]):
                link.wait_recv()
                part["forward"][1 + d].start()

    def sixth(self):
        for part in self.parts:
            for link in part["forward"]:
                link.wait_recv()

    def steps(self):
        return [self.start, self.first, self.second, self.third, self.fourth, self.fifth, self.sixth]

    def drain(self):
        for link in self.core:
            link.wait_send()
        for part in self.parts:
            for item in part["send1"] + part["send2"]:
                item[-1].wait_send()
            for name in ("gather2", "gather1", "forward"):
                for link in part[name]:
                    link.wait_send()


def total_scratch(plan):
    shapes = [pltpu.VMEM((plan.core_rows, plan.c), F32)]
    for j, count in enumerate(plan.part_rows):
        ways = (plan.nxy, plan.nrow) if j == 0 else (plan.nrow, plan.nxy)
        big = count // ways[0]
        small = big // ways[1]
        for rows, k in ((big, ways[0]), (big, ways[0]), (small, ways[1]), (small, ways[1])):
            shapes.append(pltpu.VMEM((max(1, k - 1), max(rows, 16), plan.c), BF16))
    return shapes


def around(value, by):
    rows = value.reshape(value.shape[0] // SLOT, SLOT, value.shape[1])
    return pltpu.roll(rows, by, axis=1).reshape(value.shape)


def convolve_split(plan, padded, weight, out, keep, future):
    c = plan.c
    for t in range(plan.frames):
        pieces, used = [], []
        for p in range(3):
            source = t + p if future else t + p - 2
            if not 0 <= source < plan.frames:
                continue
            used.append(p)
            for q in range(3):
                pieces.append(padded[pl.ds(source * plan.pn + q * SLOT, plan.fn), :])
        lhs = jnp.concatenate(pieces, axis=1)
        rhs = weight[3 * used[0] : 3 * used[-1] + 3].reshape(3 * len(used) * c, 3 * c)
        wide = jnp.dot(lhs, rhs, preferred_element_type=F32)
        total = around(wide[:, 0:c], 1) + wide[:, c : 2 * c] + around(wide[:, 2 * c :], SLOT - 1)
        out[pl.ds(t * plan.fn, plan.fn), :] = keep(total)


def place_padded(plan, ref, value, top, bot):
    for t in range(plan.frames):
        at = t * plan.pn
        ref[pl.ds(at, SLOT), :] = top[t * SLOT : (t + 1) * SLOT].astype(BF16)
        ref[pl.ds(at + SLOT, plan.fn), :] = value[t * plan.fn : (t + 1) * plan.fn].astype(BF16)
        ref[pl.ds(at + SLOT + plan.fn, SLOT), :] = bot[t * SLOT : (t + 1) * SLOT].astype(BF16)


def shifted_grad(plan, ref, value):
    c = plan.c
    for s, moved in enumerate((around(value, SLOT - 1), value, around(value, 1))):
        for t in range(plan.frames):
            ref[pl.ds(t * plan.gn, plan.fn), s * c : (s + 1) * c] = moved[
                t * plan.fn : (t + 1) * plan.fn
            ].astype(BF16)


def turned_acted(plan, padded, ref):
    c = plan.c
    for q in range(3):
        for t in range(plan.frames):
            slab = padded[pl.ds(t * plan.pn + q * SLOT, plan.gn), :]
            ref[q * c : (q + 1) * c, t * plan.gn : (t + 1) * plan.gn] = slab.T


def kernel_grad(plan, turned, moved, acc):
    c = plan.c
    for p in range(3):
        lag = 2 - p
        count = (plan.frames - lag) * plan.gn
        term = jnp.dot(
            turned[:, 0:count], moved[pl.ds(lag * plan.gn, count), :], preferred_element_type=F32
        )
        for q in range(3):
            for s in range(3):
                acc[pl.ds((9 * p + 3 * q + s) * c, c), :] = term[
                    q * c : (q + 1) * c, s * c : (s + 1) * c
                ]


def turn_weight(plan, weight, out):
    c = plan.c
    for k in range(27):
        j = 26 - k
        source = weight[j // 3, :, (j % 3) * c : (j % 3 + 1) * c]
        out[k // 3, :, (k % 3) * c : (k % 3 + 1) * c] = source.T


def split_body(plan, *refs):
    refs = list(refs)
    take = lambda k: [refs.pop(0) for _ in range(k)]
    features, cotangent, conv_one, conv_two, *norms = take(8)
    block_out, grad_input, done_one, done_two = take(4)
    (w32,) = take(1)
    wide_h, wide_l, wide_b, unit_h = take(4)
    spread_mid, spread_top, spread_bot = take(3)
    weight_one, weight_two, turned_one, turned_two = take(4)
    pad_one, pad_two, pad_g, pad_h = take(4)
    at_one, at_two, moved_g, moved_h = take(4)
    acc_one, acc_two = take(2)
    norm_in = take(4)
    pair_x, pair_g = take(2)
    halo_refs = [take(5) for _ in range(4)]
    total_refs = [take(2) for _ in range(4)]
    sum_refs = [take(9) for _ in range(2)]
    out_refs = [take(2) for _ in range(2)]
    sems = take(2)
    (local_sem,) = take(1)

    spot = Spot(plan)
    peers = spot.peers(plan)
    counter = Counter()
    c = plan.c

    loads = []
    for k, (src, dst) in enumerate(
        list(zip(norms, norm_in))
        + [(conv_one.at[:, s], weight_one.at[:, :, pl.ds(s * c, c)]) for s in range(3)]
        + [(conv_two.at[:, s], weight_two.at[:, :, pl.ds(s * c, c)]) for s in range(3)]
    ):
        copy = pltpu.make_async_copy(src, dst, local_sem.at[k])
        copy.start()
        loads.append(copy)

    ex_x = Reshard(plan, spot, pair_x, halo_refs[0], sems, counter)
    ex_g = Reshard(plan, spot, pair_g, halo_refs[1], sems, counter)
    ex_h = Border(plan, spot, halo_refs[2], sems, counter)
    ex_l = Border(plan, spot, halo_refs[3], sems, counter)
    totals = [Total(peers, *r, sems, counter) for r in total_refs]
    sum_two = KernelTotal(plan, spot, acc_two, done_two, sum_refs[0], sems, counter)
    sum_one = KernelTotal(plan, spot, acc_one, done_one, sum_refs[1], sems, counter)
    outs = []
    for (mine, theirs) in out_refs:
        outs.append(
            Link(
                mine.at[pl.ds(plan.f * (1 - spot.t), plan.f)], theirs, sems, counter.take(),
                {"tm": 1 - spot.t}, None, None,
            )
        )
    assert counter.at <= MANY

    for ex in (ex_x, ex_g, ex_h, ex_l):
        ex.clear()
    barrier = pltpu.get_barrier_semaphore()
    for dev in peers:
        pl.semaphore_signal(barrier, inc=1, device_id=dev, device_id_type=MESH)

    per_group = c // GROUPS
    members = float(plan.n // SLOT * plan.half * 2 * plan.nrow * plan.ncol * per_group)
    lane_i = lax.broadcasted_iota(jnp.int32, (c, c), 0)
    lane_j = lax.broadcasted_iota(jnp.int32, (c, c), 1)
    same = (lax.div(lane_i, per_group) == lax.div(lane_j, per_group)).astype(F32)

    def group_means(total):
        sums = jnp.dot(total, same, preferred_element_type=F32, precision=lax.Precision.HIGHEST)
        return sums[0:1] / members, sums[1:2] / members

    def moments(total):
        average, square = group_means(total)
        return average, lax.rsqrt(square - average * average + EPSILON)

    ex_x.start(features, w32)
    x = w32[...]
    first, second = column_sum(x), column_sum(x * x)
    pl.semaphore_wait(barrier, len(peers))
    totals[0].start(first, second)
    ex_x.send()
    ex_g.start(cotangent, w32)
    ex_g.send()
    ex_x.keep()
    ex_g.keep()

    rel = (lax.broadcasted_iota(jnp.int32, (SLOT, c), 0) - plan.half * spot.t) & (SLOT - 1)
    one = lambda cond: cond.astype(jnp.int32)
    inside = rel < plan.half
    inner = jnp.where(spot.t == 0, plan.half, SLOT - 1)
    kept = jnp.logical_or(inside, rel == inner)
    legal = jnp.where(
        inside, 1, jnp.where(rel == plan.half, one(spot.right), jnp.where(rel == SLOT - 1, one(spot.left), 0))
    )

    def masked(value, mask):
        rows = value.reshape(value.shape[0] // SLOT, SLOT, c)
        return jnp.where(mask[None], rows, 0.0).reshape(value.shape)

    interior = lambda value: masked(value, inside)

    def targets(rows, source):
        i = lax.broadcasted_iota(jnp.int32, (rows, 2 * plan.ext), 0)
        j = lax.broadcasted_iota(jnp.int32, (rows, 2 * plan.ext), 1)
        where = ((i & (SLOT - 1)) - plan.half * spot.t) & (SLOT - 1)
        code = source(i >> 4)
        aim = jnp.where(where == SLOT - 1, code, jnp.where(where == plan.half, code + plan.ext, -1))
        return (j == aim).astype(F32).astype(BF16)

    def of_group(g):
        t = 0
        for k in range(1, plan.frames):
            t = t + (g >= k * plan.h).astype(jnp.int32)
        return g + t * (plan.hs - plan.h)

    spread_mid[...] = targets(plan.n, of_group)
    spread_top[...] = targets(plan.frames * SLOT, lambda t: t * plan.hs + plan.h - 1)
    spread_bot[...] = targets(plan.frames * SLOT, lambda t: t * plan.hs)
    for ref in (pad_one, pad_two):
        ref[pl.ds(plan.frames * plan.pn, SLOT), :] = jnp.zeros((SLOT, c), BF16)
    if plan.gn > plan.fn:
        for ref in (moved_g, moved_h):
            for t in range(plan.frames):
                ref[pl.ds(t * plan.gn + plan.fn, plan.gn - plan.fn), :] = jnp.zeros(
                    (plan.gn - plan.fn, 3 * c), BF16
                )
    for ref in (wide_h, wide_l):
        ref[pl.ds(plan.n, SLOT), :] = jnp.zeros((SLOT, c), F32)
    for acc in (acc_one, acc_two):
        acc[pl.ds(plan.taps_rows, plan.sum_rows - plan.taps_rows)] = jnp.zeros(
            (plan.sum_rows - plan.taps_rows, c), F32
        )
    for copy in loads:
        copy.wait()
    gain_one, shift_one, gain_two, shift_two = (ref[...] for ref in norm_in)
    turn_weight(plan, weight_two, turned_two)

    def assemble(ex, value, mask):
        flat = lambda ref: ref[...].astype(F32).reshape(plan.frames * SLOT, c)
        spread = lambda by, k: jnp.dot(by[...], ex.ch[k], preferred_element_type=F32)
        return (
            masked(value, mask) + spread(spread_mid, 0),
            masked(flat(ex.top), mask) + spread(spread_top, 1),
            masked(flat(ex.bot), mask) + spread(spread_bot, 2),
        )

    def clip(values):
        value, top, bot = values
        return (
            masked(value, legal > 0),
            masked(top, legal * one(spot.up) > 0),
            masked(bot, legal * one(spot.down) > 0),
        )

    def flat_block(ex):
        return ex.block[...].astype(F32).reshape(plan.n, c)

    ex_x.wait()
    values_x = assemble(ex_x, flat_block(ex_x), kept)
    mean_one, scale_one = moments(totals[0].finish())

    def unit_one(v):
        return (v - mean_one) * scale_one

    place_padded(
        plan, pad_one, *clip([silu(unit_one(v) * gain_one + shift_one) for v in values_x])
    )
    convolve_split(plan, pad_one, weight_one, wide_h, interior, False)
    hidden = wide_h[pl.ds(0, plan.n)]
    totals[1].start(column_sum(hidden), column_sum(hidden * hidden))
    ex_h.start(wide_h)

    ex_g.wait()
    place_padded(plan, pad_g, *clip(assemble(ex_g, flat_block(ex_g), kept)))
    convolve_split(plan, pad_g, turned_two, wide_b, interior, True)
    shifted_grad(plan, moved_g, interior(flat_block(ex_g)))
    turned_acted(plan, pad_one, at_one)
    mean_two, scale_two = moments(totals[1].finish())

    def unit_two(v):
        return (v - mean_two) * scale_two

    unit = unit_two(wide_h[pl.ds(0, plan.n)])
    lifted = interior(wide_b[...] * slope(unit * gain_two + shift_two) * gain_two)
    wide_l[pl.ds(0, plan.n)] = lifted
    totals[2].start(column_sum(lifted), column_sum(lifted * unit))
    ex_l.start(wide_l)

    ex_h.wait()
    units = [unit_two(v) for v in assemble(ex_h, wide_h[pl.ds(0, plan.n)], inside)]
    at = 0
    for v in units:
        unit_h[pl.ds(at, v.shape[0])] = v
        at += v.shape[0]
    place_padded(plan, pad_two, *clip([silu(v * gain_two + shift_two) for v in units]))
    turned_acted(plan, pad_two, at_two)
    kernel_grad(plan, at_two, moved_g, acc_two)
    steps_two, steps_one = sum_two.steps(), sum_one.steps()
    steps_two.pop(0)()
    turn_weight(plan, weight_one, turned_one)
    a_two, b_two = group_means(totals[2].finish())
    steps_two.pop(0)()
    ex_l.wait()
    grads, at = [], 0
    for lift in assemble(ex_l, wide_l[pl.ds(0, plan.n)], inside):
        count = lift.shape[0]
        grads.append(scale_two * (lift - a_two - unit_h[pl.ds(at, count)] * b_two))
        at += count
    grads = clip(grads)
    shifted_grad(plan, moved_h, interior(grads[0]))
    kernel_grad(plan, at_one, moved_h, acc_one)
    steps_one.pop(0)()
    place_padded(plan, pad_h, *grads)
    steps_two.pop(0)()
    convolve_split(plan, pad_h, turned_one, wide_b, interior, True)
    steps_one.pop(0)()
    unit = unit_one(flat_block(ex_x))
    lifted = interior(wide_b[...] * slope(unit * gain_one + shift_one) * gain_one)
    wide_l[pl.ds(0, plan.n)] = lifted
    totals[3].start(column_sum(lifted), column_sum(lifted * unit))
    steps_two.pop(0)()
    convolve_split(plan, pad_two, weight_two, wide_b, interior, False)
    out_refs[0][0][...] = (flat_block(ex_x) + wide_b[...]).astype(BF16).reshape(
        plan.frames, plan.fn, c
    )
    outs[0].start()
    steps_one.pop(0)()
    a_one, b_one = group_means(totals[3].finish())
    steps_two.pop(0)()
    unit = unit_one(flat_block(ex_x))
    out_refs[1][0][...] = (
        flat_block(ex_g) + scale_one * (wide_l[pl.ds(0, plan.n)] - a_one - unit * b_one)
    ).astype(BF16).reshape(plan.frames, plan.fn, c)
    outs[1].start()

    slot = lax.broadcasted_iota(jnp.int32, (plan.h, SLOT, c), 1)

    def emit(k, target):
        mine, theirs = out_refs[k]
        outs[k].wait_recv()
        for f in range(plan.f):
            a = mine[plan.f * spot.t + f].astype(F32).reshape(plan.h, SLOT, c)
            b = theirs[f].astype(F32).reshape(plan.h, SLOT, c)
            low = jnp.where(spot.t == 0, a, b)
            high = jnp.where(spot.t == 0, b, a)
            low = jnp.where(slot < plan.half, low, high).astype(BF16)
            high = high.astype(BF16)
            for y in range(plan.h):
                target[f, y, 0:SLOT] = low[y]
                target[f, y, SLOT : plan.w] = high[y, 0 : plan.w - SLOT]

    steps_one.pop(0)()
    emit(0, block_out)
    while steps_two or steps_one:
        if steps_two:
            steps_two.pop(0)()
        if len(steps_one) == 2:
            emit(1, grad_input)
        if steps_one:
            steps_one.pop(0)()
    for item in [ex_x, ex_g, ex_h, ex_l] + totals + [sum_two, sum_one]:
        item.drain()
    for link in outs:
        link.wait_send()


def split_kernel(plan, features, cotangent, kernel_one, kernel_two, *norms):
    c, n = plan.c, plan.n
    frames, fn = plan.frames, plan.fn
    vm = pltpu.VMEM
    halos = []
    for k in range(4):
        edge = plan.f * plan.hs if k < 2 else plan.ext
        halos += [
            vm((frames, fn, c), BF16),
            vm((2, edge, c), BF16),
            vm((frames, SLOT, c), BF16),
            vm((frames, SLOT, c), BF16),
            vm((3, 2 * plan.ext, c), BF16),
        ]
    count = plan.ntm * plan.nrow * plan.ncol - 1
    vmem = pl.BlockSpec(memory_space=pltpu.VMEM)
    hbm = pl.BlockSpec(memory_space=pltpu.HBM)
    pads = plan.frames * plan.pn + SLOT
    return pl.pallas_call(
        functools.partial(split_body, plan),
        out_shape=(
            jax.ShapeDtypeStruct(features.shape, BF16),
            jax.ShapeDtypeStruct(features.shape, BF16),
            jax.ShapeDtypeStruct((plan.sum_rows, c), BF16),
            jax.ShapeDtypeStruct((plan.sum_rows, c), BF16),
        ),
        in_specs=[vmem] * 2 + [hbm] * 6,
        out_specs=(vmem,) * 4,
        scratch_shapes=[vm((plan.f * plan.h * plan.wide + 2 * plan.wide, c), F32)]
        + [vm((n + SLOT, c), F32)] * 2
        + [vm((n, c), F32)]
        + [vm((n + 2 * frames * SLOT, c), F32)]
        + [vm((n, 2 * plan.ext), BF16)]
        + [vm((frames * SLOT, 2 * plan.ext), BF16)] * 2
        + [vm((9, c, 3 * c), BF16)] * 4
        + [vm((pads, c), BF16)] * 4
        + [vm((3 * c, frames * plan.gn), BF16)] * 2
        + [vm((frames * plan.gn, 3 * c), BF16)] * 2
        + [vm((plan.sum_rows, c), F32)] * 2
        + [vm((1, c), F32)] * 4
        + [vm((2, plan.f, fn, c), BF16)] * 2
        + halos
        + [vm((8, c), F32), vm((count, 8, c), F32)] * 4
        + total_scratch(plan) * 2
        + [vm((frames, fn, c), BF16), vm((plan.f, fn, c), BF16)] * 2
        + [pltpu.SemaphoreType.DMA((MANY,))] * 2
        + [pltpu.SemaphoreType.DMA((16,))],
        compiler_params=pltpu.CompilerParams(
            collective_id=0, has_side_effects=True, vmem_limit_bytes=52 * 2**20
        ),
    )(features, cotangent, kernel_one, kernel_two, *norms)


def local_split(plan, features, cotangent, conv_one, conv_two, *norms):
    c = plan.c
    norms = [v.reshape(1, c) for v in norms]
    shape = (9, 3, c, c)
    block_out, grad_input, part_one, part_two = split_kernel(
        plan, features, cotangent, conv_one.reshape(shape), conv_two.reshape(shape), *norms
    )
    return (
        block_out,
        grad_input,
        part_one[: plan.taps_rows].astype(F32).reshape(conv_one.shape),
        part_two[: plan.taps_rows].astype(F32).reshape(conv_two.shape),
    )


def local(features, cotangent, conv_one, conv_two, gain_one, shift_one, gain_two, shift_two):
    f, h, w, c = features.shape
    sizes = tuple(lax.axis_size(a) for a in AXES)
    if Split.fits(f, h, w, c, sizes):
        return local_split(
            Split(f, h, w, c, sizes), features, cotangent, conv_one, conv_two,
            gain_one, shift_one, gain_two, shift_two,
        )
    plan = Plan(f, h, w, c, sizes)
    norms = [v.reshape(1, c) for v in (gain_one, shift_one, gain_two, shift_two)]
    block_out, grad_input, part_one, part_two = block_kernel(
        plan, features, cotangent, conv_one.reshape(-1, c), conv_two.reshape(-1, c), *norms
    )
    return (
        block_out,
        grad_input,
        part_one.astype(F32).reshape(conv_one.shape),
        part_two.astype(F32).reshape(conv_two.shape),
    )


def solution(mesh):
    block = P("tm", "row", "col", None)
    return jax.shard_map(
        local,
        mesh=mesh,
        in_specs=(block, block) + (P(),) * 6,
        out_specs=(block, block, P(), P()),
        check_vma=False,
    )
```

```python
import functools

import jax
import jax.numpy as jnp
from jax import lax
from jax.experimental import pallas as pl
from jax.experimental.pallas import tpu as pltpu
from jax.sharding import PartitionSpec as P

GROUPS = 32
EPSILON = 1e-05
MESH = pl.DeviceIdType.MESH
F32 = jnp.float32
BF16 = jnp.bfloat16
AXES = ("tm", "row", "col")


class Plan:
    def __init__(self, f, h, w, c, sizes):
        self.f, self.h, self.w, self.c = f, h, w, c
        self.wp = 16
        while self.wp < w + 2:
            self.wp *= 2
        self.n = f * h * self.wp
        self.hp = h + 2
        self.np = (f + 2) * self.hp * self.wp
        self.cb = -(-(f * h) // 16) * 16
        self.rb = 2 * self.wp
        self.ntm, self.nrow, self.ncol = sizes
        self.na = self.nrow
        self.nb = self.ntm * self.ncol
        self.taps_rows = 27 * c
        unit = 16 * self.ntm * self.nrow * self.ncol
        units = -(-self.taps_rows // unit)
        first = -(-units // 2)
        self.sum_rows = units * unit
        self.parts = [(0, first * unit)]
        if units > first:
            self.parts.append((first * unit, (units - first) * unit))

    def stages(self, order):
        near = 2 if self.ncol % 2 == 0 else 1
        known = dict(
            near=("col", 1, near, True),
            col=("col", near, self.ncol // near, False),
            tm=("tm", 1, self.ntm, False),
            row=("row", 1, self.nrow, False),
        )
        return [known[name] for name in order if known[name][2] > 1]


class Link:
    def __init__(self, src, dst, sems, index, device, sends, receives):
        self.make = lambda: pltpu.make_async_remote_copy(
            src_ref=src,
            dst_ref=dst,
            send_sem=sems[0].at[index],
            recv_sem=sems[1].at[index],
            device_id=device,
            device_id_type=MESH,
        )
        self.sends, self.receives = sends, receives

    def start(self):
        if self.sends is None:
            self.make().start()
            return

        @pl.when(self.sends)
        def _():
            self.make().start()

    def wait_send(self):
        if self.sends is None:
            self.make().wait_send()
            return

        @pl.when(self.sends)
        def _():
            self.make().wait_send()

    def wait_recv(self):
        if self.receives is None:
            self.make().wait_recv()
            return

        @pl.when(self.receives)
        def _():
            self.make().wait_recv()


class Place:
    def __init__(self, plan):
        self.t, self.r, self.c = (lax.axis_index(a) for a in AXES)
        self.has = dict(
            left=self.c > 0,
            right=self.c < plan.ncol - 1,
            up=self.r > 0,
            down=self.r < plan.nrow - 1,
            past=self.t > 0,
            future=self.t < plan.ntm - 1,
        )
        self.dev = dict(
            left={"col": self.c - 1},
            right={"col": self.c + 1},
            up={"row": self.r - 1},
            down={"row": self.r + 1},
            past={"tm": self.t - 1},
            future={"tm": self.t + 1},
        )

    def partners(self, plan):
        rows = [{"row": lax.rem(self.r + d, plan.na)} for d in range(1, plan.na)]
        index = self.t * plan.ncol + self.c
        others = []
        for d in range(1, plan.nb):
            to = lax.rem(index + d, plan.nb)
            others.append({"tm": lax.div(to, plan.ncol), "col": lax.rem(to, plan.ncol)})
        return rows, others


class Reduce:
    def __init__(self, plan, place, refs, sems, base):
        self.own, self.slots_a, self.mid, self.slots_b = refs
        rows, others = place.partners(plan)
        self.a = [
            Link(self.own, self.slots_a.at[d], sems, base + d, dev, None, None)
            for d, dev in enumerate(rows)
        ]
        self.b = [
            Link(self.mid, self.slots_b.at[d], sems, base + len(rows) + d, dev, None, None)
            for d, dev in enumerate(others)
        ]

    def start(self, first, second):
        self.own[...] = jnp.zeros_like(self.own)
        self.own[0:1] = first
        self.own[1:2] = second
        for link in self.a:
            link.start()

    def middle(self):
        for link in self.a:
            link.wait_recv()
        total = self.own[...]
        for d in range(len(self.a)):
            total = total + self.slots_a[d]
        self.mid[...] = total
        for link in self.b:
            link.start()

    def finish(self):
        for link in self.b:
            link.wait_recv()
        total = self.mid[...]
        for d in range(len(self.b)):
            total = total + self.slots_b[d]
        return total

    def drain(self):
        for link in self.a + self.b:
            link.wait_send()


class KernelSum:
    def __init__(self, plan, place, stages, span, acc, done, outs, ins, sems, base):
        self.acc, self.done, self.outs, self.ins = acc, done, outs, ins
        self.stages = stages
        at, count = span
        self.spans, self.reduce, self.gather = [], [], []
        for k, (axis, stride, ways, wide) in enumerate(stages):
            here = dict(tm=place.t, row=place.r, col=place.c)[axis]
            mine = lax.rem(lax.div(here, stride), ways)
            piece = count // ways
            aligned = lambda v: pl.multiple_of(v, 16)
            kept = aligned(at + mine * piece)
            links, sources = [], []
            for d in range(1, ways):
                other = lax.rem(mine + d, ways)
                dev = {axis: here + (other - mine) * stride}
                sent = aligned(at + other * piece)
                if wide:
                    src = acc.at[pl.ds(sent, piece)]
                else:
                    src = outs[k].at[d - 1]
                    sources.append((d - 1, sent))
                links.append((Link(src, ins[k].at[d - 1], sems, base, dev, None, None), dev))
                base += 1
            self.reduce.append([link for link, _ in links])
            gathers = []
            for _, dev in links:
                part = done.at[pl.ds(kept, piece)]
                gathers.append(Link(part, part, sems, base, dev, None, None))
                base += 1
            self.gather.append(gathers)
            self.spans.append((kept, piece, sources))
            at, count = kept, piece
        self.base = base

    def steps(self):
        out = []
        last = len(self.stages) - 1
        for k in range(len(self.stages)):
            out.append(functools.partial(self.reduce_step, k))
        for k in range(last, -1, -1):
            out.append(functools.partial(self.gather_step, k))
        out.append(self.last_step)
        return out

    def reduce_step(self, k):
        if k:
            self.settle(k - 1)
        kept, piece, sources = self.spans[k]
        for slot, sent in sources:
            self.outs[k][slot] = self.acc[pl.ds(sent, piece)].astype(BF16)
        for link in self.reduce[k]:
            link.start()

    def settle(self, k):
        kept, piece, _ = self.spans[k]
        for link in self.reduce[k]:
            link.wait_recv()
        total = self.acc[pl.ds(kept, piece)]
        for d in range(len(self.reduce[k])):
            total = total + self.ins[k][d].astype(F32)
        if k == len(self.stages) - 1:
            self.done[pl.ds(kept, piece)] = total.astype(BF16)
        else:
            self.acc[pl.ds(kept, piece)] = total

    def gather_step(self, k):
        if k == len(self.stages) - 1:
            self.settle(k)
        else:
            for link in self.gather[k + 1]:
                link.wait_recv()
        for link in self.gather[k]:
            link.start()

    def last_step(self):
        for link in self.gather[0]:
            link.wait_recv()

    def drain(self):
        for links in self.reduce + self.gather:
            for link in links:
                link.wait_send()


ORDERS = (("near", "col", "tm", "row"), ("near", "tm", "col", "row"))


def sum_scratch(plan):
    shapes, counts = [], []
    for order, (_, count) in zip(ORDERS, plan.parts):
        outs, ins = [], []
        for axis, stride, ways, wide in plan.stages(order):
            piece = count // ways
            shape = (ways - 1, piece, plan.c)
            outs.append(pltpu.VMEM((1, 16, plan.c) if wide else shape, BF16))
            ins.append(pltpu.VMEM(shape, F32 if wide else BF16))
            count = piece
        counts.append(len(outs))
        shapes += outs + ins
    return shapes, counts


def sum_sems(plan):
    return 2 * sum(
        stage[2] - 1 for order, _ in zip(ORDERS, plan.parts) for stage in plan.stages(order)
    )


EX_SEMS = 10


class Exchange:
    def __init__(self, plan, place, refs, sems, base, directions):
        self.plan, self.place, self.directions = plan, place, directions
        self.own, self.cols_out, self.cols_in, self.rows_out, self.rows_in = refs[:5]
        has, dev = place.has, place.dev
        cb, half = plan.cb, plan.f * plan.wp
        self.cols = [
            Link(self.cols_out.at[pl.ds(0, cb)], self.cols_in.at[pl.ds(0, cb)], sems, base,
                 dev["left"], has["left"], has["right"]),
            Link(self.cols_out.at[pl.ds(cb, cb)], self.cols_in.at[pl.ds(cb, cb)], sems, base + 1,
                 dev["right"], has["right"], has["left"]),
        ]
        self.rows = [
            Link(self.rows_out.at[pl.ds(0, half)], self.rows_in.at[pl.ds(half, half)], sems,
                 base + 2, dev["up"], has["up"], has["down"]),
            Link(self.rows_out.at[pl.ds(half, half)], self.rows_in.at[pl.ds(0, half)], sems,
                 base + 3, dev["down"], has["down"], has["up"]),
        ]
        self.tm = {}
        for k, source in enumerate(directions):
            block, cols, rows = refs[5 + 3 * k : 8 + 3 * k]
            target = "future" if source == "past" else "past"
            links = [
                Link(src, dst, sems, base + 4 + 3 * k + j, dev[target], has[target], has[source])
                for j, (src, dst) in enumerate(
                    [(self.own, block), (self.cols_in, cols), (self.rows_in, rows)]
                )
            ]
            self.tm[source] = ((block, cols, rows), links)

    def clear(self):
        cb, half = self.plan.cb, self.plan.f * self.plan.wp
        has = self.place.has

        def zero(ref, part, cond):
            @pl.when(jnp.logical_not(cond))
            def _():
                ref[part] = jnp.zeros(ref.at[part].shape, ref.dtype)

        zero(self.cols_in, pl.ds(0, cb), has["right"])
        zero(self.cols_in, pl.ds(cb, cb), has["left"])
        zero(self.rows_in, pl.ds(0, half), has["up"])
        zero(self.rows_in, pl.ds(half, half), has["down"])
        for source, (refs, _) in self.tm.items():
            for ref in refs:
                zero(ref, pl.ds(0, ref.shape[0]), has[source])

    def start(self, wide, pick):
        self.own[...] = wide[...].astype(BF16)
        for source in self.directions:
            self.tm[source][1][0].start()
        self.cols_out[...] = jnp.dot(pick[...], self.own[...], preferred_element_type=F32).astype(BF16)
        for link in self.cols:
            link.start()

    def middle(self, wide, spread):
        plan = self.plan
        for link in self.cols:
            link.wait_recv()
        for source in self.directions:
            self.tm[source][1][1].start()
        ends = spread_cols(self.cols_in, spread)
        size = plan.h * plan.wp
        for f in range(plan.f):
            for k, at in enumerate((f * size, (f + 1) * size - plan.wp)):
                self.rows_out[pl.ds((k * plan.f + f) * plan.wp, plan.wp)] = (
                    wide[pl.ds(at, plan.wp)] + ends[at : at + plan.wp]
                ).astype(BF16)
        for link in self.rows:
            link.start()

    def later(self):
        for link in self.rows:
            link.wait_recv()
        for source in self.directions:
            self.tm[source][1][2].start()

    def finish(self):
        for source in self.directions:
            for link in self.tm[source][1]:
                link.wait_recv()

    def drain(self):
        for link in self.cols + self.rows:
            link.wait_send()
        for source in self.directions:
            for link in self.tm[source][1]:
                link.wait_send()

    def pieces(self, wide, spread, source):
        plan = self.plan
        size = plan.h * plan.wp
        (block, cols, rows), _ = self.tm[source]

        def of(value, border, side):
            out = []
            for f in range(plan.f):
                top = border[pl.ds(f * plan.wp, plan.wp)].astype(F32)
                low = border[pl.ds((plan.f + f) * plan.wp, plan.wp)].astype(F32)
                out.append((side, top, value[f * size : (f + 1) * size], low))
            return out

        inner = of(wide[...] + spread_cols(self.cols_in, spread), self.rows_in, None)
        outer = of(block[...].astype(F32) + spread_cols(cols, spread), rows, source)
        if source == "past":
            return outer[plan.f - 2 :] + inner
        return inner + outer[:2]


def spread_cols(cols, spread):
    return jnp.dot(spread[...], cols[...], preferred_element_type=F32)


def silu(v):
    return v / (1.0 + jnp.exp(-v))


def slope(v):
    sigm = 1.0 / (1.0 + jnp.exp(-v))
    return sigm * (1.0 + v * (1.0 - sigm))


def valid(plan, place, count, side, border):
    has = place.has
    w = lax.broadcasted_iota(jnp.int32, (count, plan.c), 0) & (plan.wp - 1)
    one = lambda cond: cond.astype(jnp.int32)
    mask = jnp.where(
        w < plan.w,
        1,
        jnp.where(
            w == plan.w,
            one(has["right"]),
            jnp.where(w == plan.wp - 1, one(has["left"]), 0),
        ),
    )
    for name in (side, border):
        if name is not None:
            mask = mask * one(has[name])
    return mask > 0


def store_shifted(plan, ref, at, value):
    count = value.shape[0]
    rows = value.reshape(count // plan.wp, plan.wp, plan.c)
    before = pltpu.roll(rows, 1, axis=1).reshape(value.shape)
    after = pltpu.roll(rows, plan.wp - 1, axis=1).reshape(value.shape)
    c = plan.c
    ref[pl.ds(at, count), 0:c] = before.astype(BF16)
    ref[pl.ds(at, count), c : 2 * c] = value.astype(BF16)
    ref[pl.ds(at, count), 2 * c : 3 * c] = after.astype(BF16)


def build(plan, ref, frames):
    for k, (top, rows, low) in enumerate(frames):
        at = k * plan.hp * plan.wp
        store_shifted(plan, ref, at, top)
        store_shifted(plan, ref, at + plan.wp, rows)
        store_shifted(plan, ref, at + (plan.h + 1) * plan.wp, low)


def convolve(plan, ref, kernel, out):
    size = plan.h * plan.wp

    def frame(f, carry):
        pieces = []
        for p in range(3):
            for q in range(3):
                at = pl.multiple_of(((f + p) * plan.hp + q) * plan.wp, plan.wp)
                pieces.append(ref[pl.ds(at, size), :])
        wide = jnp.dot(jnp.concatenate(pieces, axis=1), kernel[...], preferred_element_type=F32)
        w = lax.broadcasted_iota(jnp.int32, wide.shape, 0) & (plan.wp - 1)
        out[pl.ds(pl.multiple_of(f * size, size), size), :] = jnp.where(w < plan.w, wide, 0.0)
        return carry

    lax.fori_loop(0, plan.f, frame, 0)


def kernel_term(plan, ref, turned, part, low, high):
    size = plan.h * plan.wp

    def tap(pq, carry):
        p, q = lax.div(pq, 3), lax.rem(pq, 3)
        pieces = []
        for f in range(plan.f):
            at = pl.multiple_of(((f + p) * plan.hp + q) * plan.wp, plan.wp)
            pieces.append(ref[pl.ds(at, size), :])
        term = jnp.dot(turned, jnp.concatenate(pieces, axis=0), preferred_element_type=F32)
        part[pl.ds(pl.multiple_of(pq * 3 * plan.c, 3 * plan.c), 3 * plan.c), :] = term.T
        return carry

    lax.fori_loop(low, high, tap, 0)


def turn_kernel(plan, kernel, out):
    taps, c = 27, plan.c

    def tap(k, carry):
        source = kernel[pl.ds(pl.multiple_of((taps - 1 - k) * c, c), c), :]
        out[pl.ds(pl.multiple_of(k * c, c), c), :] = source.astype(F32).T.astype(BF16)
        return carry

    lax.fori_loop(0, taps, tap, 0)


def spaced(plan, ref, wide):
    wide[...] = jnp.zeros_like(wide)
    for f in range(plan.f):
        for y in range(plan.h):
            wide[pl.ds((f * plan.h + y) * plan.wp, plan.w)] = ref[f, y].astype(F32)


def unspaced(plan, value, ref):
    for f in range(plan.f):
        for y in range(plan.h):
            at = (f * plan.h + y) * plan.wp
            ref[f, y] = value[at : at + plan.w].astype(BF16)


def column_sum(value):
    return jnp.sum(value, axis=0, keepdims=True)


def body(plan, n_ex, *refs):
    refs = list(refs)
    take = lambda k: [refs.pop(0) for _ in range(k)]
    features, cotangent, kernel_one, kernel_two, *norms = take(8)
    block_out, grad_input, part_one, part_two = take(4)
    wide_x, wide_g, wide_h, wide_l, wide_b = take(5)
    pick, spread, turned_one, turned_two = take(4)
    x3_one, x3_two, x3_g, x3_h = take(4)
    exchange_refs = [take(k) for k in n_ex]
    reduce_refs = [take(4) for _ in range(4)]
    acc_one, acc_two, done_one, done_two = take(4)
    sum_refs = []
    for _ in range(2):
        for count in sum_scratch(plan)[1]:
            sum_refs.append((take(count), take(count)))
    sems = take(2)

    place = Place(plan)
    rows, others = place.partners(plan)
    per_reduce = len(rows) + len(others)
    exchanges = [
        Exchange(plan, place, r, sems, EX_SEMS * k, d)
        for k, (r, d) in enumerate(
            zip(exchange_refs, (("past",), ("future",), ("past", "future"), ("future",)))
        )
    ]
    ex_x, ex_g, ex_h, ex_l = exchanges
    reduces = [
        Reduce(plan, place, r, sems, EX_SEMS * 4 + per_reduce * k)
        for k, r in enumerate(reduce_refs)
    ]
    sums = []
    base = EX_SEMS * 4 + per_reduce * 4
    for acc, done in ((acc_two, done_two), (acc_one, done_one)):
        for order, span in zip(ORDERS, plan.parts):
            outs, ins = sum_refs[len(sums)]
            sums.append(
                KernelSum(plan, place, plan.stages(order), span, acc, done, outs, ins, sems, base)
            )
            base = sums[-1].base
        acc[pl.ds(plan.taps_rows, plan.sum_rows - plan.taps_rows)] = jnp.zeros(
            (plan.sum_rows - plan.taps_rows, plan.c), F32
        )
    sums_two, sums_one = sums[: len(plan.parts)], sums[len(plan.parts) :]
    steps_two = [list(group) for group in zip(*[item.steps() for item in sums_two])]

    def advance():
        if steps_two:
            for step in steps_two.pop(0):
                step()

    for ex in exchanges:
        ex.clear()

    barrier = pltpu.get_barrier_semaphore()
    for dev in rows + others:
        pl.semaphore_signal(barrier, inc=1, device_id=dev, device_id_type=MESH)

    c = plan.c
    per_group = c // GROUPS
    members = float(plan.f * plan.h * plan.w * plan.ntm * plan.nrow * plan.ncol * per_group)
    lane_i = lax.broadcasted_iota(jnp.int32, (c, c), 0)
    lane_j = lax.broadcasted_iota(jnp.int32, (c, c), 1)
    same = (lax.div(lane_i, per_group) == lax.div(lane_j, per_group)).astype(F32)

    def group_means(total):
        sums = jnp.dot(
            total, same, preferred_element_type=F32, precision=lax.Precision.HIGHEST
        )
        return sums[0:1] / members, sums[1:2] / members

    def moments(total):
        average, square = group_means(total)
        return average, lax.rsqrt(square - average * average + EPSILON)

    spaced(plan, features, wide_x)
    j = lax.broadcasted_iota(jnp.int32, (2 * plan.cb, plan.n), 0)
    at = lax.broadcasted_iota(jnp.int32, (2 * plan.cb, plan.n), 1)
    first = j < plan.cb
    pick[...] = (
        at == jnp.where(first, j * plan.wp, (j - plan.cb) * plan.wp + plan.w - 1)
    ).astype(F32).astype(BF16)
    at = lax.broadcasted_iota(jnp.int32, (plan.n, 2 * plan.cb), 0)
    j = lax.broadcasted_iota(jnp.int32, (plan.n, 2 * plan.cb), 1)
    first = j < plan.cb
    spread[...] = (
        at == jnp.where(first, j * plan.wp + plan.w, (j - plan.cb) * plan.wp + plan.wp - 1)
    ).astype(F32).astype(BF16)

    pl.semaphore_wait(barrier, per_reduce)
    gain_one, shift_one, gain_two, shift_two = (ref[...] for ref in norms)

    x = wide_x[...]
    reduces[0].start(column_sum(x), column_sum(x * x))
    ex_x.start(wide_x, pick)
    spaced(plan, cotangent, wide_g)
    ex_g.start(wide_g, pick)
    reduces[0].middle()
    ex_x.middle(wide_x, spread)
    ex_g.middle(wide_g, spread)
    turn_kernel(plan, kernel_two, turned_two)
    ex_x.later()
    ex_g.later()
    turn_kernel(plan, kernel_one, turned_one)
    mean_one, scale_one = moments(reduces[0].finish())
    ex_x.finish()

    def unit_one(v):
        return (v - mean_one) * scale_one

    def frames_of(pieces, fn):
        out = []
        for side, top, rows_, low in pieces:
            keep = lambda v, border: jnp.where(
                valid(plan, place, v.shape[0], side, border), fn(v), 0.0
            )
            out.append((keep(top, "up"), keep(rows_, None), keep(low, "down")))
        return out

    build(
        plan,
        x3_one,
        frames_of(
            ex_x.pieces(wide_x, spread, "past"),
            lambda v: silu(unit_one(v) * gain_one + shift_one),
        ),
    )
    convolve(plan, x3_one, kernel_one, wide_h)
    hidden = wide_h[...]
    reduces[1].start(column_sum(hidden), column_sum(hidden * hidden))
    ex_h.start(wide_h, pick)
    reduces[1].middle()
    ex_h.middle(wide_h, spread)
    ex_g.finish()
    build(plan, x3_g, [p[1:] for p in ex_g.pieces(wide_g, spread, "future")])
    ex_h.later()
    convolve(plan, x3_g, turned_two, wide_b)
    mean_two, scale_two = moments(reduces[1].finish())

    def unit_two(v):
        return (v - mean_two) * scale_two

    unit = unit_two(wide_h[...])
    lifted = wide_b[...] * slope(unit * gain_two + shift_two) * gain_two
    wide_l[...] = lifted
    reduces[2].start(column_sum(lifted), column_sum(lifted * unit))
    ex_l.start(wide_l, pick)
    reduces[2].middle()
    ex_l.middle(wide_l, spread)
    ex_h.finish()
    build(
        plan,
        x3_two,
        frames_of(
            ex_h.pieces(wide_h, spread, "past"),
            lambda v: silu(unit_two(v) * gain_two + shift_two),
        ),
    )
    ex_l.later()
    kernel_term(plan, x3_two, wide_g[...].T.astype(BF16), acc_two, 0, 9)
    a_two, b_two = group_means(reduces[2].finish())
    advance()
    ex_l.finish()
    frames = []
    for (side, *lifts), (_, *hids) in zip(
        ex_l.pieces(wide_l, spread, "future"), ex_h.pieces(wide_h, spread, "future")
    ):
        out = []
        for border, lift, hid in zip(("up", None, "down"), lifts, hids):
            value = scale_two * (lift - a_two - unit_two(hid) * b_two)
            out.append(jnp.where(valid(plan, place, lift.shape[0], side, border), value, 0.0))
        frames.append(tuple(out))
    build(plan, x3_h, frames)
    advance()
    w = lax.broadcasted_iota(jnp.int32, (plan.h * plan.wp, c), 0) & (plan.wp - 1)
    own = jnp.concatenate(
        [jnp.where(w < plan.w, frames[f][1], 0.0) for f in range(plan.f)], axis=0
    )
    turned = own.T.astype(BF16)
    ready = min(9, -(-plan.parts[0][1] // (3 * c)))
    kernel_term(plan, x3_one, turned, acc_one, 0, ready)
    steps_one = [item.steps() for item in sums_one]
    steps_one[0].pop(0)()
    advance()
    kernel_term(plan, x3_one, turned, acc_one, ready, 9)
    for steps in steps_one[1:]:
        steps.pop(0)()

    def advance_one():
        for steps in steps_one:
            steps.pop(0)()

    convolve(plan, x3_h, turned_one, wide_b)
    unit = unit_one(wide_x[...])
    lifted = wide_b[...] * slope(unit * gain_one + shift_one) * gain_one
    reduces[3].start(column_sum(lifted), column_sum(lifted * unit))
    wide_l[...] = lifted
    advance_one()
    advance()
    reduces[3].middle()
    convolve(plan, x3_two, kernel_two, wide_b)
    advance_one()
    advance()
    unspaced(plan, wide_x[...] + wide_b[...], block_out)
    a_one, b_one = group_means(reduces[3].finish())
    advance_one()
    advance()
    unit = unit_one(wide_x[...])
    unspaced(
        plan,
        wide_g[...] + scale_one * (wide_l[...] - a_one - unit * b_one),
        grad_input,
    )
    while steps_one[0]:
        advance_one()
        advance()
    part_two[...] = done_two[pl.ds(0, plan.taps_rows)]
    part_one[...] = done_one[pl.ds(0, plan.taps_rows)]
    for item in exchanges + reduces + sums:
        item.drain()


def block_kernel(plan, features, cotangent, kernel_one, kernel_two, *norms):
    c, n = plan.c, plan.n
    half = plan.f * plan.wp
    exchange = []
    n_ex = []
    for count in (1, 1, 2, 1):
        shapes = [(n, c), (2 * plan.cb, c), (2 * plan.cb, c), (2 * half, c), (2 * half, c)]
        shapes += [(n, c), (2 * plan.cb, c), (2 * half, c)] * count
        n_ex.append(len(shapes))
        exchange += [pltpu.VMEM(s, BF16) for s in shapes]
    reduce = [
        pltpu.VMEM((8, c), F32),
        pltpu.VMEM((max(1, plan.na - 1), 8, c), F32),
        pltpu.VMEM((8, c), F32),
        pltpu.VMEM((max(1, plan.nb - 1), 8, c), F32),
    ] * 4
    sems = 4 * EX_SEMS + 4 * (plan.na + plan.nb - 2) + 2 * sum_sems(plan)
    vmem = pl.BlockSpec(memory_space=pltpu.VMEM)
    taps = kernel_one.shape[0]
    return pl.pallas_call(
        functools.partial(body, plan, n_ex),
        out_shape=(
            jax.ShapeDtypeStruct(features.shape, BF16),
            jax.ShapeDtypeStruct(features.shape, BF16),
            jax.ShapeDtypeStruct((taps, c), BF16),
            jax.ShapeDtypeStruct((taps, c), BF16),
        ),
        in_specs=[vmem] * 8,
        out_specs=(vmem,) * 4,
        scratch_shapes=[pltpu.VMEM((n, c), F32)] * 5
        + [pltpu.VMEM((2 * plan.cb, n), BF16), pltpu.VMEM((n, 2 * plan.cb), BF16)]
        + [pltpu.VMEM((taps, c), BF16)] * 2
        + [pltpu.VMEM((plan.np, 3 * c), BF16)] * 4
        + exchange
        + reduce
        + [pltpu.VMEM((plan.sum_rows, c), F32)] * 2
        + [pltpu.VMEM((plan.sum_rows, c), BF16)] * 2
        + sum_scratch(plan)[0] * 2
        + [pltpu.SemaphoreType.DMA((sems,))] * 2,
        compiler_params=pltpu.CompilerParams(
            collective_id=0, has_side_effects=True, vmem_limit_bytes=52 * 2**20
        ),
    )(features, cotangent, kernel_one, kernel_two, *norms)


SLOT = 16
MANY = 256
VMEM_ASK = 60 * 2**20


class Split:
    def __init__(self, f, h, w, c, sizes):
        self.f, self.h, self.w, self.c = f, h, w, c
        self.ntm, self.nrow, self.ncol = sizes
        self.frames = f * self.ntm
        self.half = w // 2
        self.fn = h * SLOT
        self.pn = (h + 2) * SLOT
        self.n = self.frames * self.fn
        self.hs = -(-h // 16) * 16
        self.ext = self.frames * self.hs
        self.wide = 2 * SLOT
        self.gn = -(-self.fn // 128) * 128
        self.taps_rows = 27 * c
        self.nxy = self.ntm * (self.ncol // 2)
        unit = 32 * self.nxy * self.nrow
        units = -(-self.taps_rows // unit)
        self.sum_rows = units * unit
        self.parts, at = [], 0
        third, rest = 2 * units // 7, 3 * units // 7
        for count, plane_first in (
            (third, False), (rest, True), (units - third - rest, True)
        ):
            if count:
                self.parts.append((at * unit, count * unit, plane_first))
            at += count
        self.cells = h * w
        self.cells_up = -(-self.cells // 8) * 8

    @staticmethod
    def fits(f, h, w, c, sizes):
        ntm, nrow, ncol = sizes
        return (
            ntm == 2
            and ncol % 2 == 0
            and w % 2 == 0
            and SLOT < w <= 2 * SLOT
            and w // 2 + 2 <= SLOT
            and w - SLOT <= w // 2 - 1
            and h <= 16
            and f * ntm * 16 <= 64
            and f * ntm >= 3
        )


class Spot:
    def __init__(self, plan):
        self.t, self.r, self.c = (lax.axis_index(a) for a in AXES)
        self.k = 2 * self.c + self.t
        self.left = self.k > 0
        self.right = self.k < 2 * plan.ncol - 1
        self.up = self.r > 0
        self.down = self.r < plan.nrow - 1
        self.core = lax.rem(self.c, 2)
        self.y = lax.div(self.c, 2)

    def peers(self, plan):
        offsets = [
            (dt, dr, dc)
            for dt in range(plan.ntm)
            for dr in range(plan.nrow)
            for dc in range(plan.ncol)
            if (dt, dr, dc) != (0, 0, 0)
        ]
        offsets.sort(key=lambda o: -(o[0] + min(1, o[2]) + 2 * (o[1] == plan.nrow // 2) + (o[1] > 0)))
        out = []
        for dt, dr, dc in offsets:
            out.append(
                {
                    "tm": lax.rem(self.t + dt, plan.ntm),
                    "row": lax.rem(self.r + dr, plan.nrow),
                    "col": lax.rem(self.c + dc, plan.ncol),
                }
            )
        return out

    def plane(self, plan):
        me = self.t * (plan.ncol // 2) + self.y
        out = []
        for d in range(1, plan.nxy):
            o = lax.rem(me + d, plan.nxy)
            dev = {
                "tm": lax.div(o, plan.ncol // 2),
                "col": 2 * lax.rem(o, plan.ncol // 2) + self.core,
            }
            out.append((o, dev))
        return me, out

    def line(self, plan):
        out = []
        for d in range(1, plan.nrow):
            o = lax.rem(self.r + d, plan.nrow)
            out.append((o, {"row": o}))
        return self.r, out


class Counter:
    def __init__(self):
        self.at = 0

    def take(self):
        self.at += 1
        return self.at - 1


class Total:
    def __init__(self, peers, own, slots, sems, counter):
        self.own, self.slots, self.peers, self.sems = own, slots, peers, sems
        self.index = counter.take()

    def start(self, first, second):
        self.own[0:1] = first
        self.own[1:2] = second
        for d, dev in enumerate(self.peers):
            pltpu.make_async_remote_copy(
                src_ref=self.own.at[pl.ds(0, 2)],
                dst_ref=self.slots.at[d, pl.ds(0, 2)],
                send_sem=self.sems[0].at[self.index],
                recv_sem=self.sems[1].at[self.index],
                device_id=dev,
                device_id_type=MESH,
            ).start()

    def whole(self, k):
        part = self.slots.at[pl.ds(0, len(self.peers)), pl.ds(0, 2)]
        return pltpu.make_async_copy(part, part, self.sems[k].at[self.index])

    def finish(self):
        self.whole(1).wait()
        total = self.own[0:2]
        for d in range(len(self.peers)):
            total = total + self.slots[d, 0:2]
        return total

    def drain(self):
        self.whole(0).wait()


class Halo:
    def __init__(self, plan, spot, refs, sems, counter):
        self.plan, self.spot = plan, spot
        self.block, self.edge, self.top, self.bot, self.ch = refs
        self.sems, self.counter = sems, counter
        self.links = []

    def link(self, src, dst, dev, sends, receives):
        item = Link(src, dst, self.sems, self.counter.take(), dev, sends, receives)
        self.links.append(item)
        return item

    def rows(self):
        s = self.spot
        return ((1, s.r + 1, s.down, s.up), (2, s.r - 1, s.up, s.down))

    def lines(self):
        s = self.spot
        return ((0, None, None, None),) + self.rows()

    def clear(self):
        for ref in (self.top, self.bot, self.ch):
            ref[...] = jnp.zeros(ref.shape, BF16)

    def wait(self):
        for link in self.links:
            link.wait_recv()

    def drain(self):
        for link in self.links:
            link.wait_send()


def both(*conds):
    out = None
    for cond in conds:
        if cond is not None:
            out = cond if out is None else jnp.logical_and(out, cond)
    return out


class Reshard(Halo):
    def __init__(self, plan, spot, pair, refs, sems, counter):
        super().__init__(plan, spot, refs, sems, counter)
        self.pair = pair
        t, r, c, f = spot.t, spot.r, spot.c, plan.f
        n = plan.ncol
        for which, row, sends, receives in self.rows():
            src_at = plan.fn - SLOT if which == 1 else 0
            dst = (self.top if which == 1 else self.bot).at[pl.ds(f * t, f)]
            for d in range(2):
                to = t if d == 0 else 1 - t
                self.link(pair.at[to, :, pl.ds(src_at, SLOT)], dst, {"tm": to, "row": row}, sends, receives)
        rows = f * plan.hs
        for which, row, sends, receives in self.lines():
            for d in range(2):
                dev = {"tm": t - d, "col": c + 1}
                if row is not None:
                    dev["row"] = row
                self.link(
                    self.edge.at[1], self.ch.at[which, pl.ds(rows * d, rows)], dev,
                    both(t == d, c < n - 1, sends), both(t == 0, c > 0, receives),
                )
                dev = {"tm": t - d + 1, "col": c - 1}
                if row is not None:
                    dev["row"] = row
                self.link(
                    self.edge.at[0], self.ch.at[which, pl.ds(plan.ext + rows * d, rows)], dev,
                    both(t == d, c > 0, sends), both(t == 1, c < n - 1, receives),
                )
        self.link(pair.at[1 - t], self.block.at[pl.ds(f * t, f)], {"tm": 1 - t}, None, None)

    def start(self, stage, rows, w32):
        plan, t = self.plan, self.spot.t
        step = 8 * plan.f
        for k in range(plan.cells_up // 8):
            rows[pl.ds(step * k, step)] = stage[pl.ds(8 * k, 8)].astype(F32).reshape(step, plan.c)
        for f in range(plan.f):
            for y in range(plan.h):
                w32[pl.ds((f * plan.h + y) * plan.wide, plan.w)] = rows[
                    pl.ds(y * plan.w * plan.f + f, plan.w, plan.f)
                ]
        slot = lax.broadcasted_iota(jnp.int32, (plan.h, SLOT, plan.c), 1)
        for f in range(plan.f):
            v = w32[pl.ds(f * plan.h * plan.wide, plan.h * plan.wide)]
            v = v.reshape(plan.h, plan.wide, plan.c)
            low, high = v[:, :SLOT], v[:, SLOT:]
            second = jnp.where(slot >= plan.half - 1, low, high)
            self.pair[0, f] = low.reshape(plan.fn, plan.c).astype(BF16)
            self.pair[1, f] = second.reshape(plan.fn, plan.c).astype(BF16)
            for side, x in ((0, 0), (1, plan.w - 1)):
                at = f * plan.h * plan.wide + x
                self.edge[side, pl.ds(f * plan.hs, plan.hs)] = w32[
                    pl.ds(at, plan.hs, plan.wide)
                ].astype(BF16)

    def send(self):
        for link in self.links:
            link.start()

    def keep(self):
        self.block[pl.ds(self.plan.f * self.spot.t, self.plan.f)] = self.pair[self.spot.t]


class Border(Halo):
    def __init__(self, plan, spot, refs, sems, counter):
        super().__init__(plan, spot, refs, sems, counter)
        t, c = spot.t, spot.c
        for which, row, sends, receives in self.rows():
            at = plan.fn - SLOT if which == 1 else 0
            dst = self.top if which == 1 else self.bot
            self.link(self.block.at[:, pl.ds(at, SLOT)], dst, {"row": row}, sends, receives)
        for which, row, sends, receives in self.lines():
            dev = {"tm": 1 - t, "col": c - 1 + t}
            if row is not None:
                dev["row"] = row
            self.link(
                self.edge.at[0], self.ch.at[which, pl.ds(plan.ext, plan.ext)], dev,
                both(spot.left, sends), both(spot.right, receives),
            )
            dev = {"tm": 1 - t, "col": c + t}
            if row is not None:
                dev["row"] = row
            self.link(
                self.edge.at[1], self.ch.at[which, pl.ds(0, plan.ext)], dev,
                both(spot.right, sends), both(spot.left, receives),
            )

    def start(self, wide):
        plan, t = self.plan, self.spot.t
        for f in range(plan.frames):
            self.block[f] = wide[pl.ds(f * plan.fn, plan.fn)].astype(BF16)
            for side, offset in ((0, 0), (1, plan.half - 1)):
                values = [
                    wide[pl.ds(f * plan.fn + (plan.half * k + offset) % SLOT, plan.hs, SLOT)]
                    for k in range(2)
                ]
                self.edge[side, pl.ds(f * plan.hs, plan.hs)] = jnp.where(
                    t == 0, values[0], values[1]
                ).astype(BF16)
        for link in self.links:
            link.start()


class Part:
    def __init__(self, plan, spot, span, acc, done, out, refs, sems, counter, local_sem):
        self.acc, self.done = acc, done
        self.core_in, out1, self.in1, out2, self.in2 = refs
        self.at, self.count, plane_first = span
        rows = pl.ds(self.at, min(self.count, plan.taps_rows - self.at))
        self.out = pltpu.make_async_copy(done.at[rows], out.at[rows], local_sem)
        link = lambda src, dst, dev: Link(src, dst, sems, counter.take(), dev, None, None)
        aligned = lambda v: pl.multiple_of(v, 16)
        half = self.count // 2
        base = aligned(self.at + spot.core * half)
        other = aligned(self.at + (1 - spot.core) * half)
        sibling = {"col": spot.c + 1 - 2 * spot.core}
        self.core = link(acc.at[pl.ds(other, half)], self.core_in, sibling)
        stages = (spot.plane(plan), spot.line(plan))
        if not plane_first:
            stages = stages[::-1]
        (one, ones), (two, twos) = stages
        self.big = big = half // (len(ones) + 1)
        self.small = small = big // (len(twos) + 1)
        self.own1_in = aligned(one * big)
        self.own1 = own1 = aligned(base + one * big)
        self.own2 = own2 = aligned(own1 + two * small)
        self.send1 = [
            (aligned(base + o * big), aligned(o * big), out1.at[d], link(out1.at[d], self.in1.at[d], dev))
            for d, (o, dev) in enumerate(ones)
        ]
        self.send2 = [
            (aligned(own1 + o * small), out2.at[d], link(out2.at[d], self.in2.at[d], dev))
            for d, (o, dev) in enumerate(twos)
        ]
        piece2 = done.at[pl.ds(own2, small)]
        self.gather2 = [link(piece2, piece2, dev) for _, dev in twos]
        piece1 = done.at[pl.ds(own1, big)]
        self.gather1 = [link(piece1, piece1, dev) for _, dev in ones]
        self.forward = [link(piece1, piece1, sibling)]
        for d in range(len(ones)):
            o, _ = ones[len(ones) - 1 - d]
            ref = done.at[pl.ds(aligned(base + o * big), big)]
            self.forward.append(link(ref, ref, sibling))

    def start(self):
        self.core.start()

    def first(self):
        self.core.wait_recv()
        for at, inside, out, link in self.send1:
            out[...] = (
                self.acc[pl.ds(at, self.big)] + self.core_in[pl.ds(inside, self.big)]
            ).astype(BF16)
            link.start()

    def second(self):
        big, own1 = self.big, self.own1
        total = self.acc[pl.ds(own1, big)] + self.core_in[pl.ds(self.own1_in, big)]
        for d, item in enumerate(self.send1):
            item[-1].wait_recv()
            total = total + self.in1[d].astype(F32)
        self.acc[pl.ds(own1, big)] = total
        for at, out, link in self.send2:
            out[...] = self.acc[pl.ds(at, self.small)].astype(BF16)
            link.start()

    def third(self):
        total = self.acc[pl.ds(self.own2, self.small)]
        for d, item in enumerate(self.send2):
            item[-1].wait_recv()
            total = total + self.in2[d].astype(F32)
        self.done[pl.ds(self.own2, self.small)] = total.astype(BF16)
        for link in self.gather2:
            link.start()

    def fourth(self):
        for link in self.gather2:
            link.wait_recv()
        for link in self.gather1:
            link.start()
        self.forward[0].start()

    def fifth(self):
        for d, link in enumerate(self.gather1):
            link.wait_recv()
            self.forward[1 + d].start()

    def sixth(self):
        for link in self.forward:
            link.wait_recv()
        self.out.start()

    def drain(self):
        self.core.wait_send()
        for item in self.send1 + self.send2:
            item[-1].wait_send()
        for link in self.gather2 + self.gather1 + self.forward:
            link.wait_send()
        self.out.wait()


def part_scratch(plan):
    shapes = []
    for _, count, plane_first in plan.parts:
        ways = (plan.nxy, plan.nrow) if plane_first else (plan.nrow, plan.nxy)
        big = count // 2 // ways[0]
        small = big // ways[1]
        shapes.append(pltpu.VMEM((count // 2, plan.c), F32))
        for rows, k in ((big, ways[0]), (big, ways[0]), (small, ways[1]), (small, ways[1])):
            shapes.append(pltpu.VMEM((max(1, k - 1), rows, plan.c), BF16))
    return shapes


def around(value, by):
    rows = value.reshape(value.shape[0] // SLOT, SLOT, value.shape[1])
    return pltpu.roll(rows, by, axis=1).reshape(value.shape)


def convolve_split(plan, padded, weight, out, keep, future):
    c = plan.c
    for t in range(plan.frames):
        pieces, used = [], []
        for p in range(3):
            source = t + p if future else t + p - 2
            if not 0 <= source < plan.frames:
                continue
            used.append(p)
            for q in range(3):
                pieces.append(padded[pl.ds(source * plan.pn + q * SLOT, plan.fn), :])
        lhs = jnp.concatenate(pieces, axis=1)
        rhs = weight[3 * used[0] : 3 * used[-1] + 3].reshape(3 * len(used) * c, 3 * c)
        wide = jnp.dot(lhs, rhs, preferred_element_type=F32)
        total = around(wide[:, 0:c], 1) + wide[:, c : 2 * c] + around(wide[:, 2 * c :], SLOT - 1)
        out[pl.ds(t * plan.fn, plan.fn), :] = keep(total)


def place_padded(plan, ref, value, top, bot):
    for t in range(plan.frames):
        at = t * plan.pn
        ref[pl.ds(at, SLOT), :] = top[t * SLOT : (t + 1) * SLOT].astype(BF16)
        ref[pl.ds(at + SLOT, plan.fn), :] = value[t * plan.fn : (t + 1) * plan.fn].astype(BF16)
        ref[pl.ds(at + SLOT + plan.fn, SLOT), :] = bot[t * SLOT : (t + 1) * SLOT].astype(BF16)


def shifted_grad(plan, ref, value):
    c = plan.c
    for s, moved in enumerate((around(value, SLOT - 1), value, around(value, 1))):
        for t in range(plan.frames):
            ref[pl.ds(t * plan.gn, plan.fn), s * c : (s + 1) * c] = moved[
                t * plan.fn : (t + 1) * plan.fn
            ].astype(BF16)


def turned_acted(plan, padded, ref):
    c = plan.c
    for q in range(3):
        for t in range(plan.frames):
            slab = padded[pl.ds(t * plan.pn + q * SLOT, plan.gn), :]
            ref[q * c : (q + 1) * c, t * plan.gn : (t + 1) * plan.gn] = slab.T


def kernel_grad(plan, turned, moved, acc, p):
    c = plan.c
    lag = 2 - p
    count = (plan.frames - lag) * plan.gn
    term = jnp.dot(
        turned[:, 0:count], moved[pl.ds(lag * plan.gn, count), :], preferred_element_type=F32
    )
    for q in range(3):
        for s in range(3):
            acc[pl.ds((9 * p + 3 * q + s) * c, c), :] = term[
                q * c : (q + 1) * c, s * c : (s + 1) * c
            ]


def turn_weight(plan, weight, out):
    c = plan.c
    for k in range(27):
        j = 26 - k
        source = weight[j // 3, :, (j % 3) * c : (j % 3 + 1) * c]
        out[k // 3, :, (k % 3) * c : (k % 3 + 1) * c] = source.T


def split_body(plan, *refs):
    refs = list(refs)
    take = lambda k: [refs.pop(0) for _ in range(k)]
    features, cotangent, conv_one, conv_two, *norms = take(8)
    block_out, grad_input, part_one, part_two = take(4)
    w32, rows32, stage_x, stage_g = take(4)
    done_one, done_two = take(2)
    wide_h, wide_l, wide_b, unit_h = take(4)
    spread_mid, spread_top, spread_bot = take(3)
    weight_one, weight_two, turned_one, turned_two = take(4)
    pad_one, pad_two, pad_g, pad_h = take(4)
    at_one, at_two, moved_g, moved_h = take(4)
    acc_one, acc_two = take(2)
    norm_in = take(4)
    pair_x, pair_g = take(2)
    halo_refs = [take(5) for _ in range(4)]
    total_refs = [take(2) for _ in range(4)]
    sum_refs = [[take(5) for _ in plan.parts] for _ in range(2)]
    out_refs = [take(2) for _ in range(2)]
    sems = take(2)
    (local_sem,) = take(1)

    spot = Spot(plan)
    peers = spot.peers(plan)
    counter = Counter()
    c = plan.c

    loads = []
    cells = pl.ds(0, plan.cells)
    for k, (src, dst) in enumerate(
        [(features, stage_x.at[cells]), (cotangent, stage_g.at[cells])]
        + list(zip(norms, norm_in))
        + [(conv_one.at[:, s], weight_one.at[:, :, pl.ds(s * c, c)]) for s in range(3)]
        + [(conv_two.at[:, s], weight_two.at[:, :, pl.ds(s * c, c)]) for s in range(3)]
    ):
        copy = pltpu.make_async_copy(src, dst, local_sem.at[k])
        copy.start()
        loads.append(copy)

    ex_x = Reshard(plan, spot, pair_x, halo_refs[0], sems, counter)
    ex_g = Reshard(plan, spot, pair_g, halo_refs[1], sems, counter)
    ex_h = Border(plan, spot, halo_refs[2], sems, counter)
    ex_l = Border(plan, spot, halo_refs[3], sems, counter)
    totals = [Total(peers, *r, sems, counter) for r in total_refs]
    sums_two, sums_one = (
        [
            Part(plan, spot, span, acc, done, out, r, sems, counter, local_sem.at[first + k])
            for k, (span, r) in enumerate(zip(plan.parts, group))
        ]
        for acc, done, out, group, first in (
            (acc_two, done_two, part_two, sum_refs[0], 16),
            (acc_one, done_one, part_one, sum_refs[1], 16 + len(plan.parts)),
        )
    )
    outs = []
    for (mine, theirs) in out_refs:
        outs.append(
            Link(
                mine.at[pl.ds(plan.f * (1 - spot.t), plan.f)], theirs, sems, counter.take(),
                {"tm": 1 - spot.t}, None, None,
            )
        )
    assert counter.at <= MANY

    for ex in (ex_x, ex_g, ex_h, ex_l):
        ex.clear()
    barrier = pltpu.get_barrier_semaphore()
    for dev in peers:
        pl.semaphore_signal(barrier, inc=1, device_id=dev, device_id_type=MESH)

    per_group = c // GROUPS
    members = float(plan.n // SLOT * plan.half * 2 * plan.nrow * plan.ncol * per_group)
    lane_i = lax.broadcasted_iota(jnp.int32, (c, c), 0)
    lane_j = lax.broadcasted_iota(jnp.int32, (c, c), 1)
    same = (lax.div(lane_i, per_group) == lax.div(lane_j, per_group)).astype(F32)

    def group_means(total):
        sums = jnp.dot(total, same, preferred_element_type=F32, precision=lax.Precision.HIGHEST)
        return sums[0:1] / members, sums[1:2] / members

    def moments(total):
        average, square = group_means(total)
        return average, lax.rsqrt(square - average * average + EPSILON)

    w32[...] = jnp.zeros(w32.shape, F32)
    for stage in (stage_x, stage_g):
        spare = plan.cells_up - plan.cells
        if spare:
            stage[pl.ds(plan.cells, spare)] = jnp.zeros((spare, plan.f, c), BF16)
    loads[0].wait()
    ex_x.start(stage_x, rows32, w32)
    x = w32[...]
    first, second = column_sum(x), column_sum(x * x)
    pl.semaphore_wait(barrier, len(peers))
    totals[0].start(first, second)
    ex_x.send()
    loads[1].wait()
    ex_g.start(stage_g, rows32, w32)
    ex_g.send()
    ex_x.keep()
    ex_g.keep()

    rel = (lax.broadcasted_iota(jnp.int32, (SLOT, c), 0) - plan.half * spot.t) & (SLOT - 1)
    one = lambda cond: cond.astype(jnp.int32)
    inside = rel < plan.half
    inner = jnp.where(spot.t == 0, plan.half, SLOT - 1)
    kept = jnp.logical_or(inside, rel == inner)
    legal = jnp.where(
        inside, 1, jnp.where(rel == plan.half, one(spot.right), jnp.where(rel == SLOT - 1, one(spot.left), 0))
    )

    def masked(value, mask):
        rows = value.reshape(value.shape[0] // SLOT, SLOT, c)
        return jnp.where(mask[None], rows, 0.0).reshape(value.shape)

    interior = lambda value: masked(value, inside)

    def targets(rows, source):
        i = lax.broadcasted_iota(jnp.int32, (rows, 2 * plan.ext), 0)
        j = lax.broadcasted_iota(jnp.int32, (rows, 2 * plan.ext), 1)
        where = ((i & (SLOT - 1)) - plan.half * spot.t) & (SLOT - 1)
        code = source(i >> 4)
        aim = jnp.where(where == SLOT - 1, code, jnp.where(where == plan.half, code + plan.ext, -1))
        return (j == aim).astype(F32).astype(BF16)

    def of_group(g):
        t = 0
        for k in range(1, plan.frames):
            t = t + (g >= k * plan.h).astype(jnp.int32)
        return g + t * (plan.hs - plan.h)

    spread_mid[...] = targets(plan.n, of_group)
    spread_top[...] = targets(plan.frames * SLOT, lambda t: t * plan.hs + plan.h - 1)
    spread_bot[...] = targets(plan.frames * SLOT, lambda t: t * plan.hs)
    for ref in (pad_one, pad_two):
        ref[pl.ds(plan.frames * plan.pn, SLOT), :] = jnp.zeros((SLOT, c), BF16)
    if plan.gn > plan.fn:
        for ref in (moved_g, moved_h):
            for t in range(plan.frames):
                ref[pl.ds(t * plan.gn + plan.fn, plan.gn - plan.fn), :] = jnp.zeros(
                    (plan.gn - plan.fn, 3 * c), BF16
                )
    for ref in (wide_h, wide_l):
        ref[pl.ds(plan.n, SLOT), :] = jnp.zeros((SLOT, c), F32)
    for acc in (acc_one, acc_two):
        acc[pl.ds(plan.taps_rows, plan.sum_rows - plan.taps_rows)] = jnp.zeros(
            (plan.sum_rows - plan.taps_rows, c), F32
        )
    for copy in loads[2:]:
        copy.wait()
    gain_one, shift_one, gain_two, shift_two = (ref[...] for ref in norm_in)
    turn_weight(plan, weight_two, turned_two)

    def assemble(ex, value, mask):
        flat = lambda ref: ref[...].astype(F32).reshape(plan.frames * SLOT, c)
        spread = lambda by, k: jnp.dot(by[...], ex.ch[k], preferred_element_type=F32)
        return (
            masked(value, mask) + spread(spread_mid, 0),
            masked(flat(ex.top), mask) + spread(spread_top, 1),
            masked(flat(ex.bot), mask) + spread(spread_bot, 2),
        )

    def clip(values):
        value, top, bot = values
        return (
            masked(value, legal > 0),
            masked(top, legal * one(spot.up) > 0),
            masked(bot, legal * one(spot.down) > 0),
        )

    def flat_block(ex):
        return ex.block[...].astype(F32).reshape(plan.n, c)

    ex_x.wait()
    values_x = assemble(ex_x, flat_block(ex_x), kept)
    mean_one, scale_one = moments(totals[0].finish())

    def unit_one(v):
        return (v - mean_one) * scale_one

    place_padded(
        plan, pad_one, *clip([silu(unit_one(v) * gain_one + shift_one) for v in values_x])
    )
    convolve_split(plan, pad_one, weight_one, wide_h, interior, False)
    hidden = wide_h[pl.ds(0, plan.n)]
    totals[1].start(column_sum(hidden), column_sum(hidden * hidden))
    ex_h.start(wide_h)

    ex_g.wait()
    place_padded(plan, pad_g, *clip(assemble(ex_g, flat_block(ex_g), kept)))
    convolve_split(plan, pad_g, turned_two, wide_b, interior, True)
    shifted_grad(plan, moved_g, interior(flat_block(ex_g)))
    turned_acted(plan, pad_one, at_one)
    mean_two, scale_two = moments(totals[1].finish())

    def unit_two(v):
        return (v - mean_two) * scale_two

    unit = unit_two(wide_h[pl.ds(0, plan.n)])
    lifted = interior(wide_b[...] * slope(unit * gain_two + shift_two) * gain_two)
    wide_l[pl.ds(0, plan.n)] = lifted
    totals[2].start(column_sum(lifted), column_sum(lifted * unit))
    ex_l.start(wide_l)

    ex_h.wait()
    units = [unit_two(v) for v in assemble(ex_h, wide_h[pl.ds(0, plan.n)], inside)]
    at = 0
    for v in units:
        unit_h[pl.ds(at, v.shape[0])] = v
        at += v.shape[0]
    place_padded(plan, pad_two, *clip([silu(v * gain_two + shift_two) for v in units]))
    turned_acted(plan, pad_two, at_two)
    def starts(parts, p):
        ready = plan.taps_rows if p == 2 else (p + 1) * 9 * c
        before = p * 9 * c
        for part in parts:
            end = min(part.at + part.count, plan.taps_rows)
            if before < end <= ready:
                part.start()

    for p in range(3):
        kernel_grad(plan, at_two, moved_g, acc_two, p)
        starts(sums_two, p)
    turn_weight(plan, weight_one, turned_one)
    for part in sums_two:
        part.first()
    a_two, b_two = group_means(totals[2].finish())
    ex_l.wait()
    grads, at = [], 0
    for lift in assemble(ex_l, wide_l[pl.ds(0, plan.n)], inside):
        count = lift.shape[0]
        grads.append(scale_two * (lift - a_two - unit_h[pl.ds(at, count)] * b_two))
        at += count
    grads = clip(grads)
    shifted_grad(plan, moved_h, interior(grads[0]))
    for p in range(3):
        kernel_grad(plan, at_one, moved_h, acc_one, p)
        starts(sums_one, p)
    place_padded(plan, pad_h, *grads)
    sums_one[0].first()
    for part in sums_two[:2]:
        part.second()
    convolve_split(plan, pad_h, turned_one, wide_b, interior, True)
    for part in sums_one[1:]:
        part.first()
    unit = unit_one(flat_block(ex_x))
    lifted = interior(wide_b[...] * slope(unit * gain_one + shift_one) * gain_one)
    wide_l[pl.ds(0, plan.n)] = lifted
    totals[3].start(column_sum(lifted), column_sum(lifted * unit))
    for part in sums_two[2:]:
        part.second()
    convolve_split(plan, pad_two, weight_two, wide_b, interior, False)
    out_refs[0][0][...] = (flat_block(ex_x) + wide_b[...]).astype(BF16).reshape(
        plan.frames, plan.fn, c
    )
    outs[0].start()
    for part in sums_two:
        part.third()
    sums_one[0].second()
    a_one, b_one = group_means(totals[3].finish())
    unit = unit_one(flat_block(ex_x))
    out_refs[1][0][...] = (
        flat_block(ex_g) + scale_one * (wide_l[pl.ds(0, plan.n)] - a_one - unit * b_one)
    ).astype(BF16).reshape(plan.frames, plan.fn, c)
    outs[1].start()
    for part in sums_one[1:]:
        part.second()
    for part in sums_two:
        part.fourth()

    slot = lax.broadcasted_iota(jnp.int32, (plan.h, SLOT, c), 1)

    leave = [
        pltpu.make_async_copy(stage.at[cells], target, local_sem.at[14 + k])
        for k, (stage, target) in enumerate(((stage_x, block_out), (stage_g, grad_input)))
    ]

    def emit(k, stage):
        mine, theirs = out_refs[k]
        outs[k].wait_recv()
        for f in range(plan.f):
            a = mine[plan.f * spot.t + f].astype(F32).reshape(plan.h, SLOT, c)
            b = theirs[f].astype(F32).reshape(plan.h, SLOT, c)
            low = jnp.where(spot.t == 0, a, b)
            high = jnp.where(spot.t == 0, b, a)
            low = jnp.where(slot < plan.half, low, high)
            for y in range(plan.h):
                at = y * plan.w * plan.f + f
                rows32[pl.ds(at, SLOT, plan.f)] = low[y]
                rows32[pl.ds(at + SLOT * plan.f, plan.w - SLOT, plan.f)] = high[y, 0 : plan.w - SLOT]
        for at in range(0, plan.cells, 8):
            n = min(8, plan.cells - at)
            block = rows32[pl.ds(at * plan.f, n * plan.f)]
            stage[pl.ds(at, n)] = block.reshape(n, plan.f, c).astype(BF16)
        leave[k].start()

    emit(0, stage_x)
    for part in sums_one:
        part.third()
    for part in sums_two:
        part.fifth()
    emit(1, stage_g)
    for part in sums_one:
        part.fourth()
    for part in sums_two:
        part.sixth()
    for part in sums_one:
        part.fifth()
    for part in sums_one:
        part.sixth()
    for item in [ex_x, ex_g, ex_h, ex_l] + totals + sums_two + sums_one:
        item.drain()
    for link in outs:
        link.wait_send()
    for copy in leave:
        copy.wait()


def split_kernel(plan, features, cotangent, kernel_one, kernel_two, *norms):
    c, n = plan.c, plan.n
    frames, fn = plan.frames, plan.fn
    vm = pltpu.VMEM
    halos = []
    for k in range(4):
        edge = plan.f * plan.hs if k < 2 else plan.ext
        halos += [
            vm((frames, fn, c), BF16),
            vm((2, edge, c), BF16),
            vm((frames, SLOT, c), BF16),
            vm((frames, SLOT, c), BF16),
            vm((3, 2 * plan.ext, c), BF16),
        ]
    count = plan.ntm * plan.nrow * plan.ncol - 1
    hbm = pl.BlockSpec(memory_space=pltpu.HBM)
    pads = plan.frames * plan.pn + SLOT
    return pl.pallas_call(
        functools.partial(split_body, plan),
        out_shape=(
            jax.ShapeDtypeStruct(features.shape, BF16),
            jax.ShapeDtypeStruct(features.shape, BF16),
            jax.ShapeDtypeStruct((plan.taps_rows, c), BF16),
            jax.ShapeDtypeStruct((plan.taps_rows, c), BF16),
        ),
        in_specs=[hbm] * 8,
        out_specs=(hbm,) * 4,
        scratch_shapes=[vm((plan.f * plan.h * plan.wide + 2 * plan.wide, c), F32)]
        + [vm((plan.cells_up * plan.f, c), F32)]
        + [vm((plan.cells_up, plan.f, c), BF16)] * 2
        + [vm((plan.sum_rows, c), BF16)] * 2
        + [vm((n + SLOT, c), F32)] * 2
        + [vm((n, c), F32)]
        + [vm((n + 2 * frames * SLOT, c), F32)]
        + [vm((n, 2 * plan.ext), BF16)]
        + [vm((frames * SLOT, 2 * plan.ext), BF16)] * 2
        + [vm((9, c, 3 * c), BF16)] * 4
        + [vm((pads, c), BF16)] * 4
        + [vm((3 * c, frames * plan.gn), BF16)] * 2
        + [vm((frames * plan.gn, 3 * c), BF16)] * 2
        + [vm((plan.sum_rows, c), F32)] * 2
        + [vm((1, c), F32)] * 4
        + [vm((2, plan.f, fn, c), BF16)] * 2
        + halos
        + [vm((8, c), F32), vm((count, 8, c), F32)] * 4
        + part_scratch(plan) * 2
        + [vm((frames, fn, c), BF16), vm((plan.f, fn, c), BF16)] * 2
        + [pltpu.SemaphoreType.DMA((MANY,))] * 2
        + [pltpu.SemaphoreType.DMA((32,))],
        compiler_params=pltpu.CompilerParams(
            collective_id=0, has_side_effects=True, vmem_limit_bytes=VMEM_ASK
        ),
    )(features, cotangent, kernel_one, kernel_two, *norms)


def widen_body(parts, *refs):
    ins, outs, narrow, wide, held, sems = refs[:4], refs[4:8], *refs[8:]
    moves = [pltpu.make_async_copy(ins[k], held.at[k], sems.at[0, k]) for k in range(2)]
    leave = [pltpu.make_async_copy(held.at[k], outs[k], sems.at[0, 2 + k]) for k in range(2)]
    loads, stores = [], []
    for a in range(2):
        for j, (at, count) in enumerate(parts):
            rows = pl.ds(at, count)
            k = len(parts) * a + j
            loads.append(
                pltpu.make_async_copy(ins[2 + a].at[rows], narrow.at[a, rows], sems.at[1, k])
            )
            stores.append(
                pltpu.make_async_copy(wide.at[a, rows], outs[2 + a].at[rows], sems.at[2, k])
            )
    for copy in loads[: len(parts)] + moves + loads[len(parts) :]:
        copy.start()
    for a in range(2):
        for j, (at, count) in enumerate(parts):
            k = len(parts) * a + j
            loads[k].wait()
            wide[a, pl.ds(at, count)] = narrow[a, pl.ds(at, count)].astype(F32)
            stores[k].start()
        moves[a].wait()
        leave[a].start()
    for copy in stores + leave:
        copy.wait()


def widen(block_out, grad_input, part_one, part_two):
    rows, c = part_one.shape
    piece = -(-rows // 64) * 16
    parts = [(at, min(piece, rows - at)) for at in range(0, rows, piece)]
    hbm = pl.BlockSpec(memory_space=pltpu.HBM)
    shape = jax.ShapeDtypeStruct
    return pl.pallas_call(
        functools.partial(widen_body, parts),
        out_shape=(
            shape(block_out.shape, BF16),
            shape(grad_input.shape, BF16),
            shape((rows, c), F32),
            shape((rows, c), F32),
        ),
        in_specs=[hbm] * 4,
        out_specs=(hbm,) * 4,
        scratch_shapes=[
            pltpu.VMEM((2, rows, c), BF16),
            pltpu.VMEM((2, rows, c), F32),
            pltpu.VMEM((2,) + block_out.shape, BF16),
            pltpu.SemaphoreType.DMA((3, 2 * len(parts))),
        ],
        compiler_params=pltpu.CompilerParams(vmem_limit_bytes=VMEM_ASK),
    )(block_out, grad_input, part_one, part_two)


def local_split(plan, features, cotangent, conv_one, conv_two, *norms):
    c = plan.c
    norms = [v.reshape(1, c) for v in norms]
    shape = (9, 3, c, c)
    turn = lambda v: v.transpose(1, 2, 0, 3).reshape(plan.cells, plan.f, c)
    back = lambda v: v.reshape(plan.h, plan.w, plan.f, c).transpose(2, 0, 1, 3)
    block_out, grad_input, part_one, part_two = widen(
        *split_kernel(
            plan, turn(features), turn(cotangent), conv_one.reshape(shape), conv_two.reshape(shape), *norms
        )
    )
    return (
        back(block_out),
        back(grad_input),
        part_one.reshape(conv_one.shape),
        part_two.reshape(conv_two.shape),
    )


def local(features, cotangent, conv_one, conv_two, gain_one, shift_one, gain_two, shift_two):
    f, h, w, c = features.shape
    sizes = tuple(lax.axis_size(a) for a in AXES)
    if Split.fits(f, h, w, c, sizes):
        return local_split(
            Split(f, h, w, c, sizes), features, cotangent, conv_one, conv_two,
            gain_one, shift_one, gain_two, shift_two,
        )
    plan = Plan(f, h, w, c, sizes)
    norms = [v.reshape(1, c) for v in (gain_one, shift_one, gain_two, shift_two)]
    block_out, grad_input, part_one, part_two = block_kernel(
        plan, features, cotangent, conv_one.reshape(-1, c), conv_two.reshape(-1, c), *norms
    )
    return (
        block_out,
        grad_input,
        part_one.astype(F32).reshape(conv_one.shape),
        part_two.astype(F32).reshape(conv_two.shape),
    )


def solution(mesh):
    block = P("tm", "row", "col", None)
    return jax.shard_map(
        local,
        mesh=mesh,
        in_specs=(block, block) + (P(),) * 6,
        out_specs=(block, block, P(), P()),
        check_vma=False,
    )
```

```python
import functools

import jax
import jax.numpy as jnp
from jax import lax
from jax.experimental import pallas as pl
from jax.experimental.pallas import tpu as pltpu
from jax.sharding import PartitionSpec as P

GROUPS = 32
EPSILON = 1e-05
MESH = pl.DeviceIdType.MESH
F32 = jnp.float32
BF16 = jnp.bfloat16
AXES = ("tm", "row", "col")


class Plan:
    def __init__(self, f, h, w, c, sizes):
        self.f, self.h, self.w, self.c = f, h, w, c
        self.wp = 16
        while self.wp < w + 2:
            self.wp *= 2
        self.n = f * h * self.wp
        self.hp = h + 2
        self.np = (f + 2) * self.hp * self.wp
        self.cb = -(-(f * h) // 16) * 16
        self.rb = 2 * self.wp
        self.ntm, self.nrow, self.ncol = sizes
        self.na = self.nrow
        self.nb = self.ntm * self.ncol
        self.taps_rows = 27 * c
        unit = 16 * self.ntm * self.nrow * self.ncol
        units = -(-self.taps_rows // unit)
        first = -(-units // 2)
        self.sum_rows = units * unit
        self.parts = [(0, first * unit)]
        if units > first:
            self.parts.append((first * unit, (units - first) * unit))

    def stages(self, order):
        near = 2 if self.ncol % 2 == 0 else 1
        known = dict(
            near=("col", 1, near, True),
            col=("col", near, self.ncol // near, False),
            tm=("tm", 1, self.ntm, False),
            row=("row", 1, self.nrow, False),
        )
        return [known[name] for name in order if known[name][2] > 1]


class Link:
    def __init__(self, src, dst, sems, index, device, sends, receives):
        self.make = lambda: pltpu.make_async_remote_copy(
            src_ref=src,
            dst_ref=dst,
            send_sem=sems[0].at[index],
            recv_sem=sems[1].at[index],
            device_id=device,
            device_id_type=MESH,
        )
        self.sends, self.receives = sends, receives

    def start(self):
        if self.sends is None:
            self.make().start()
            return

        @pl.when(self.sends)
        def _():
            self.make().start()

    def wait_send(self):
        if self.sends is None:
            self.make().wait_send()
            return

        @pl.when(self.sends)
        def _():
            self.make().wait_send()

    def wait_recv(self):
        if self.receives is None:
            self.make().wait_recv()
            return

        @pl.when(self.receives)
        def _():
            self.make().wait_recv()


class Place:
    def __init__(self, plan):
        self.t, self.r, self.c = (lax.axis_index(a) for a in AXES)
        self.has = dict(
            left=self.c > 0,
            right=self.c < plan.ncol - 1,
            up=self.r > 0,
            down=self.r < plan.nrow - 1,
            past=self.t > 0,
            future=self.t < plan.ntm - 1,
        )
        self.dev = dict(
            left={"col": self.c - 1},
            right={"col": self.c + 1},
            up={"row": self.r - 1},
            down={"row": self.r + 1},
            past={"tm": self.t - 1},
            future={"tm": self.t + 1},
        )

    def partners(self, plan):
        rows = [{"row": lax.rem(self.r + d, plan.na)} for d in range(1, plan.na)]
        index = self.t * plan.ncol + self.c
        others = []
        for d in range(1, plan.nb):
            to = lax.rem(index + d, plan.nb)
            others.append({"tm": lax.div(to, plan.ncol), "col": lax.rem(to, plan.ncol)})
        return rows, others


class Reduce:
    def __init__(self, plan, place, refs, sems, base):
        self.own, self.slots_a, self.mid, self.slots_b = refs
        rows, others = place.partners(plan)
        self.a = [
            Link(self.own, self.slots_a.at[d], sems, base + d, dev, None, None)
            for d, dev in enumerate(rows)
        ]
        self.b = [
            Link(self.mid, self.slots_b.at[d], sems, base + len(rows) + d, dev, None, None)
            for d, dev in enumerate(others)
        ]

    def start(self, first, second):
        self.own[...] = jnp.zeros_like(self.own)
        self.own[0:1] = first
        self.own[1:2] = second
        for link in self.a:
            link.start()

    def middle(self):
        for link in self.a:
            link.wait_recv()
        total = self.own[...]
        for d in range(len(self.a)):
            total = total + self.slots_a[d]
        self.mid[...] = total
        for link in self.b:
            link.start()

    def finish(self):
        for link in self.b:
            link.wait_recv()
        total = self.mid[...]
        for d in range(len(self.b)):
            total = total + self.slots_b[d]
        return total

    def drain(self):
        for link in self.a + self.b:
            link.wait_send()


class KernelSum:
    def __init__(self, plan, place, stages, span, acc, done, outs, ins, sems, base):
        self.acc, self.done, self.outs, self.ins = acc, done, outs, ins
        self.stages = stages
        at, count = span
        self.spans, self.reduce, self.gather = [], [], []
        for k, (axis, stride, ways, wide) in enumerate(stages):
            here = dict(tm=place.t, row=place.r, col=place.c)[axis]
            mine = lax.rem(lax.div(here, stride), ways)
            piece = count // ways
            aligned = lambda v: pl.multiple_of(v, 16)
            kept = aligned(at + mine * piece)
            links, sources = [], []
            for d in range(1, ways):
                other = lax.rem(mine + d, ways)
                dev = {axis: here + (other - mine) * stride}
                sent = aligned(at + other * piece)
                if wide:
                    src = acc.at[pl.ds(sent, piece)]
                else:
                    src = outs[k].at[d - 1]
                    sources.append((d - 1, sent))
                links.append((Link(src, ins[k].at[d - 1], sems, base, dev, None, None), dev))
                base += 1
            self.reduce.append([link for link, _ in links])
            gathers = []
            for _, dev in links:
                part = done.at[pl.ds(kept, piece)]
                gathers.append(Link(part, part, sems, base, dev, None, None))
                base += 1
            self.gather.append(gathers)
            self.spans.append((kept, piece, sources))
            at, count = kept, piece
        self.base = base

    def steps(self):
        out = []
        last = len(self.stages) - 1
        for k in range(len(self.stages)):
            out.append(functools.partial(self.reduce_step, k))
        for k in range(last, -1, -1):
            out.append(functools.partial(self.gather_step, k))
        out.append(self.last_step)
        return out

    def reduce_step(self, k):
        if k:
            self.settle(k - 1)
        kept, piece, sources = self.spans[k]
        for slot, sent in sources:
            self.outs[k][slot] = self.acc[pl.ds(sent, piece)].astype(BF16)
        for link in self.reduce[k]:
            link.start()

    def settle(self, k):
        kept, piece, _ = self.spans[k]
        for link in self.reduce[k]:
            link.wait_recv()
        total = self.acc[pl.ds(kept, piece)]
        for d in range(len(self.reduce[k])):
            total = total + self.ins[k][d].astype(F32)
        if k == len(self.stages) - 1:
            self.done[pl.ds(kept, piece)] = total.astype(BF16)
        else:
            self.acc[pl.ds(kept, piece)] = total

    def gather_step(self, k):
        if k == len(self.stages) - 1:
            self.settle(k)
        else:
            for link in self.gather[k + 1]:
                link.wait_recv()
        for link in self.gather[k]:
            link.start()

    def last_step(self):
        for link in self.gather[0]:
            link.wait_recv()

    def drain(self):
        for links in self.reduce + self.gather:
            for link in links:
                link.wait_send()


ORDERS = (("near", "col", "tm", "row"), ("near", "tm", "col", "row"))


def sum_scratch(plan):
    shapes, counts = [], []
    for order, (_, count) in zip(ORDERS, plan.parts):
        outs, ins = [], []
        for axis, stride, ways, wide in plan.stages(order):
            piece = count // ways
            shape = (ways - 1, piece, plan.c)
            outs.append(pltpu.VMEM((1, 16, plan.c) if wide else shape, BF16))
            ins.append(pltpu.VMEM(shape, F32 if wide else BF16))
            count = piece
        counts.append(len(outs))
        shapes += outs + ins
    return shapes, counts


def sum_sems(plan):
    return 2 * sum(
        stage[2] - 1 for order, _ in zip(ORDERS, plan.parts) for stage in plan.stages(order)
    )


EX_SEMS = 10


class Exchange:
    def __init__(self, plan, place, refs, sems, base, directions):
        self.plan, self.place, self.directions = plan, place, directions
        self.own, self.cols_out, self.cols_in, self.rows_out, self.rows_in = refs[:5]
        has, dev = place.has, place.dev
        cb, half = plan.cb, plan.f * plan.wp
        self.cols = [
            Link(self.cols_out.at[pl.ds(0, cb)], self.cols_in.at[pl.ds(0, cb)], sems, base,
                 dev["left"], has["left"], has["right"]),
            Link(self.cols_out.at[pl.ds(cb, cb)], self.cols_in.at[pl.ds(cb, cb)], sems, base + 1,
                 dev["right"], has["right"], has["left"]),
        ]
        self.rows = [
            Link(self.rows_out.at[pl.ds(0, half)], self.rows_in.at[pl.ds(half, half)], sems,
                 base + 2, dev["up"], has["up"], has["down"]),
            Link(self.rows_out.at[pl.ds(half, half)], self.rows_in.at[pl.ds(0, half)], sems,
                 base + 3, dev["down"], has["down"], has["up"]),
        ]
        self.tm = {}
        for k, source in enumerate(directions):
            block, cols, rows = refs[5 + 3 * k : 8 + 3 * k]
            target = "future" if source == "past" else "past"
            links = [
                Link(src, dst, sems, base + 4 + 3 * k + j, dev[target], has[target], has[source])
                for j, (src, dst) in enumerate(
                    [(self.own, block), (self.cols_in, cols), (self.rows_in, rows)]
                )
            ]
            self.tm[source] = ((block, cols, rows), links)

    def clear(self):
        cb, half = self.plan.cb, self.plan.f * self.plan.wp
        has = self.place.has

        def zero(ref, part, cond):
            @pl.when(jnp.logical_not(cond))
            def _():
                ref[part] = jnp.zeros(ref.at[part].shape, ref.dtype)

        zero(self.cols_in, pl.ds(0, cb), has["right"])
        zero(self.cols_in, pl.ds(cb, cb), has["left"])
        zero(self.rows_in, pl.ds(0, half), has["up"])
        zero(self.rows_in, pl.ds(half, half), has["down"])
        for source, (refs, _) in self.tm.items():
            for ref in refs:
                zero(ref, pl.ds(0, ref.shape[0]), has[source])

    def start(self, wide, pick):
        self.own[...] = wide[...].astype(BF16)
        for source in self.directions:
            self.tm[source][1][0].start()
        self.cols_out[...] = jnp.dot(pick[...], self.own[...], preferred_element_type=F32).astype(BF16)
        for link in self.cols:
            link.start()

    def middle(self, wide, spread):
        plan = self.plan
        for link in self.cols:
            link.wait_recv()
        for source in self.directions:
            self.tm[source][1][1].start()
        ends = spread_cols(self.cols_in, spread)
        size = plan.h * plan.wp
        for f in range(plan.f):
            for k, at in enumerate((f * size, (f + 1) * size - plan.wp)):
                self.rows_out[pl.ds((k * plan.f + f) * plan.wp, plan.wp)] = (
                    wide[pl.ds(at, plan.wp)] + ends[at : at + plan.wp]
                ).astype(BF16)
        for link in self.rows:
            link.start()

    def later(self):
        for link in self.rows:
            link.wait_recv()
        for source in self.directions:
            self.tm[source][1][2].start()

    def finish(self):
        for source in self.directions:
            for link in self.tm[source][1]:
                link.wait_recv()

    def drain(self):
        for link in self.cols + self.rows:
            link.wait_send()
        for source in self.directions:
            for link in self.tm[source][1]:
                link.wait_send()

    def pieces(self, wide, spread, source):
        plan = self.plan
        size = plan.h * plan.wp
        (block, cols, rows), _ = self.tm[source]

        def of(value, border, side):
            out = []
            for f in range(plan.f):
                top = border[pl.ds(f * plan.wp, plan.wp)].astype(F32)
                low = border[pl.ds((plan.f + f) * plan.wp, plan.wp)].astype(F32)
                out.append((side, top, value[f * size : (f + 1) * size], low))
            return out

        inner = of(wide[...] + spread_cols(self.cols_in, spread), self.rows_in, None)
        outer = of(block[...].astype(F32) + spread_cols(cols, spread), rows, source)
        if source == "past":
            return outer[plan.f - 2 :] + inner
        return inner + outer[:2]


def spread_cols(cols, spread):
    return jnp.dot(spread[...], cols[...], preferred_element_type=F32)


def silu(v):
    return v / (1.0 + jnp.exp(-v))


def slope(v):
    sigm = 1.0 / (1.0 + jnp.exp(-v))
    return sigm * (1.0 + v * (1.0 - sigm))


def valid(plan, place, count, side, border):
    has = place.has
    w = lax.broadcasted_iota(jnp.int32, (count, plan.c), 0) & (plan.wp - 1)
    one = lambda cond: cond.astype(jnp.int32)
    mask = jnp.where(
        w < plan.w,
        1,
        jnp.where(
            w == plan.w,
            one(has["right"]),
            jnp.where(w == plan.wp - 1, one(has["left"]), 0),
        ),
    )
    for name in (side, border):
        if name is not None:
            mask = mask * one(has[name])
    return mask > 0


def store_shifted(plan, ref, at, value):
    count = value.shape[0]
    rows = value.reshape(count // plan.wp, plan.wp, plan.c)
    before = pltpu.roll(rows, 1, axis=1).reshape(value.shape)
    after = pltpu.roll(rows, plan.wp - 1, axis=1).reshape(value.shape)
    c = plan.c
    ref[pl.ds(at, count), 0:c] = before.astype(BF16)
    ref[pl.ds(at, count), c : 2 * c] = value.astype(BF16)
    ref[pl.ds(at, count), 2 * c : 3 * c] = after.astype(BF16)


def build(plan, ref, frames):
    for k, (top, rows, low) in enumerate(frames):
        at = k * plan.hp * plan.wp
        store_shifted(plan, ref, at, top)
        store_shifted(plan, ref, at + plan.wp, rows)
        store_shifted(plan, ref, at + (plan.h + 1) * plan.wp, low)


def convolve(plan, ref, kernel, out):
    size = plan.h * plan.wp

    def frame(f, carry):
        pieces = []
        for p in range(3):
            for q in range(3):
                at = pl.multiple_of(((f + p) * plan.hp + q) * plan.wp, plan.wp)
                pieces.append(ref[pl.ds(at, size), :])
        wide = jnp.dot(jnp.concatenate(pieces, axis=1), kernel[...], preferred_element_type=F32)
        w = lax.broadcasted_iota(jnp.int32, wide.shape, 0) & (plan.wp - 1)
        out[pl.ds(pl.multiple_of(f * size, size), size), :] = jnp.where(w < plan.w, wide, 0.0)
        return carry

    lax.fori_loop(0, plan.f, frame, 0)


def kernel_term(plan, ref, turned, part, low, high):
    size = plan.h * plan.wp

    def tap(pq, carry):
        p, q = lax.div(pq, 3), lax.rem(pq, 3)
        pieces = []
        for f in range(plan.f):
            at = pl.multiple_of(((f + p) * plan.hp + q) * plan.wp, plan.wp)
            pieces.append(ref[pl.ds(at, size), :])
        term = jnp.dot(turned, jnp.concatenate(pieces, axis=0), preferred_element_type=F32)
        part[pl.ds(pl.multiple_of(pq * 3 * plan.c, 3 * plan.c), 3 * plan.c), :] = term.T
        return carry

    lax.fori_loop(low, high, tap, 0)


def turn_kernel(plan, kernel, out):
    taps, c = 27, plan.c

    def tap(k, carry):
        source = kernel[pl.ds(pl.multiple_of((taps - 1 - k) * c, c), c), :]
        out[pl.ds(pl.multiple_of(k * c, c), c), :] = source.astype(F32).T.astype(BF16)
        return carry

    lax.fori_loop(0, taps, tap, 0)


def spaced(plan, ref, wide):
    wide[...] = jnp.zeros_like(wide)
    for f in range(plan.f):
        for y in range(plan.h):
            wide[pl.ds((f * plan.h + y) * plan.wp, plan.w)] = ref[f, y].astype(F32)


def unspaced(plan, value, ref):
    for f in range(plan.f):
        for y in range(plan.h):
            at = (f * plan.h + y) * plan.wp
            ref[f, y] = value[at : at + plan.w].astype(BF16)


def column_sum(value):
    return jnp.sum(value, axis=0, keepdims=True)


def body(plan, n_ex, *refs):
    refs = list(refs)
    take = lambda k: [refs.pop(0) for _ in range(k)]
    features, cotangent, kernel_one, kernel_two, *norms = take(8)
    block_out, grad_input, part_one, part_two = take(4)
    wide_x, wide_g, wide_h, wide_l, wide_b = take(5)
    pick, spread, turned_one, turned_two = take(4)
    x3_one, x3_two, x3_g, x3_h = take(4)
    exchange_refs = [take(k) for k in n_ex]
    reduce_refs = [take(4) for _ in range(4)]
    acc_one, acc_two, done_one, done_two = take(4)
    sum_refs = []
    for _ in range(2):
        for count in sum_scratch(plan)[1]:
            sum_refs.append((take(count), take(count)))
    sems = take(2)

    place = Place(plan)
    rows, others = place.partners(plan)
    per_reduce = len(rows) + len(others)
    exchanges = [
        Exchange(plan, place, r, sems, EX_SEMS * k, d)
        for k, (r, d) in enumerate(
            zip(exchange_refs, (("past",), ("future",), ("past", "future"), ("future",)))
        )
    ]
    ex_x, ex_g, ex_h, ex_l = exchanges
    reduces = [
        Reduce(plan, place, r, sems, EX_SEMS * 4 + per_reduce * k)
        for k, r in enumerate(reduce_refs)
    ]
    sums = []
    base = EX_SEMS * 4 + per_reduce * 4
    for acc, done in ((acc_two, done_two), (acc_one, done_one)):
        for order, span in zip(ORDERS, plan.parts):
            outs, ins = sum_refs[len(sums)]
            sums.append(
                KernelSum(plan, place, plan.stages(order), span, acc, done, outs, ins, sems, base)
            )
            base = sums[-1].base
        acc[pl.ds(plan.taps_rows, plan.sum_rows - plan.taps_rows)] = jnp.zeros(
            (plan.sum_rows - plan.taps_rows, plan.c), F32
        )
    sums_two, sums_one = sums[: len(plan.parts)], sums[len(plan.parts) :]
    steps_two = [list(group) for group in zip(*[item.steps() for item in sums_two])]

    def advance():
        if steps_two:
            for step in steps_two.pop(0):
                step()

    for ex in exchanges:
        ex.clear()

    barrier = pltpu.get_barrier_semaphore()
    for dev in rows + others:
        pl.semaphore_signal(barrier, inc=1, device_id=dev, device_id_type=MESH)

    c = plan.c
    per_group = c // GROUPS
    members = float(plan.f * plan.h * plan.w * plan.ntm * plan.nrow * plan.ncol * per_group)
    lane_i = lax.broadcasted_iota(jnp.int32, (c, c), 0)
    lane_j = lax.broadcasted_iota(jnp.int32, (c, c), 1)
    same = (lax.div(lane_i, per_group) == lax.div(lane_j, per_group)).astype(F32)

    def group_means(total):
        sums = jnp.dot(
            total, same, preferred_element_type=F32, precision=lax.Precision.HIGHEST
        )
        return sums[0:1] / members, sums[1:2] / members

    def moments(total):
        average, square = group_means(total)
        return average, lax.rsqrt(square - average * average + EPSILON)

    spaced(plan, features, wide_x)
    j = lax.broadcasted_iota(jnp.int32, (2 * plan.cb, plan.n), 0)
    at = lax.broadcasted_iota(jnp.int32, (2 * plan.cb, plan.n), 1)
    first = j < plan.cb
    pick[...] = (
        at == jnp.where(first, j * plan.wp, (j - plan.cb) * plan.wp + plan.w - 1)
    ).astype(F32).astype(BF16)
    at = lax.broadcasted_iota(jnp.int32, (plan.n, 2 * plan.cb), 0)
    j = lax.broadcasted_iota(jnp.int32, (plan.n, 2 * plan.cb), 1)
    first = j < plan.cb
    spread[...] = (
        at == jnp.where(first, j * plan.wp + plan.w, (j - plan.cb) * plan.wp + plan.wp - 1)
    ).astype(F32).astype(BF16)

    pl.semaphore_wait(barrier, per_reduce)
    gain_one, shift_one, gain_two, shift_two = (ref[...] for ref in norms)

    x = wide_x[...]
    reduces[0].start(column_sum(x), column_sum(x * x))
    ex_x.start(wide_x, pick)
    spaced(plan, cotangent, wide_g)
    ex_g.start(wide_g, pick)
    reduces[0].middle()
    ex_x.middle(wide_x, spread)
    ex_g.middle(wide_g, spread)
    turn_kernel(plan, kernel_two, turned_two)
    ex_x.later()
    ex_g.later()
    turn_kernel(plan, kernel_one, turned_one)
    mean_one, scale_one = moments(reduces[0].finish())
    ex_x.finish()

    def unit_one(v):
        return (v - mean_one) * scale_one

    def frames_of(pieces, fn):
        out = []
        for side, top, rows_, low in pieces:
            keep = lambda v, border: jnp.where(
                valid(plan, place, v.shape[0], side, border), fn(v), 0.0
            )
            out.append((keep(top, "up"), keep(rows_, None), keep(low, "down")))
        return out

    build(
        plan,
        x3_one,
        frames_of(
            ex_x.pieces(wide_x, spread, "past"),
            lambda v: silu(unit_one(v) * gain_one + shift_one),
        ),
    )
    convolve(plan, x3_one, kernel_one, wide_h)
    hidden = wide_h[...]
    reduces[1].start(column_sum(hidden), column_sum(hidden * hidden))
    ex_h.start(wide_h, pick)
    reduces[1].middle()
    ex_h.middle(wide_h, spread)
    ex_g.finish()
    build(plan, x3_g, [p[1:] for p in ex_g.pieces(wide_g, spread, "future")])
    ex_h.later()
    convolve(plan, x3_g, turned_two, wide_b)
    mean_two, scale_two = moments(reduces[1].finish())

    def unit_two(v):
        return (v - mean_two) * scale_two

    unit = unit_two(wide_h[...])
    lifted = wide_b[...] * slope(unit * gain_two + shift_two) * gain_two
    wide_l[...] = lifted
    reduces[2].start(column_sum(lifted), column_sum(lifted * unit))
    ex_l.start(wide_l, pick)
    reduces[2].middle()
    ex_l.middle(wide_l, spread)
    ex_h.finish()
    build(
        plan,
        x3_two,
        frames_of(
            ex_h.pieces(wide_h, spread, "past"),
            lambda v: silu(unit_two(v) * gain_two + shift_two),
        ),
    )
    ex_l.later()
    kernel_term(plan, x3_two, wide_g[...].T.astype(BF16), acc_two, 0, 9)
    a_two, b_two = group_means(reduces[2].finish())
    advance()
    ex_l.finish()
    frames = []
    for (side, *lifts), (_, *hids) in zip(
        ex_l.pieces(wide_l, spread, "future"), ex_h.pieces(wide_h, spread, "future")
    ):
        out = []
        for border, lift, hid in zip(("up", None, "down"), lifts, hids):
            value = scale_two * (lift - a_two - unit_two(hid) * b_two)
            out.append(jnp.where(valid(plan, place, lift.shape[0], side, border), value, 0.0))
        frames.append(tuple(out))
    build(plan, x3_h, frames)
    advance()
    w = lax.broadcasted_iota(jnp.int32, (plan.h * plan.wp, c), 0) & (plan.wp - 1)
    own = jnp.concatenate(
        [jnp.where(w < plan.w, frames[f][1], 0.0) for f in range(plan.f)], axis=0
    )
    turned = own.T.astype(BF16)
    ready = min(9, -(-plan.parts[0][1] // (3 * c)))
    kernel_term(plan, x3_one, turned, acc_one, 0, ready)
    steps_one = [item.steps() for item in sums_one]
    steps_one[0].pop(0)()
    advance()
    kernel_term(plan, x3_one, turned, acc_one, ready, 9)
    for steps in steps_one[1:]:
        steps.pop(0)()

    def advance_one():
        for steps in steps_one:
            steps.pop(0)()

    convolve(plan, x3_h, turned_one, wide_b)
    unit = unit_one(wide_x[...])
    lifted = wide_b[...] * slope(unit * gain_one + shift_one) * gain_one
    reduces[3].start(column_sum(lifted), column_sum(lifted * unit))
    wide_l[...] = lifted
    advance_one()
    advance()
    reduces[3].middle()
    convolve(plan, x3_two, kernel_two, wide_b)
    advance_one()
    advance()
    unspaced(plan, wide_x[...] + wide_b[...], block_out)
    a_one, b_one = group_means(reduces[3].finish())
    advance_one()
    advance()
    unit = unit_one(wide_x[...])
    unspaced(
        plan,
        wide_g[...] + scale_one * (wide_l[...] - a_one - unit * b_one),
        grad_input,
    )
    while steps_one[0]:
        advance_one()
        advance()
    part_two[...] = done_two[pl.ds(0, plan.taps_rows)]
    part_one[...] = done_one[pl.ds(0, plan.taps_rows)]
    for item in exchanges + reduces + sums:
        item.drain()


def block_kernel(plan, features, cotangent, kernel_one, kernel_two, *norms):
    c, n = plan.c, plan.n
    half = plan.f * plan.wp
    exchange = []
    n_ex = []
    for count in (1, 1, 2, 1):
        shapes = [(n, c), (2 * plan.cb, c), (2 * plan.cb, c), (2 * half, c), (2 * half, c)]
        shapes += [(n, c), (2 * plan.cb, c), (2 * half, c)] * count
        n_ex.append(len(shapes))
        exchange += [pltpu.VMEM(s, BF16) for s in shapes]
    reduce = [
        pltpu.VMEM((8, c), F32),
        pltpu.VMEM((max(1, plan.na - 1), 8, c), F32),
        pltpu.VMEM((8, c), F32),
        pltpu.VMEM((max(1, plan.nb - 1), 8, c), F32),
    ] * 4
    sems = 4 * EX_SEMS + 4 * (plan.na + plan.nb - 2) + 2 * sum_sems(plan)
    vmem = pl.BlockSpec(memory_space=pltpu.VMEM)
    taps = kernel_one.shape[0]
    return pl.pallas_call(
        functools.partial(body, plan, n_ex),
        out_shape=(
            jax.ShapeDtypeStruct(features.shape, BF16),
            jax.ShapeDtypeStruct(features.shape, BF16),
            jax.ShapeDtypeStruct((taps, c), BF16),
            jax.ShapeDtypeStruct((taps, c), BF16),
        ),
        in_specs=[vmem] * 8,
        out_specs=(vmem,) * 4,
        scratch_shapes=[pltpu.VMEM((n, c), F32)] * 5
        + [pltpu.VMEM((2 * plan.cb, n), BF16), pltpu.VMEM((n, 2 * plan.cb), BF16)]
        + [pltpu.VMEM((taps, c), BF16)] * 2
        + [pltpu.VMEM((plan.np, 3 * c), BF16)] * 4
        + exchange
        + reduce
        + [pltpu.VMEM((plan.sum_rows, c), F32)] * 2
        + [pltpu.VMEM((plan.sum_rows, c), BF16)] * 2
        + sum_scratch(plan)[0] * 2
        + [pltpu.SemaphoreType.DMA((sems,))] * 2,
        compiler_params=pltpu.CompilerParams(
            collective_id=0, has_side_effects=True, vmem_limit_bytes=52 * 2**20
        ),
    )(features, cotangent, kernel_one, kernel_two, *norms)


SLOT = 16
MANY = 256
SHARES = (((3, True), (2, True), (2, True)), ((2, False), (3, True), (2, True)))
VMEM_ASK = 60 * 2**20


class Split:
    def __init__(self, f, h, w, c, sizes):
        self.f, self.h, self.w, self.c = f, h, w, c
        self.ntm, self.nrow, self.ncol = sizes
        self.frames = f * self.ntm
        self.half = w // 2
        self.fn = h * SLOT
        self.pn = (h + 2) * SLOT
        self.n = self.frames * self.fn
        self.hs = -(-h // 16) * 16
        self.ext = self.frames * self.hs
        self.wide = 2 * SLOT
        self.gn = -(-self.fn // 128) * 128
        self.taps_rows = 27 * c
        self.nxy = self.ntm * (self.ncol // 2)
        unit = 32 * self.nxy * self.nrow
        units = -(-self.taps_rows // unit)
        self.sum_rows = units * unit
        self.parts = [self.cut(units, unit, shares) for shares in SHARES]
        self.cells = h * w
        self.cells_up = -(-self.cells // 8) * 8

    @staticmethod
    def cut(units, unit, shares):
        whole = sum(share for share, _ in shares)
        parts, at, taken = [], 0, 0
        for share, plane_first in shares:
            taken += share
            end = units * taken // whole
            if end > at:
                parts.append((at * unit, (end - at) * unit, plane_first))
            at = end
        return parts

    @staticmethod
    def fits(f, h, w, c, sizes):
        ntm, nrow, ncol = sizes
        return (
            ntm == 2
            and ncol % 2 == 0
            and w % 2 == 0
            and SLOT < w <= 2 * SLOT
            and w // 2 + 2 <= SLOT
            and w - SLOT <= w // 2 - 1
            and h <= 16
            and f * ntm * 16 <= 64
            and f * ntm >= 3
        )


class Spot:
    def __init__(self, plan):
        self.t, self.r, self.c = (lax.axis_index(a) for a in AXES)
        self.k = 2 * self.c + self.t
        self.left = self.k > 0
        self.right = self.k < 2 * plan.ncol - 1
        self.up = self.r > 0
        self.down = self.r < plan.nrow - 1
        self.core = lax.rem(self.c, 2)
        self.y = lax.div(self.c, 2)

    def peers(self, plan):
        offsets = [
            (dt, dr, dc)
            for dt in range(plan.ntm)
            for dr in range(plan.nrow)
            for dc in range(plan.ncol)
            if (dt, dr, dc) != (0, 0, 0)
        ]
        offsets.sort(key=lambda o: -(o[0] + min(1, o[2]) + 2 * (o[1] == plan.nrow // 2) + (o[1] > 0)))
        out = []
        for dt, dr, dc in offsets:
            out.append(
                {
                    "tm": lax.rem(self.t + dt, plan.ntm),
                    "row": lax.rem(self.r + dr, plan.nrow),
                    "col": lax.rem(self.c + dc, plan.ncol),
                }
            )
        return out

    def plane(self, plan):
        me = self.t * (plan.ncol // 2) + self.y
        out = []
        for d in range(1, plan.nxy):
            o = lax.rem(me + d, plan.nxy)
            dev = {
                "tm": lax.div(o, plan.ncol // 2),
                "col": 2 * lax.rem(o, plan.ncol // 2) + self.core,
            }
            out.append((o, dev))
        return me, out

    def line(self, plan):
        out = []
        for d in range(1, plan.nrow):
            o = lax.rem(self.r + d, plan.nrow)
            out.append((o, {"row": o}))
        return self.r, out


class Counter:
    def __init__(self):
        self.at = 0

    def take(self):
        self.at += 1
        return self.at - 1


class Total:
    def __init__(self, peers, own, slots, sems, counter):
        self.own, self.slots, self.peers, self.sems = own, slots, peers, sems
        self.index = counter.take()

    def start(self, first, second):
        self.own[0:1] = first
        self.own[1:2] = second
        for d, dev in enumerate(self.peers):
            pltpu.make_async_remote_copy(
                src_ref=self.own.at[pl.ds(0, 2)],
                dst_ref=self.slots.at[d, pl.ds(0, 2)],
                send_sem=self.sems[0].at[self.index],
                recv_sem=self.sems[1].at[self.index],
                device_id=dev,
                device_id_type=MESH,
            ).start()

    def whole(self, k):
        part = self.slots.at[pl.ds(0, len(self.peers)), pl.ds(0, 2)]
        return pltpu.make_async_copy(part, part, self.sems[k].at[self.index])

    def finish(self):
        self.whole(1).wait()
        total = self.own[0:2]
        for d in range(len(self.peers)):
            total = total + self.slots[d, 0:2]
        return total

    def drain(self):
        self.whole(0).wait()


class Halo:
    def __init__(self, plan, spot, refs, sems, counter):
        self.plan, self.spot = plan, spot
        self.block, self.edge, self.top, self.bot, self.ch = refs
        self.sems, self.counter = sems, counter
        self.links = []

    def link(self, src, dst, dev, sends, receives):
        item = Link(src, dst, self.sems, self.counter.take(), dev, sends, receives)
        self.links.append(item)
        return item

    def rows(self):
        s = self.spot
        return ((1, s.r + 1, s.down, s.up), (2, s.r - 1, s.up, s.down))

    def lines(self):
        s = self.spot
        return ((0, None, None, None),) + self.rows()

    def clear(self):
        for ref in (self.top, self.bot, self.ch):
            ref[...] = jnp.zeros(ref.shape, BF16)

    def wait(self):
        for link in self.links:
            link.wait_recv()

    def drain(self):
        for link in self.links:
            link.wait_send()


def both(*conds):
    out = None
    for cond in conds:
        if cond is not None:
            out = cond if out is None else jnp.logical_and(out, cond)
    return out


class Reshard(Halo):
    def __init__(self, plan, spot, pair, refs, sems, counter):
        super().__init__(plan, spot, refs, sems, counter)
        self.pair = pair
        t, r, c, f = spot.t, spot.r, spot.c, plan.f
        n = plan.ncol
        self.link(pair.at[1 - t], self.block.at[pl.ds(f * t, f)], {"tm": 1 - t}, None, None)
        for which, row, sends, receives in self.rows():
            src_at = plan.fn - SLOT if which == 1 else 0
            dst = (self.top if which == 1 else self.bot).at[pl.ds(f * t, f)]
            for d in range(2):
                to = t if d == 0 else 1 - t
                self.link(pair.at[to, :, pl.ds(src_at, SLOT)], dst, {"tm": to, "row": row}, sends, receives)
        rows = f * plan.hs
        for which, row, sends, receives in self.lines():
            for d in range(2):
                dev = {"tm": t - d, "col": c + 1}
                if row is not None:
                    dev["row"] = row
                self.link(
                    self.edge.at[1], self.ch.at[which, pl.ds(rows * d, rows)], dev,
                    both(t == d, c < n - 1, sends), both(t == 0, c > 0, receives),
                )
                dev = {"tm": t - d + 1, "col": c - 1}
                if row is not None:
                    dev["row"] = row
                self.link(
                    self.edge.at[0], self.ch.at[which, pl.ds(plan.ext + rows * d, rows)], dev,
                    both(t == d, c > 0, sends), both(t == 1, c < n - 1, receives),
                )

    def start(self, stage, rows, w32):
        plan, t = self.plan, self.spot.t
        step = 8 * plan.f
        for k in range(plan.cells_up // 8):
            rows[pl.ds(step * k, step)] = stage[pl.ds(8 * k, 8)].astype(F32).reshape(step, plan.c)
        for f in range(plan.f):
            for y in range(plan.h):
                w32[pl.ds((f * plan.h + y) * plan.wide, plan.w)] = rows[
                    pl.ds(y * plan.w * plan.f + f, plan.w, plan.f)
                ]
        slot = lax.broadcasted_iota(jnp.int32, (plan.h, SLOT, plan.c), 1)
        for f in range(plan.f):
            v = w32[pl.ds(f * plan.h * plan.wide, plan.h * plan.wide)]
            v = v.reshape(plan.h, plan.wide, plan.c)
            low, high = v[:, :SLOT], v[:, SLOT:]
            second = jnp.where(slot >= plan.half - 1, low, high)
            self.pair[0, f] = low.reshape(plan.fn, plan.c).astype(BF16)
            self.pair[1, f] = second.reshape(plan.fn, plan.c).astype(BF16)
            for side, x in ((0, 0), (1, plan.w - 1)):
                at = f * plan.h * plan.wide + x
                self.edge[side, pl.ds(f * plan.hs, plan.hs)] = w32[
                    pl.ds(at, plan.hs, plan.wide)
                ].astype(BF16)

    def send(self):
        self.links[0].start()

    def send_rest(self):
        for link in self.links[1:]:
            link.start()

    def keep(self):
        self.block[pl.ds(self.plan.f * self.spot.t, self.plan.f)] = self.pair[self.spot.t]


class Border(Halo):
    def __init__(self, plan, spot, refs, sems, counter):
        super().__init__(plan, spot, refs, sems, counter)
        t, c = spot.t, spot.c
        for which, row, sends, receives in self.rows():
            at = plan.fn - SLOT if which == 1 else 0
            dst = self.top if which == 1 else self.bot
            self.link(self.block.at[:, pl.ds(at, SLOT)], dst, {"row": row}, sends, receives)
        for which, row, sends, receives in self.lines():
            dev = {"tm": 1 - t, "col": c - 1 + t}
            if row is not None:
                dev["row"] = row
            self.link(
                self.edge.at[0], self.ch.at[which, pl.ds(plan.ext, plan.ext)], dev,
                both(spot.left, sends), both(spot.right, receives),
            )
            dev = {"tm": 1 - t, "col": c + t}
            if row is not None:
                dev["row"] = row
            self.link(
                self.edge.at[1], self.ch.at[which, pl.ds(0, plan.ext)], dev,
                both(spot.right, sends), both(spot.left, receives),
            )

    def start(self, wide):
        plan, t = self.plan, self.spot.t
        for f in range(plan.frames):
            self.block[f] = wide[pl.ds(f * plan.fn, plan.fn)].astype(BF16)
            for side, offset in ((0, 0), (1, plan.half - 1)):
                values = [
                    wide[pl.ds(f * plan.fn + (plan.half * k + offset) % SLOT, plan.hs, SLOT)]
                    for k in range(2)
                ]
                self.edge[side, pl.ds(f * plan.hs, plan.hs)] = jnp.where(
                    t == 0, values[0], values[1]
                ).astype(BF16)
        for link in self.links:
            link.start()


class Part:
    def __init__(self, plan, spot, span, acc, done, out, refs, sems, counter, local_sem):
        self.acc, self.done = acc, done
        self.core_in, out1, self.in1, out2, self.in2 = refs
        self.at, self.count, plane_first = span
        rows = pl.ds(self.at, min(self.count, plan.taps_rows - self.at))
        self.out = pltpu.make_async_copy(done.at[rows], out.at[rows], local_sem)
        link = lambda src, dst, dev: Link(src, dst, sems, counter.take(), dev, None, None)
        aligned = lambda v: pl.multiple_of(v, 16)
        half = self.count // 2
        base = aligned(self.at + spot.core * half)
        other = aligned(self.at + (1 - spot.core) * half)
        sibling = {"col": spot.c + 1 - 2 * spot.core}
        self.core = link(acc.at[pl.ds(other, half)], self.core_in, sibling)
        stages = (spot.plane(plan), spot.line(plan))
        if not plane_first:
            stages = stages[::-1]
        (one, ones), (two, twos) = stages
        self.big = big = half // (len(ones) + 1)
        self.small = small = big // (len(twos) + 1)
        self.own1_in = aligned(one * big)
        self.own1 = own1 = aligned(base + one * big)
        self.own2 = own2 = aligned(own1 + two * small)
        self.send1 = [
            (aligned(base + o * big), aligned(o * big), out1.at[d], link(out1.at[d], self.in1.at[d], dev))
            for d, (o, dev) in enumerate(ones)
        ]
        self.send2 = [
            (aligned(own1 + o * small), out2.at[d], link(out2.at[d], self.in2.at[d], dev))
            for d, (o, dev) in enumerate(twos)
        ]
        piece2 = done.at[pl.ds(own2, small)]
        self.gather2 = [link(piece2, piece2, dev) for _, dev in twos]
        piece1 = done.at[pl.ds(own1, big)]
        self.gather1 = [link(piece1, piece1, dev) for _, dev in ones]
        self.forward = [link(piece1, piece1, sibling)]
        for d in range(len(ones)):
            o, _ = ones[len(ones) - 1 - d]
            ref = done.at[pl.ds(aligned(base + o * big), big)]
            self.forward.append(link(ref, ref, sibling))

    def start(self):
        self.core.start()

    def first(self):
        self.core.wait_recv()
        for at, inside, out, link in self.send1:
            out[...] = (
                self.acc[pl.ds(at, self.big)] + self.core_in[pl.ds(inside, self.big)]
            ).astype(BF16)
            link.start()

    def second(self):
        big, own1 = self.big, self.own1
        total = self.acc[pl.ds(own1, big)] + self.core_in[pl.ds(self.own1_in, big)]
        for d, item in enumerate(self.send1):
            item[-1].wait_recv()
            total = total + self.in1[d].astype(F32)
        self.acc[pl.ds(own1, big)] = total
        for at, out, link in self.send2:
            out[...] = self.acc[pl.ds(at, self.small)].astype(BF16)
            link.start()

    def third(self):
        total = self.acc[pl.ds(self.own2, self.small)]
        for d, item in enumerate(self.send2):
            item[-1].wait_recv()
            total = total + self.in2[d].astype(F32)
        self.done[pl.ds(self.own2, self.small)] = total.astype(BF16)
        for link in self.gather2:
            link.start()

    def fourth(self):
        for link in self.gather2:
            link.wait_recv()
        for link in self.gather1:
            link.start()
        self.forward[0].start()

    def fifth(self):
        for d, link in enumerate(self.gather1):
            link.wait_recv()
            self.forward[1 + d].start()

    def sixth(self):
        for link in self.forward:
            link.wait_recv()
        self.out.start()

    def drain(self):
        self.core.wait_send()
        for item in self.send1 + self.send2:
            item[-1].wait_send()
        for link in self.gather2 + self.gather1 + self.forward:
            link.wait_send()
        self.out.wait()


def part_scratch(plan):
    shapes = []
    for _, count, plane_first in plan.parts[0] + plan.parts[1]:
        ways = (plan.nxy, plan.nrow) if plane_first else (plan.nrow, plan.nxy)
        big = count // 2 // ways[0]
        small = big // ways[1]
        shapes.append(pltpu.VMEM((count // 2, plan.c), F32))
        for rows, k in ((big, ways[0]), (big, ways[0]), (small, ways[1]), (small, ways[1])):
            shapes.append(pltpu.VMEM((max(1, k - 1), rows, plan.c), BF16))
    return shapes


def around(value, by):
    rows = value.reshape(value.shape[0] // SLOT, SLOT, value.shape[1])
    return pltpu.roll(rows, by, axis=1).reshape(value.shape)


def convolve_split(plan, padded, weight, out, keep, future):
    c = plan.c
    for t in range(plan.frames):
        pieces, used = [], []
        for p in range(3):
            source = t + p if future else t + p - 2
            if not 0 <= source < plan.frames:
                continue
            used.append(p)
            for q in range(3):
                pieces.append(padded[pl.ds(source * plan.pn + q * SLOT, plan.fn), :])
        lhs = jnp.concatenate(pieces, axis=1)
        rhs = weight[3 * used[0] : 3 * used[-1] + 3].reshape(3 * len(used) * c, 3 * c)
        wide = jnp.dot(lhs, rhs, preferred_element_type=F32)
        total = around(wide[:, 0:c], 1) + wide[:, c : 2 * c] + around(wide[:, 2 * c :], SLOT - 1)
        out[pl.ds(t * plan.fn, plan.fn), :] = keep(total)


def place_padded(plan, ref, value, top, bot):
    for t in range(plan.frames):
        at = t * plan.pn
        ref[pl.ds(at, SLOT), :] = top[t * SLOT : (t + 1) * SLOT].astype(BF16)
        ref[pl.ds(at + SLOT, plan.fn), :] = value[t * plan.fn : (t + 1) * plan.fn].astype(BF16)
        ref[pl.ds(at + SLOT + plan.fn, SLOT), :] = bot[t * SLOT : (t + 1) * SLOT].astype(BF16)


def shifted_grad(plan, ref, value):
    c = plan.c
    for s, moved in enumerate((around(value, SLOT - 1), value, around(value, 1))):
        for t in range(plan.frames):
            ref[pl.ds(t * plan.gn, plan.fn), s * c : (s + 1) * c] = moved[
                t * plan.fn : (t + 1) * plan.fn
            ].astype(BF16)


def turned_acted(plan, padded, ref):
    c = plan.c
    for q in range(3):
        for t in range(plan.frames):
            slab = padded[pl.ds(t * plan.pn + q * SLOT, plan.gn), :]
            ref[q * c : (q + 1) * c, t * plan.gn : (t + 1) * plan.gn] = slab.T


def kernel_grad(plan, turned, moved, acc, p):
    c = plan.c
    lag = 2 - p
    count = (plan.frames - lag) * plan.gn
    term = jnp.dot(
        turned[:, 0:count], moved[pl.ds(lag * plan.gn, count), :], preferred_element_type=F32
    )
    for q in range(3):
        for s in range(3):
            acc[pl.ds((9 * p + 3 * q + s) * c, c), :] = term[
                q * c : (q + 1) * c, s * c : (s + 1) * c
            ]


def turn_weight(plan, weight, out):
    c = plan.c
    for k in range(27):
        j = 26 - k
        source = weight[j // 3, :, (j % 3) * c : (j % 3 + 1) * c]
        out[k // 3, :, (k % 3) * c : (k % 3 + 1) * c] = source.T


def split_body(plan, *refs):
    refs = list(refs)
    take = lambda k: [refs.pop(0) for _ in range(k)]
    features, cotangent, conv_one, conv_two, *norms = take(8)
    block_out, grad_input, part_one, part_two = take(4)
    w32, rows32, stage_x, stage_g = take(4)
    done_one, done_two = take(2)
    wide_h, wide_l, wide_b, unit_h = take(4)
    spread_mid, spread_top, spread_bot = take(3)
    weight_one, weight_two, turned_one, turned_two = take(4)
    pad_one, pad_two, pad_g, pad_h = take(4)
    at_one, at_two, moved_g, moved_h = take(4)
    acc_one, acc_two = take(2)
    norm_in = take(4)
    pair_x, pair_g = take(2)
    halo_refs = [take(5) for _ in range(4)]
    total_refs = [take(2) for _ in range(4)]
    sum_refs = [[take(5) for _ in parts] for parts in plan.parts]
    out_refs = [take(2) for _ in range(2)]
    sems = take(2)
    (local_sem,) = take(1)

    spot = Spot(plan)
    peers = spot.peers(plan)
    counter = Counter()
    c = plan.c

    loads = []
    cells = pl.ds(0, plan.cells)
    for k, (src, dst) in enumerate(
        [(features, stage_x.at[cells]), (cotangent, stage_g.at[cells])]
        + list(zip(norms, norm_in))
        + [(conv_one.at[:, s], weight_one.at[:, :, pl.ds(s * c, c)]) for s in range(3)]
        + [(conv_two.at[:, s], weight_two.at[:, :, pl.ds(s * c, c)]) for s in range(3)]
    ):
        loads.append(pltpu.make_async_copy(src, dst, local_sem.at[k]))
    for copy in loads[:2]:
        copy.start()

    ex_x = Reshard(plan, spot, pair_x, halo_refs[0], sems, counter)
    ex_g = Reshard(plan, spot, pair_g, halo_refs[1], sems, counter)
    ex_h = Border(plan, spot, halo_refs[2], sems, counter)
    ex_l = Border(plan, spot, halo_refs[3], sems, counter)
    totals = [Total(peers, *r, sems, counter) for r in total_refs]
    sums_two, sums_one = (
        [
            Part(plan, spot, span, acc, done, out, r, sems, counter, local_sem.at[first + k])
            for k, (span, r) in enumerate(zip(parts, group))
        ]
        for acc, done, out, parts, group, first in (
            (acc_two, done_two, part_two, plan.parts[0], sum_refs[0], 16),
            (acc_one, done_one, part_one, plan.parts[1], sum_refs[1], 16 + len(plan.parts[0])),
        )
    )
    outs = []
    for (mine, theirs) in out_refs:
        outs.append(
            Link(
                mine.at[pl.ds(plan.f * (1 - spot.t), plan.f)], theirs, sems, counter.take(),
                {"tm": 1 - spot.t}, None, None,
            )
        )
    assert counter.at <= MANY

    for ex in (ex_x, ex_g, ex_h, ex_l):
        ex.clear()
    barrier = pltpu.get_barrier_semaphore()
    for dev in peers:
        pl.semaphore_signal(barrier, inc=1, device_id=dev, device_id_type=MESH)
    for copy in loads[2:]:
        copy.start()

    per_group = c // GROUPS
    members = float(plan.n // SLOT * plan.half * 2 * plan.nrow * plan.ncol * per_group)
    lane_i = lax.broadcasted_iota(jnp.int32, (c, c), 0)
    lane_j = lax.broadcasted_iota(jnp.int32, (c, c), 1)
    same = (lax.div(lane_i, per_group) == lax.div(lane_j, per_group)).astype(F32)

    def group_means(total):
        sums = jnp.dot(total, same, preferred_element_type=F32, precision=lax.Precision.HIGHEST)
        return sums[0:1] / members, sums[1:2] / members

    def moments(total):
        average, square = group_means(total)
        return average, lax.rsqrt(square - average * average + EPSILON)

    w32[...] = jnp.zeros(w32.shape, F32)
    for stage in (stage_x, stage_g):
        spare = plan.cells_up - plan.cells
        if spare:
            stage[pl.ds(plan.cells, spare)] = jnp.zeros((spare, plan.f, c), BF16)
    loads[0].wait()
    ex_x.start(stage_x, rows32, w32)
    x = w32[...]
    first, second = column_sum(x), column_sum(x * x)
    pl.semaphore_wait(barrier, len(peers))
    ex_x.send()
    totals[0].start(first, second)
    ex_x.send_rest()
    loads[1].wait()
    ex_g.start(stage_g, rows32, w32)
    ex_g.send()
    ex_g.send_rest()
    ex_x.keep()
    ex_g.keep()

    rel = (lax.broadcasted_iota(jnp.int32, (SLOT, c), 0) - plan.half * spot.t) & (SLOT - 1)
    one = lambda cond: cond.astype(jnp.int32)
    inside = rel < plan.half
    inner = jnp.where(spot.t == 0, plan.half, SLOT - 1)
    kept = jnp.logical_or(inside, rel == inner)
    legal = jnp.where(
        inside, 1, jnp.where(rel == plan.half, one(spot.right), jnp.where(rel == SLOT - 1, one(spot.left), 0))
    )

    def masked(value, mask):
        rows = value.reshape(value.shape[0] // SLOT, SLOT, c)
        return jnp.where(mask[None], rows, 0.0).reshape(value.shape)

    interior = lambda value: masked(value, inside)

    def targets(rows, source):
        i = lax.broadcasted_iota(jnp.int32, (rows, 2 * plan.ext), 0)
        j = lax.broadcasted_iota(jnp.int32, (rows, 2 * plan.ext), 1)
        where = ((i & (SLOT - 1)) - plan.half * spot.t) & (SLOT - 1)
        code = source(i >> 4)
        aim = jnp.where(where == SLOT - 1, code, jnp.where(where == plan.half, code + plan.ext, -1))
        return (j == aim).astype(F32).astype(BF16)

    def of_group(g):
        t = 0
        for k in range(1, plan.frames):
            t = t + (g >= k * plan.h).astype(jnp.int32)
        return g + t * (plan.hs - plan.h)

    spread_mid[...] = targets(plan.n, of_group)
    spread_top[...] = targets(plan.frames * SLOT, lambda t: t * plan.hs + plan.h - 1)
    spread_bot[...] = targets(plan.frames * SLOT, lambda t: t * plan.hs)
    for ref in (pad_one, pad_two):
        ref[pl.ds(plan.frames * plan.pn, SLOT), :] = jnp.zeros((SLOT, c), BF16)
    if plan.gn > plan.fn:
        for ref in (moved_g, moved_h):
            for t in range(plan.frames):
                ref[pl.ds(t * plan.gn + plan.fn, plan.gn - plan.fn), :] = jnp.zeros(
                    (plan.gn - plan.fn, 3 * c), BF16
                )
    for ref in (wide_h, wide_l):
        ref[pl.ds(plan.n, SLOT), :] = jnp.zeros((SLOT, c), F32)
    for acc in (acc_one, acc_two):
        acc[pl.ds(plan.taps_rows, plan.sum_rows - plan.taps_rows)] = jnp.zeros(
            (plan.sum_rows - plan.taps_rows, c), F32
        )
    for copy in loads[2:]:
        copy.wait()
    gain_one, shift_one, gain_two, shift_two = (ref[...] for ref in norm_in)
    turn_weight(plan, weight_two, turned_two)

    def assemble(ex, value, mask):
        flat = lambda ref: ref[...].astype(F32).reshape(plan.frames * SLOT, c)
        spread = lambda by, k: jnp.dot(by[...], ex.ch[k], preferred_element_type=F32)
        return (
            masked(value, mask) + spread(spread_mid, 0),
            masked(flat(ex.top), mask) + spread(spread_top, 1),
            masked(flat(ex.bot), mask) + spread(spread_bot, 2),
        )

    def clip(values):
        value, top, bot = values
        return (
            masked(value, legal > 0),
            masked(top, legal * one(spot.up) > 0),
            masked(bot, legal * one(spot.down) > 0),
        )

    def flat_block(ex):
        return ex.block[...].astype(F32).reshape(plan.n, c)

    ex_x.wait()
    values_x = assemble(ex_x, flat_block(ex_x), kept)
    mean_one, scale_one = moments(totals[0].finish())

    def unit_one(v):
        return (v - mean_one) * scale_one

    place_padded(
        plan, pad_one, *clip([silu(unit_one(v) * gain_one + shift_one) for v in values_x])
    )
    convolve_split(plan, pad_one, weight_one, wide_h, interior, False)
    hidden = wide_h[pl.ds(0, plan.n)]
    totals[1].start(column_sum(hidden), column_sum(hidden * hidden))
    ex_h.start(wide_h)

    ex_g.wait()
    place_padded(plan, pad_g, *clip(assemble(ex_g, flat_block(ex_g), kept)))
    convolve_split(plan, pad_g, turned_two, wide_b, interior, True)
    shifted_grad(plan, moved_g, interior(flat_block(ex_g)))
    turned_acted(plan, pad_one, at_one)
    mean_two, scale_two = moments(totals[1].finish())

    def unit_two(v):
        return (v - mean_two) * scale_two

    unit = unit_two(wide_h[pl.ds(0, plan.n)])
    lifted = interior(wide_b[...] * slope(unit * gain_two + shift_two) * gain_two)
    wide_l[pl.ds(0, plan.n)] = lifted
    totals[2].start(column_sum(lifted), column_sum(lifted * unit))
    ex_l.start(wide_l)

    ex_h.wait()
    units = [unit_two(v) for v in assemble(ex_h, wide_h[pl.ds(0, plan.n)], inside)]
    at = 0
    for v in units:
        unit_h[pl.ds(at, v.shape[0])] = v
        at += v.shape[0]
    place_padded(plan, pad_two, *clip([silu(v * gain_two + shift_two) for v in units]))
    turned_acted(plan, pad_two, at_two)
    def starts(parts, p):
        ready = plan.taps_rows if p == 2 else (p + 1) * 9 * c
        before = p * 9 * c
        for part in parts:
            end = min(part.at + part.count, plan.taps_rows)
            if before < end <= ready:
                part.start()

    for p in range(3):
        kernel_grad(plan, at_two, moved_g, acc_two, p)
        starts(sums_two, p)
    turn_weight(plan, weight_one, turned_one)
    for part in sums_two:
        part.first()
    a_two, b_two = group_means(totals[2].finish())
    ex_l.wait()
    grads, at = [], 0
    for lift in assemble(ex_l, wide_l[pl.ds(0, plan.n)], inside):
        count = lift.shape[0]
        grads.append(scale_two * (lift - a_two - unit_h[pl.ds(at, count)] * b_two))
        at += count
    grads = clip(grads)
    shifted_grad(plan, moved_h, interior(grads[0]))
    for p in range(3):
        kernel_grad(plan, at_one, moved_h, acc_one, p)
        starts(sums_one, p)
    slot = lax.broadcasted_iota(jnp.int32, (plan.h, SLOT, c), 1)

    leave = [
        pltpu.make_async_copy(stage.at[cells], target, local_sem.at[14 + k])
        for k, (stage, target) in enumerate(((stage_x, block_out), (stage_g, grad_input)))
    ]

    def emit(k, stage):
        mine, theirs = out_refs[k]
        outs[k].wait_recv()
        for f in range(plan.f):
            a = mine[plan.f * spot.t + f].astype(F32).reshape(plan.h, SLOT, c)
            b = theirs[f].astype(F32).reshape(plan.h, SLOT, c)
            low = jnp.where(spot.t == 0, a, b)
            high = jnp.where(spot.t == 0, b, a)
            low = jnp.where(slot < plan.half, low, high)
            for y in range(plan.h):
                at = y * plan.w * plan.f + f
                rows32[pl.ds(at, SLOT, plan.f)] = low[y]
                rows32[pl.ds(at + SLOT * plan.f, plan.w - SLOT, plan.f)] = high[y, 0 : plan.w - SLOT]
        for at in range(0, plan.cells, 8):
            n = min(8, plan.cells - at)
            block = rows32[pl.ds(at * plan.f, n * plan.f)]
            stage[pl.ds(at, n)] = block.reshape(n, plan.f, c).astype(BF16)
        leave[k].start()

    def go(which, *steps):
        parts = dict(one=sums_one, two=sums_two)[which]
        for k, step in steps:
            if k < len(parts):
                getattr(parts[k], step)()

    go("one", (0, "first"))
    place_padded(plan, pad_h, *grads)
    convolve_split(plan, pad_h, turned_one, wide_b, interior, True)
    go("one", (1, "first"), (2, "first"))
    unit = unit_one(flat_block(ex_x))
    lifted = interior(wide_b[...] * slope(unit * gain_one + shift_one) * gain_one)
    wide_l[pl.ds(0, plan.n)] = lifted
    totals[3].start(column_sum(lifted), column_sum(lifted * unit))
    go("two", (1, "second"), (0, "second"), (2, "second"))
    convolve_split(plan, pad_two, weight_two, wide_b, interior, False)
    out_refs[0][0][...] = (flat_block(ex_x) + wide_b[...]).astype(BF16).reshape(
        plan.frames, plan.fn, c
    )
    outs[0].start()
    go("two", (0, "third"))
    go("one", (0, "second"), (1, "second"))
    go("two", (1, "third"))
    a_one, b_one = group_means(totals[3].finish())
    unit = unit_one(flat_block(ex_x))
    out_refs[1][0][...] = (
        flat_block(ex_g) + scale_one * (wide_l[pl.ds(0, plan.n)] - a_one - unit * b_one)
    ).astype(BF16).reshape(plan.frames, plan.fn, c)
    outs[1].start()
    go("one", (2, "second"))
    go("two", (2, "third"), (0, "fourth"))
    go("one", (0, "third"), (1, "third"))
    go("two", (1, "fourth"))
    go("one", (2, "third"))
    go("two", (2, "fourth"))
    emit(0, stage_x)
    go("one", (0, "fourth"))
    go("two", (0, "fifth"))
    emit(1, stage_g)
    go("one", (1, "fourth"), (2, "fourth"))
    go("two", (1, "fifth"), (2, "fifth"), (0, "sixth"), (1, "sixth"), (2, "sixth"))
    go("one", (0, "fifth"), (1, "fifth"), (2, "fifth"), (0, "sixth"), (1, "sixth"), (2, "sixth"))
    for item in [ex_x, ex_g, ex_h, ex_l] + totals + sums_two + sums_one:
        item.drain()
    for link in outs:
        link.wait_send()
    for copy in leave:
        copy.wait()


def split_kernel(plan, features, cotangent, kernel_one, kernel_two, *norms):
    c, n = plan.c, plan.n
    frames, fn = plan.frames, plan.fn
    vm = pltpu.VMEM
    halos = []
    for k in range(4):
        edge = plan.f * plan.hs if k < 2 else plan.ext
        halos += [
            vm((frames, fn, c), BF16),
            vm((2, edge, c), BF16),
            vm((frames, SLOT, c), BF16),
            vm((frames, SLOT, c), BF16),
            vm((3, 2 * plan.ext, c), BF16),
        ]
    count = plan.ntm * plan.nrow * plan.ncol - 1
    hbm = pl.BlockSpec(memory_space=pltpu.HBM)
    pads = plan.frames * plan.pn + SLOT
    return pl.pallas_call(
        functools.partial(split_body, plan),
        out_shape=(
            jax.ShapeDtypeStruct(features.shape, BF16),
            jax.ShapeDtypeStruct(features.shape, BF16),
            jax.ShapeDtypeStruct((plan.taps_rows, c), BF16),
            jax.ShapeDtypeStruct((plan.taps_rows, c), BF16),
        ),
        in_specs=[hbm] * 8,
        out_specs=(hbm,) * 4,
        scratch_shapes=[vm((plan.f * plan.h * plan.wide + 2 * plan.wide, c), F32)]
        + [vm((plan.cells_up * plan.f, c), F32)]
        + [vm((plan.cells_up, plan.f, c), BF16)] * 2
        + [vm((plan.sum_rows, c), BF16)] * 2
        + [vm((n + SLOT, c), F32)] * 2
        + [vm((n, c), F32)]
        + [vm((n + 2 * frames * SLOT, c), F32)]
        + [vm((n, 2 * plan.ext), BF16)]
        + [vm((frames * SLOT, 2 * plan.ext), BF16)] * 2
        + [vm((9, c, 3 * c), BF16)] * 4
        + [vm((pads, c), BF16)] * 4
        + [vm((3 * c, frames * plan.gn), BF16)] * 2
        + [vm((frames * plan.gn, 3 * c), BF16)] * 2
        + [vm((plan.sum_rows, c), F32)] * 2
        + [vm((1, c), F32)] * 4
        + [vm((2, plan.f, fn, c), BF16)] * 2
        + halos
        + [vm((8, c), F32), vm((count, 8, c), F32)] * 4
        + part_scratch(plan)
        + [vm((frames, fn, c), BF16), vm((plan.f, fn, c), BF16)] * 2
        + [pltpu.SemaphoreType.DMA((MANY,))] * 2
        + [pltpu.SemaphoreType.DMA((32,))],
        compiler_params=pltpu.CompilerParams(
            collective_id=0, has_side_effects=True, vmem_limit_bytes=VMEM_ASK
        ),
    )(features, cotangent, kernel_one, kernel_two, *norms)


def widen_body(parts, *refs):
    ins, outs, narrow, wide, held, sems = refs[:4], refs[4:8], *refs[8:]
    moves = [pltpu.make_async_copy(ins[k], held.at[k], sems.at[0, k]) for k in range(2)]
    leave = [pltpu.make_async_copy(held.at[k], outs[k], sems.at[0, 2 + k]) for k in range(2)]
    loads, stores = [], []
    for a in range(2):
        for j, (at, count) in enumerate(parts):
            rows = pl.ds(at, count)
            k = len(parts) * a + j
            loads.append(
                pltpu.make_async_copy(ins[2 + a].at[rows], narrow.at[a, rows], sems.at[1, k])
            )
            stores.append(
                pltpu.make_async_copy(wide.at[a, rows], outs[2 + a].at[rows], sems.at[2, k])
            )
    for copy in loads[: len(parts)] + moves + loads[len(parts) :]:
        copy.start()
    for a in range(2):
        for j, (at, count) in enumerate(parts):
            k = len(parts) * a + j
            loads[k].wait()
            wide[a, pl.ds(at, count)] = narrow[a, pl.ds(at, count)].astype(F32)
            stores[k].start()
        moves[a].wait()
        leave[a].start()
    for copy in stores + leave:
        copy.wait()


def widen(block_out, grad_input, part_one, part_two):
    rows, c = part_one.shape
    piece = -(-rows // 64) * 16
    parts = [(at, min(piece, rows - at)) for at in range(0, rows, piece)]
    hbm = pl.BlockSpec(memory_space=pltpu.HBM)
    shape = jax.ShapeDtypeStruct
    return pl.pallas_call(
        functools.partial(widen_body, parts),
        out_shape=(
            shape(block_out.shape, BF16),
            shape(grad_input.shape, BF16),
            shape((rows, c), F32),
            shape((rows, c), F32),
        ),
        in_specs=[hbm] * 4,
        out_specs=(hbm,) * 4,
        scratch_shapes=[
            pltpu.VMEM((2, rows, c), BF16),
            pltpu.VMEM((2, rows, c), F32),
            pltpu.VMEM((2,) + block_out.shape, BF16),
            pltpu.SemaphoreType.DMA((3, 2 * len(parts))),
        ],
        compiler_params=pltpu.CompilerParams(vmem_limit_bytes=VMEM_ASK),
    )(block_out, grad_input, part_one, part_two)


def local_split(plan, features, cotangent, conv_one, conv_two, *norms):
    c = plan.c
    norms = [v.reshape(1, c) for v in norms]
    shape = (9, 3, c, c)
    turn = lambda v: v.transpose(1, 2, 0, 3).reshape(plan.cells, plan.f, c)
    back = lambda v: v.reshape(plan.h, plan.w, plan.f, c).transpose(2, 0, 1, 3)
    block_out, grad_input, part_one, part_two = widen(
        *split_kernel(
            plan, turn(features), turn(cotangent), conv_one.reshape(shape), conv_two.reshape(shape), *norms
        )
    )
    return (
        back(block_out),
        back(grad_input),
        part_one.reshape(conv_one.shape),
        part_two.reshape(conv_two.shape),
    )


def local(features, cotangent, conv_one, conv_two, gain_one, shift_one, gain_two, shift_two):
    f, h, w, c = features.shape
    sizes = tuple(lax.axis_size(a) for a in AXES)
    if Split.fits(f, h, w, c, sizes):
        return local_split(
            Split(f, h, w, c, sizes), features, cotangent, conv_one, conv_two,
            gain_one, shift_one, gain_two, shift_two,
        )
    plan = Plan(f, h, w, c, sizes)
    norms = [v.reshape(1, c) for v in (gain_one, shift_one, gain_two, shift_two)]
    block_out, grad_input, part_one, part_two = block_kernel(
        plan, features, cotangent, conv_one.reshape(-1, c), conv_two.reshape(-1, c), *norms
    )
    return (
        block_out,
        grad_input,
        part_one.astype(F32).reshape(conv_one.shape),
        part_two.astype(F32).reshape(conv_two.shape),
    )


def solution(mesh):
    block = P("tm", "row", "col", None)
    return jax.shard_map(
        local,
        mesh=mesh,
        in_specs=(block, block) + (P(),) * 6,
        out_specs=(block, block, P(), P()),
        check_vma=False,
    )
```

```python
import functools

import jax
import jax.numpy as jnp
from jax import lax
from jax.experimental import pallas as pl
from jax.experimental.pallas import tpu as pltpu
from jax.sharding import PartitionSpec as P

GROUPS = 32
EPSILON = 1e-05
MESH = pl.DeviceIdType.MESH
F32 = jnp.float32
BF16 = jnp.bfloat16
AXES = ("tm", "row", "col")


class Plan:
    def __init__(self, f, h, w, c, sizes):
        self.f, self.h, self.w, self.c = f, h, w, c
        self.wp = 16
        while self.wp < w + 2:
            self.wp *= 2
        self.n = f * h * self.wp
        self.hp = h + 2
        self.np = (f + 2) * self.hp * self.wp
        self.cb = -(-(f * h) // 16) * 16
        self.rb = 2 * self.wp
        self.ntm, self.nrow, self.ncol = sizes
        self.na = self.nrow
        self.nb = self.ntm * self.ncol
        self.taps_rows = 27 * c
        unit = 16 * self.ntm * self.nrow * self.ncol
        units = -(-self.taps_rows // unit)
        first = -(-units // 2)
        self.sum_rows = units * unit
        self.parts = [(0, first * unit)]
        if units > first:
            self.parts.append((first * unit, (units - first) * unit))

    def stages(self, order):
        near = 2 if self.ncol % 2 == 0 else 1
        known = dict(
            near=("col", 1, near, True),
            col=("col", near, self.ncol // near, False),
            tm=("tm", 1, self.ntm, False),
            row=("row", 1, self.nrow, False),
        )
        return [known[name] for name in order if known[name][2] > 1]


class Link:
    def __init__(self, src, dst, sems, index, device, sends, receives):
        self.make = lambda: pltpu.make_async_remote_copy(
            src_ref=src,
            dst_ref=dst,
            send_sem=sems[0].at[index],
            recv_sem=sems[1].at[index],
            device_id=device,
            device_id_type=MESH,
        )
        self.sends, self.receives = sends, receives

    def start(self):
        if self.sends is None:
            self.make().start()
            return

        @pl.when(self.sends)
        def _():
            self.make().start()

    def wait_send(self):
        if self.sends is None:
            self.make().wait_send()
            return

        @pl.when(self.sends)
        def _():
            self.make().wait_send()

    def wait_recv(self):
        if self.receives is None:
            self.make().wait_recv()
            return

        @pl.when(self.receives)
        def _():
            self.make().wait_recv()


class Place:
    def __init__(self, plan):
        self.t, self.r, self.c = (lax.axis_index(a) for a in AXES)
        self.has = dict(
            left=self.c > 0,
            right=self.c < plan.ncol - 1,
            up=self.r > 0,
            down=self.r < plan.nrow - 1,
            past=self.t > 0,
            future=self.t < plan.ntm - 1,
        )
        self.dev = dict(
            left={"col": self.c - 1},
            right={"col": self.c + 1},
            up={"row": self.r - 1},
            down={"row": self.r + 1},
            past={"tm": self.t - 1},
            future={"tm": self.t + 1},
        )

    def partners(self, plan):
        rows = [{"row": lax.rem(self.r + d, plan.na)} for d in range(1, plan.na)]
        index = self.t * plan.ncol + self.c
        others = []
        for d in range(1, plan.nb):
            to = lax.rem(index + d, plan.nb)
            others.append({"tm": lax.div(to, plan.ncol), "col": lax.rem(to, plan.ncol)})
        return rows, others


class Reduce:
    def __init__(self, plan, place, refs, sems, base):
        self.own, self.slots_a, self.mid, self.slots_b = refs
        rows, others = place.partners(plan)
        self.a = [
            Link(self.own, self.slots_a.at[d], sems, base + d, dev, None, None)
            for d, dev in enumerate(rows)
        ]
        self.b = [
            Link(self.mid, self.slots_b.at[d], sems, base + len(rows) + d, dev, None, None)
            for d, dev in enumerate(others)
        ]

    def start(self, first, second):
        self.own[...] = jnp.zeros_like(self.own)
        self.own[0:1] = first
        self.own[1:2] = second
        for link in self.a:
            link.start()

    def middle(self):
        for link in self.a:
            link.wait_recv()
        total = self.own[...]
        for d in range(len(self.a)):
            total = total + self.slots_a[d]
        self.mid[...] = total
        for link in self.b:
            link.start()

    def finish(self):
        for link in self.b:
            link.wait_recv()
        total = self.mid[...]
        for d in range(len(self.b)):
            total = total + self.slots_b[d]
        return total

    def drain(self):
        for link in self.a + self.b:
            link.wait_send()


class KernelSum:
    def __init__(self, plan, place, stages, span, acc, done, outs, ins, sems, base):
        self.acc, self.done, self.outs, self.ins = acc, done, outs, ins
        self.stages = stages
        at, count = span
        self.spans, self.reduce, self.gather = [], [], []
        for k, (axis, stride, ways, wide) in enumerate(stages):
            here = dict(tm=place.t, row=place.r, col=place.c)[axis]
            mine = lax.rem(lax.div(here, stride), ways)
            piece = count // ways
            aligned = lambda v: pl.multiple_of(v, 16)
            kept = aligned(at + mine * piece)
            links, sources = [], []
            for d in range(1, ways):
                other = lax.rem(mine + d, ways)
                dev = {axis: here + (other - mine) * stride}
                sent = aligned(at + other * piece)
                if wide:
                    src = acc.at[pl.ds(sent, piece)]
                else:
                    src = outs[k].at[d - 1]
                    sources.append((d - 1, sent))
                links.append((Link(src, ins[k].at[d - 1], sems, base, dev, None, None), dev))
                base += 1
            self.reduce.append([link for link, _ in links])
            gathers = []
            for _, dev in links:
                part = done.at[pl.ds(kept, piece)]
                gathers.append(Link(part, part, sems, base, dev, None, None))
                base += 1
            self.gather.append(gathers)
            self.spans.append((kept, piece, sources))
            at, count = kept, piece
        self.base = base

    def steps(self):
        out = []
        last = len(self.stages) - 1
        for k in range(len(self.stages)):
            out.append(functools.partial(self.reduce_step, k))
        for k in range(last, -1, -1):
            out.append(functools.partial(self.gather_step, k))
        out.append(self.last_step)
        return out

    def reduce_step(self, k):
        if k:
            self.settle(k - 1)
        kept, piece, sources = self.spans[k]
        for slot, sent in sources:
            self.outs[k][slot] = self.acc[pl.ds(sent, piece)].astype(BF16)
        for link in self.reduce[k]:
            link.start()

    def settle(self, k):
        kept, piece, _ = self.spans[k]
        for link in self.reduce[k]:
            link.wait_recv()
        total = self.acc[pl.ds(kept, piece)]
        for d in range(len(self.reduce[k])):
            total = total + self.ins[k][d].astype(F32)
        if k == len(self.stages) - 1:
            self.done[pl.ds(kept, piece)] = total.astype(BF16)
        else:
            self.acc[pl.ds(kept, piece)] = total

    def gather_step(self, k):
        if k == len(self.stages) - 1:
            self.settle(k)
        else:
            for link in self.gather[k + 1]:
                link.wait_recv()
        for link in self.gather[k]:
            link.start()

    def last_step(self):
        for link in self.gather[0]:
            link.wait_recv()

    def drain(self):
        for links in self.reduce + self.gather:
            for link in links:
                link.wait_send()


ORDERS = (("near", "col", "tm", "row"), ("near", "tm", "col", "row"))


def sum_scratch(plan):
    shapes, counts = [], []
    for order, (_, count) in zip(ORDERS, plan.parts):
        outs, ins = [], []
        for axis, stride, ways, wide in plan.stages(order):
            piece = count // ways
            shape = (ways - 1, piece, plan.c)
            outs.append(pltpu.VMEM((1, 16, plan.c) if wide else shape, BF16))
            ins.append(pltpu.VMEM(shape, F32 if wide else BF16))
            count = piece
        counts.append(len(outs))
        shapes += outs + ins
    return shapes, counts


def sum_sems(plan):
    return 2 * sum(
        stage[2] - 1 for order, _ in zip(ORDERS, plan.parts) for stage in plan.stages(order)
    )


EX_SEMS = 10


class Exchange:
    def __init__(self, plan, place, refs, sems, base, directions):
        self.plan, self.place, self.directions = plan, place, directions
        self.own, self.cols_out, self.cols_in, self.rows_out, self.rows_in = refs[:5]
        has, dev = place.has, place.dev
        cb, half = plan.cb, plan.f * plan.wp
        self.cols = [
            Link(self.cols_out.at[pl.ds(0, cb)], self.cols_in.at[pl.ds(0, cb)], sems, base,
                 dev["left"], has["left"], has["right"]),
            Link(self.cols_out.at[pl.ds(cb, cb)], self.cols_in.at[pl.ds(cb, cb)], sems, base + 1,
                 dev["right"], has["right"], has["left"]),
        ]
        self.rows = [
            Link(self.rows_out.at[pl.ds(0, half)], self.rows_in.at[pl.ds(half, half)], sems,
                 base + 2, dev["up"], has["up"], has["down"]),
            Link(self.rows_out.at[pl.ds(half, half)], self.rows_in.at[pl.ds(0, half)], sems,
                 base + 3, dev["down"], has["down"], has["up"]),
        ]
        self.tm = {}
        for k, source in enumerate(directions):
            block, cols, rows = refs[5 + 3 * k : 8 + 3 * k]
            target = "future" if source == "past" else "past"
            links = [
                Link(src, dst, sems, base + 4 + 3 * k + j, dev[target], has[target], has[source])
                for j, (src, dst) in enumerate(
                    [(self.own, block), (self.cols_in, cols), (self.rows_in, rows)]
                )
            ]
            self.tm[source] = ((block, cols, rows), links)

    def clear(self):
        cb, half = self.plan.cb, self.plan.f * self.plan.wp
        has = self.place.has

        def zero(ref, part, cond):
            @pl.when(jnp.logical_not(cond))
            def _():
                ref[part] = jnp.zeros(ref.at[part].shape, ref.dtype)

        zero(self.cols_in, pl.ds(0, cb), has["right"])
        zero(self.cols_in, pl.ds(cb, cb), has["left"])
        zero(self.rows_in, pl.ds(0, half), has["up"])
        zero(self.rows_in, pl.ds(half, half), has["down"])
        for source, (refs, _) in self.tm.items():
            for ref in refs:
                zero(ref, pl.ds(0, ref.shape[0]), has[source])

    def start(self, wide, pick):
        self.own[...] = wide[...].astype(BF16)
        for source in self.directions:
            self.tm[source][1][0].start()
        self.cols_out[...] = jnp.dot(pick[...], self.own[...], preferred_element_type=F32).astype(BF16)
        for link in self.cols:
            link.start()

    def middle(self, wide, spread):
        plan = self.plan
        for link in self.cols:
            link.wait_recv()
        for source in self.directions:
            self.tm[source][1][1].start()
        ends = spread_cols(self.cols_in, spread)
        size = plan.h * plan.wp
        for f in range(plan.f):
            for k, at in enumerate((f * size, (f + 1) * size - plan.wp)):
                self.rows_out[pl.ds((k * plan.f + f) * plan.wp, plan.wp)] = (
                    wide[pl.ds(at, plan.wp)] + ends[at : at + plan.wp]
                ).astype(BF16)
        for link in self.rows:
            link.start()

    def later(self):
        for link in self.rows:
            link.wait_recv()
        for source in self.directions:
            self.tm[source][1][2].start()

    def finish(self):
        for source in self.directions:
            for link in self.tm[source][1]:
                link.wait_recv()

    def drain(self):
        for link in self.cols + self.rows:
            link.wait_send()
        for source in self.directions:
            for link in self.tm[source][1]:
                link.wait_send()

    def pieces(self, wide, spread, source):
        plan = self.plan
        size = plan.h * plan.wp
        (block, cols, rows), _ = self.tm[source]

        def of(value, border, side):
            out = []
            for f in range(plan.f):
                top = border[pl.ds(f * plan.wp, plan.wp)].astype(F32)
                low = border[pl.ds((plan.f + f) * plan.wp, plan.wp)].astype(F32)
                out.append((side, top, value[f * size : (f + 1) * size], low))
            return out

        inner = of(wide[...] + spread_cols(self.cols_in, spread), self.rows_in, None)
        outer = of(block[...].astype(F32) + spread_cols(cols, spread), rows, source)
        if source == "past":
            return outer[plan.f - 2 :] + inner
        return inner + outer[:2]


def spread_cols(cols, spread):
    return jnp.dot(spread[...], cols[...], preferred_element_type=F32)


def silu(v):
    return v / (1.0 + jnp.exp(-v))


def slope(v):
    sigm = 1.0 / (1.0 + jnp.exp(-v))
    return sigm * (1.0 + v * (1.0 - sigm))


def valid(plan, place, count, side, border):
    has = place.has
    w = lax.broadcasted_iota(jnp.int32, (count, plan.c), 0) & (plan.wp - 1)
    one = lambda cond: cond.astype(jnp.int32)
    mask = jnp.where(
        w < plan.w,
        1,
        jnp.where(
            w == plan.w,
            one(has["right"]),
            jnp.where(w == plan.wp - 1, one(has["left"]), 0),
        ),
    )
    for name in (side, border):
        if name is not None:
            mask = mask * one(has[name])
    return mask > 0


def store_shifted(plan, ref, at, value):
    count = value.shape[0]
    rows = value.reshape(count // plan.wp, plan.wp, plan.c)
    before = pltpu.roll(rows, 1, axis=1).reshape(value.shape)
    after = pltpu.roll(rows, plan.wp - 1, axis=1).reshape(value.shape)
    c = plan.c
    ref[pl.ds(at, count), 0:c] = before.astype(BF16)
    ref[pl.ds(at, count), c : 2 * c] = value.astype(BF16)
    ref[pl.ds(at, count), 2 * c : 3 * c] = after.astype(BF16)


def build(plan, ref, frames):
    for k, (top, rows, low) in enumerate(frames):
        at = k * plan.hp * plan.wp
        store_shifted(plan, ref, at, top)
        store_shifted(plan, ref, at + plan.wp, rows)
        store_shifted(plan, ref, at + (plan.h + 1) * plan.wp, low)


def convolve(plan, ref, kernel, out):
    size = plan.h * plan.wp

    def frame(f, carry):
        pieces = []
        for p in range(3):
            for q in range(3):
                at = pl.multiple_of(((f + p) * plan.hp + q) * plan.wp, plan.wp)
                pieces.append(ref[pl.ds(at, size), :])
        wide = jnp.dot(jnp.concatenate(pieces, axis=1), kernel[...], preferred_element_type=F32)
        w = lax.broadcasted_iota(jnp.int32, wide.shape, 0) & (plan.wp - 1)
        out[pl.ds(pl.multiple_of(f * size, size), size), :] = jnp.where(w < plan.w, wide, 0.0)
        return carry

    lax.fori_loop(0, plan.f, frame, 0)


def kernel_term(plan, ref, turned, part, low, high):
    size = plan.h * plan.wp

    def tap(pq, carry):
        p, q = lax.div(pq, 3), lax.rem(pq, 3)
        pieces = []
        for f in range(plan.f):
            at = pl.multiple_of(((f + p) * plan.hp + q) * plan.wp, plan.wp)
            pieces.append(ref[pl.ds(at, size), :])
        term = jnp.dot(turned, jnp.concatenate(pieces, axis=0), preferred_element_type=F32)
        part[pl.ds(pl.multiple_of(pq * 3 * plan.c, 3 * plan.c), 3 * plan.c), :] = term.T
        return carry

    lax.fori_loop(low, high, tap, 0)


def turn_kernel(plan, kernel, out):
    taps, c = 27, plan.c

    def tap(k, carry):
        source = kernel[pl.ds(pl.multiple_of((taps - 1 - k) * c, c), c), :]
        out[pl.ds(pl.multiple_of(k * c, c), c), :] = source.astype(F32).T.astype(BF16)
        return carry

    lax.fori_loop(0, taps, tap, 0)


def spaced(plan, ref, wide):
    wide[...] = jnp.zeros_like(wide)
    for f in range(plan.f):
        for y in range(plan.h):
            wide[pl.ds((f * plan.h + y) * plan.wp, plan.w)] = ref[f, y].astype(F32)


def unspaced(plan, value, ref):
    for f in range(plan.f):
        for y in range(plan.h):
            at = (f * plan.h + y) * plan.wp
            ref[f, y] = value[at : at + plan.w].astype(BF16)


def column_sum(value):
    return jnp.sum(value, axis=0, keepdims=True)


def body(plan, n_ex, *refs):
    refs = list(refs)
    take = lambda k: [refs.pop(0) for _ in range(k)]
    features, cotangent, kernel_one, kernel_two, *norms = take(8)
    block_out, grad_input, part_one, part_two = take(4)
    wide_x, wide_g, wide_h, wide_l, wide_b = take(5)
    pick, spread, turned_one, turned_two = take(4)
    x3_one, x3_two, x3_g, x3_h = take(4)
    exchange_refs = [take(k) for k in n_ex]
    reduce_refs = [take(4) for _ in range(4)]
    acc_one, acc_two, done_one, done_two = take(4)
    sum_refs = []
    for _ in range(2):
        for count in sum_scratch(plan)[1]:
            sum_refs.append((take(count), take(count)))
    sems = take(2)

    place = Place(plan)
    rows, others = place.partners(plan)
    per_reduce = len(rows) + len(others)
    exchanges = [
        Exchange(plan, place, r, sems, EX_SEMS * k, d)
        for k, (r, d) in enumerate(
            zip(exchange_refs, (("past",), ("future",), ("past", "future"), ("future",)))
        )
    ]
    ex_x, ex_g, ex_h, ex_l = exchanges
    reduces = [
        Reduce(plan, place, r, sems, EX_SEMS * 4 + per_reduce * k)
        for k, r in enumerate(reduce_refs)
    ]
    sums = []
    base = EX_SEMS * 4 + per_reduce * 4
    for acc, done in ((acc_two, done_two), (acc_one, done_one)):
        for order, span in zip(ORDERS, plan.parts):
            outs, ins = sum_refs[len(sums)]
            sums.append(
                KernelSum(plan, place, plan.stages(order), span, acc, done, outs, ins, sems, base)
            )
            base = sums[-1].base
        acc[pl.ds(plan.taps_rows, plan.sum_rows - plan.taps_rows)] = jnp.zeros(
            (plan.sum_rows - plan.taps_rows, plan.c), F32
        )
    sums_two, sums_one = sums[: len(plan.parts)], sums[len(plan.parts) :]
    steps_two = [list(group) for group in zip(*[item.steps() for item in sums_two])]

    def advance():
        if steps_two:
            for step in steps_two.pop(0):
                step()

    for ex in exchanges:
        ex.clear()

    barrier = pltpu.get_barrier_semaphore()
    for dev in rows + others:
        pl.semaphore_signal(barrier, inc=1, device_id=dev, device_id_type=MESH)

    c = plan.c
    per_group = c // GROUPS
    members = float(plan.f * plan.h * plan.w * plan.ntm * plan.nrow * plan.ncol * per_group)
    lane_i = lax.broadcasted_iota(jnp.int32, (c, c), 0)
    lane_j = lax.broadcasted_iota(jnp.int32, (c, c), 1)
    same = (lax.div(lane_i, per_group) == lax.div(lane_j, per_group)).astype(F32)

    def group_means(total):
        sums = jnp.dot(
            total, same, preferred_element_type=F32, precision=lax.Precision.HIGHEST
        )
        return sums[0:1] / members, sums[1:2] / members

    def moments(total):
        average, square = group_means(total)
        return average, lax.rsqrt(square - average * average + EPSILON)

    spaced(plan, features, wide_x)
    j = lax.broadcasted_iota(jnp.int32, (2 * plan.cb, plan.n), 0)
    at = lax.broadcasted_iota(jnp.int32, (2 * plan.cb, plan.n), 1)
    first = j < plan.cb
    pick[...] = (
        at == jnp.where(first, j * plan.wp, (j - plan.cb) * plan.wp + plan.w - 1)
    ).astype(F32).astype(BF16)
    at = lax.broadcasted_iota(jnp.int32, (plan.n, 2 * plan.cb), 0)
    j = lax.broadcasted_iota(jnp.int32, (plan.n, 2 * plan.cb), 1)
    first = j < plan.cb
    spread[...] = (
        at == jnp.where(first, j * plan.wp + plan.w, (j - plan.cb) * plan.wp + plan.wp - 1)
    ).astype(F32).astype(BF16)

    pl.semaphore_wait(barrier, per_reduce)
    gain_one, shift_one, gain_two, shift_two = (ref[...] for ref in norms)

    x = wide_x[...]
    reduces[0].start(column_sum(x), column_sum(x * x))
    ex_x.start(wide_x, pick)
    spaced(plan, cotangent, wide_g)
    ex_g.start(wide_g, pick)
    reduces[0].middle()
    ex_x.middle(wide_x, spread)
    ex_g.middle(wide_g, spread)
    turn_kernel(plan, kernel_two, turned_two)
    ex_x.later()
    ex_g.later()
    turn_kernel(plan, kernel_one, turned_one)
    mean_one, scale_one = moments(reduces[0].finish())
    ex_x.finish()

    def unit_one(v):
        return (v - mean_one) * scale_one

    def frames_of(pieces, fn):
        out = []
        for side, top, rows_, low in pieces:
            keep = lambda v, border: jnp.where(
                valid(plan, place, v.shape[0], side, border), fn(v), 0.0
            )
            out.append((keep(top, "up"), keep(rows_, None), keep(low, "down")))
        return out

    build(
        plan,
        x3_one,
        frames_of(
            ex_x.pieces(wide_x, spread, "past"),
            lambda v: silu(unit_one(v) * gain_one + shift_one),
        ),
    )
    convolve(plan, x3_one, kernel_one, wide_h)
    hidden = wide_h[...]
    reduces[1].start(column_sum(hidden), column_sum(hidden * hidden))
    ex_h.start(wide_h, pick)
    reduces[1].middle()
    ex_h.middle(wide_h, spread)
    ex_g.finish()
    build(plan, x3_g, [p[1:] for p in ex_g.pieces(wide_g, spread, "future")])
    ex_h.later()
    convolve(plan, x3_g, turned_two, wide_b)
    mean_two, scale_two = moments(reduces[1].finish())

    def unit_two(v):
        return (v - mean_two) * scale_two

    unit = unit_two(wide_h[...])
    lifted = wide_b[...] * slope(unit * gain_two + shift_two) * gain_two
    wide_l[...] = lifted
    reduces[2].start(column_sum(lifted), column_sum(lifted * unit))
    ex_l.start(wide_l, pick)
    reduces[2].middle()
    ex_l.middle(wide_l, spread)
    ex_h.finish()
    build(
        plan,
        x3_two,
        frames_of(
            ex_h.pieces(wide_h, spread, "past"),
            lambda v: silu(unit_two(v) * gain_two + shift_two),
        ),
    )
    ex_l.later()
    kernel_term(plan, x3_two, wide_g[...].T.astype(BF16), acc_two, 0, 9)
    a_two, b_two = group_means(reduces[2].finish())
    advance()
    ex_l.finish()
    frames = []
    for (side, *lifts), (_, *hids) in zip(
        ex_l.pieces(wide_l, spread, "future"), ex_h.pieces(wide_h, spread, "future")
    ):
        out = []
        for border, lift, hid in zip(("up", None, "down"), lifts, hids):
            value = scale_two * (lift - a_two - unit_two(hid) * b_two)
            out.append(jnp.where(valid(plan, place, lift.shape[0], side, border), value, 0.0))
        frames.append(tuple(out))
    build(plan, x3_h, frames)
    advance()
    w = lax.broadcasted_iota(jnp.int32, (plan.h * plan.wp, c), 0) & (plan.wp - 1)
    own = jnp.concatenate(
        [jnp.where(w < plan.w, frames[f][1], 0.0) for f in range(plan.f)], axis=0
    )
    turned = own.T.astype(BF16)
    ready = min(9, -(-plan.parts[0][1] // (3 * c)))
    kernel_term(plan, x3_one, turned, acc_one, 0, ready)
    steps_one = [item.steps() for item in sums_one]
    steps_one[0].pop(0)()
    advance()
    kernel_term(plan, x3_one, turned, acc_one, ready, 9)
    for steps in steps_one[1:]:
        steps.pop(0)()

    def advance_one():
        for steps in steps_one:
            steps.pop(0)()

    convolve(plan, x3_h, turned_one, wide_b)
    unit = unit_one(wide_x[...])
    lifted = wide_b[...] * slope(unit * gain_one + shift_one) * gain_one
    reduces[3].start(column_sum(lifted), column_sum(lifted * unit))
    wide_l[...] = lifted
    advance_one()
    advance()
    reduces[3].middle()
    convolve(plan, x3_two, kernel_two, wide_b)
    advance_one()
    advance()
    unspaced(plan, wide_x[...] + wide_b[...], block_out)
    a_one, b_one = group_means(reduces[3].finish())
    advance_one()
    advance()
    unit = unit_one(wide_x[...])
    unspaced(
        plan,
        wide_g[...] + scale_one * (wide_l[...] - a_one - unit * b_one),
        grad_input,
    )
    while steps_one[0]:
        advance_one()
        advance()
    part_two[...] = done_two[pl.ds(0, plan.taps_rows)]
    part_one[...] = done_one[pl.ds(0, plan.taps_rows)]
    for item in exchanges + reduces + sums:
        item.drain()


def block_kernel(plan, features, cotangent, kernel_one, kernel_two, *norms):
    c, n = plan.c, plan.n
    half = plan.f * plan.wp
    exchange = []
    n_ex = []
    for count in (1, 1, 2, 1):
        shapes = [(n, c), (2 * plan.cb, c), (2 * plan.cb, c), (2 * half, c), (2 * half, c)]
        shapes += [(n, c), (2 * plan.cb, c), (2 * half, c)] * count
        n_ex.append(len(shapes))
        exchange += [pltpu.VMEM(s, BF16) for s in shapes]
    reduce = [
        pltpu.VMEM((8, c), F32),
        pltpu.VMEM((max(1, plan.na - 1), 8, c), F32),
        pltpu.VMEM((8, c), F32),
        pltpu.VMEM((max(1, plan.nb - 1), 8, c), F32),
    ] * 4
    sems = 4 * EX_SEMS + 4 * (plan.na + plan.nb - 2) + 2 * sum_sems(plan)
    vmem = pl.BlockSpec(memory_space=pltpu.VMEM)
    taps = kernel_one.shape[0]
    return pl.pallas_call(
        functools.partial(body, plan, n_ex),
        out_shape=(
            jax.ShapeDtypeStruct(features.shape, BF16),
            jax.ShapeDtypeStruct(features.shape, BF16),
            jax.ShapeDtypeStruct((taps, c), BF16),
            jax.ShapeDtypeStruct((taps, c), BF16),
        ),
        in_specs=[vmem] * 8,
        out_specs=(vmem,) * 4,
        scratch_shapes=[pltpu.VMEM((n, c), F32)] * 5
        + [pltpu.VMEM((2 * plan.cb, n), BF16), pltpu.VMEM((n, 2 * plan.cb), BF16)]
        + [pltpu.VMEM((taps, c), BF16)] * 2
        + [pltpu.VMEM((plan.np, 3 * c), BF16)] * 4
        + exchange
        + reduce
        + [pltpu.VMEM((plan.sum_rows, c), F32)] * 2
        + [pltpu.VMEM((plan.sum_rows, c), BF16)] * 2
        + sum_scratch(plan)[0] * 2
        + [pltpu.SemaphoreType.DMA((sems,))] * 2,
        compiler_params=pltpu.CompilerParams(
            collective_id=0, has_side_effects=True, vmem_limit_bytes=52 * 2**20
        ),
    )(features, cotangent, kernel_one, kernel_two, *norms)


SLOT = 16
MANY = 256
SHARES = (((3, True), (2, True), (2, True)), ((2, False), (3, True), (2, True)))
VMEM_ASK = 60 * 2**20


class Split:
    def __init__(self, f, h, w, c, sizes):
        self.f, self.h, self.w, self.c = f, h, w, c
        self.ntm, self.nrow, self.ncol = sizes
        self.frames = f * self.ntm
        self.half = w // 2
        self.fn = h * SLOT
        self.pn = (h + 2) * SLOT
        self.n = self.frames * self.fn
        self.hs = -(-h // 16) * 16
        self.ext = self.frames * self.hs
        self.wide = 2 * SLOT
        self.gn = -(-self.fn // 128) * 128
        self.taps_rows = 27 * c
        self.nxy = self.ntm * (self.ncol // 2)
        unit = 32 * self.nxy * self.nrow
        units = -(-self.taps_rows // unit)
        self.sum_rows = units * unit
        self.parts = [self.cut(units, unit, shares) for shares in SHARES]
        self.cells = h * w
        self.cells_up = -(-self.cells // 8) * 8

    @staticmethod
    def cut(units, unit, shares):
        whole = sum(share for share, _ in shares)
        parts, at, taken = [], 0, 0
        for share, plane_first in shares:
            taken += share
            end = units * taken // whole
            if end > at:
                parts.append((at * unit, (end - at) * unit, plane_first))
            at = end
        return parts

    @staticmethod
    def fits(f, h, w, c, sizes):
        ntm, nrow, ncol = sizes
        return (
            ntm == 2
            and ncol % 2 == 0
            and w % 2 == 0
            and SLOT < w <= 2 * SLOT
            and w // 2 + 2 <= SLOT
            and w - SLOT <= w // 2 - 1
            and h <= 16
            and f * ntm * 16 <= 64
            and f * ntm >= 3
        )


class Spot:
    def __init__(self, plan):
        self.t, self.r, self.c = (lax.axis_index(a) for a in AXES)
        self.k = 2 * self.c + self.t
        self.left = self.k > 0
        self.right = self.k < 2 * plan.ncol - 1
        self.up = self.r > 0
        self.down = self.r < plan.nrow - 1
        self.core = lax.rem(self.c, 2)
        self.y = lax.div(self.c, 2)

    def peers(self, plan):
        offsets = [
            (dt, dr, dc)
            for dt in range(plan.ntm)
            for dr in range(plan.nrow)
            for dc in range(plan.ncol)
            if (dt, dr, dc) != (0, 0, 0)
        ]
        offsets.sort(key=lambda o: -(2 * (o[1] > 0) + o[0] + min(1, o[2])))
        out = []
        for dt, dr, dc in offsets:
            out.append(
                {
                    "tm": lax.rem(self.t + dt, plan.ntm),
                    "row": lax.rem(self.r + dr, plan.nrow),
                    "col": lax.rem(self.c + dc, plan.ncol),
                }
            )
        return out

    def plane(self, plan):
        me = self.t * (plan.ncol // 2) + self.y
        out = []
        for d in range(1, plan.nxy):
            o = lax.rem(me + d, plan.nxy)
            dev = {
                "tm": lax.div(o, plan.ncol // 2),
                "col": 2 * lax.rem(o, plan.ncol // 2) + self.core,
            }
            out.append((o, dev))
        return me, out

    def line(self, plan):
        out = []
        for d in range(1, plan.nrow):
            o = lax.rem(self.r + d, plan.nrow)
            out.append((o, {"row": o}))
        return self.r, out


class Counter:
    def __init__(self):
        self.at = 0

    def take(self):
        self.at += 1
        return self.at - 1


class Total:
    def __init__(self, peers, own, slots, sems, counter):
        self.own, self.slots, self.peers, self.sems = own, slots, peers, sems
        self.index = counter.take()

    def start(self, first, second):
        self.own[0:1] = first
        self.own[1:2] = second
        for d, dev in enumerate(self.peers):
            pltpu.make_async_remote_copy(
                src_ref=self.own.at[pl.ds(0, 2)],
                dst_ref=self.slots.at[d, pl.ds(0, 2)],
                send_sem=self.sems[0].at[self.index],
                recv_sem=self.sems[1].at[self.index],
                device_id=dev,
                device_id_type=MESH,
            ).start()

    def whole(self, k):
        part = self.slots.at[pl.ds(0, len(self.peers)), pl.ds(0, 2)]
        return pltpu.make_async_copy(part, part, self.sems[k].at[self.index])

    def finish(self):
        self.whole(1).wait()
        total = self.own[0:2]
        for d in range(len(self.peers)):
            total = total + self.slots[d, 0:2]
        return total

    def drain(self):
        self.whole(0).wait()


class Halo:
    def __init__(self, plan, spot, refs, sems, counter):
        self.plan, self.spot = plan, spot
        self.block, self.edge, self.top, self.bot, self.ch = refs
        self.sems, self.counter = sems, counter
        self.links = []

    def link(self, src, dst, dev, sends, receives):
        item = Link(src, dst, self.sems, self.counter.take(), dev, sends, receives)
        self.links.append(item)
        return item

    def rows(self):
        s = self.spot
        return ((1, s.r + 1, s.down, s.up), (2, s.r - 1, s.up, s.down))

    def lines(self):
        s = self.spot
        return ((0, None, None, None),) + self.rows()

    def clear(self):
        for ref in (self.top, self.bot, self.ch):
            ref[...] = jnp.zeros(ref.shape, BF16)

    def wait(self):
        for link in self.links:
            link.wait_recv()

    def drain(self):
        for link in self.links:
            link.wait_send()


def both(*conds):
    out = None
    for cond in conds:
        if cond is not None:
            out = cond if out is None else jnp.logical_and(out, cond)
    return out


class Reshard(Halo):
    def __init__(self, plan, spot, pair, refs, sems, counter):
        super().__init__(plan, spot, refs, sems, counter)
        self.pair = pair
        t, r, c, f = spot.t, spot.r, spot.c, plan.f
        n = plan.ncol
        self.link(pair.at[1 - t], self.block.at[pl.ds(f * t, f)], {"tm": 1 - t}, None, None)
        for which, row, sends, receives in self.rows():
            src_at = plan.fn - SLOT if which == 1 else 0
            dst = (self.top if which == 1 else self.bot).at[pl.ds(f * t, f)]
            for d in range(2):
                to = t if d == 0 else 1 - t
                self.link(pair.at[to, :, pl.ds(src_at, SLOT)], dst, {"tm": to, "row": row}, sends, receives)
        rows = f * plan.hs
        for which, row, sends, receives in self.lines():
            for d in range(2):
                dev = {"tm": t - d, "col": c + 1}
                if row is not None:
                    dev["row"] = row
                self.link(
                    self.edge.at[1], self.ch.at[which, pl.ds(rows * d, rows)], dev,
                    both(t == d, c < n - 1, sends), both(t == 0, c > 0, receives),
                )
                dev = {"tm": t - d + 1, "col": c - 1}
                if row is not None:
                    dev["row"] = row
                self.link(
                    self.edge.at[0], self.ch.at[which, pl.ds(plan.ext + rows * d, rows)], dev,
                    both(t == d, c > 0, sends), both(t == 1, c < n - 1, receives),
                )

    def start(self, stage, rows, w32):
        plan, t = self.plan, self.spot.t
        step = 8 * plan.f
        for k in range(plan.cells_up // 8):
            rows[pl.ds(step * k, step)] = stage[pl.ds(8 * k, 8)].astype(F32).reshape(step, plan.c)
        for f in range(plan.f):
            for y in range(plan.h):
                w32[pl.ds((f * plan.h + y) * plan.wide, plan.w)] = rows[
                    pl.ds(y * plan.w * plan.f + f, plan.w, plan.f)
                ]
        slot = lax.broadcasted_iota(jnp.int32, (plan.h, SLOT, plan.c), 1)
        for f in range(plan.f):
            v = w32[pl.ds(f * plan.h * plan.wide, plan.h * plan.wide)]
            v = v.reshape(plan.h, plan.wide, plan.c)
            low, high = v[:, :SLOT], v[:, SLOT:]
            second = jnp.where(slot >= plan.half - 1, low, high)
            self.pair[0, f] = low.reshape(plan.fn, plan.c).astype(BF16)
            self.pair[1, f] = second.reshape(plan.fn, plan.c).astype(BF16)
            for side, x in ((0, 0), (1, plan.w - 1)):
                at = f * plan.h * plan.wide + x
                self.edge[side, pl.ds(f * plan.hs, plan.hs)] = w32[
                    pl.ds(at, plan.hs, plan.wide)
                ].astype(BF16)

    def send(self):
        self.links[0].start()

    def send_rest(self):
        for link in self.links[1:]:
            link.start()

    def keep(self):
        self.block[pl.ds(self.plan.f * self.spot.t, self.plan.f)] = self.pair[self.spot.t]


class Border(Halo):
    def __init__(self, plan, spot, refs, sems, counter):
        super().__init__(plan, spot, refs, sems, counter)
        t, c = spot.t, spot.c
        for which, row, sends, receives in self.rows():
            at = plan.fn - SLOT if which == 1 else 0
            dst = self.top if which == 1 else self.bot
            self.link(self.block.at[:, pl.ds(at, SLOT)], dst, {"row": row}, sends, receives)
        for which, row, sends, receives in self.lines():
            dev = {"tm": 1 - t, "col": c - 1 + t}
            if row is not None:
                dev["row"] = row
            self.link(
                self.edge.at[0], self.ch.at[which, pl.ds(plan.ext, plan.ext)], dev,
                both(spot.left, sends), both(spot.right, receives),
            )
            dev = {"tm": 1 - t, "col": c + t}
            if row is not None:
                dev["row"] = row
            self.link(
                self.edge.at[1], self.ch.at[which, pl.ds(0, plan.ext)], dev,
                both(spot.right, sends), both(spot.left, receives),
            )

    def start(self, wide):
        plan, t = self.plan, self.spot.t
        for f in range(plan.frames):
            self.block[f] = wide[pl.ds(f * plan.fn, plan.fn)].astype(BF16)
            for side, offset in ((0, 0), (1, plan.half - 1)):
                values = [
                    wide[pl.ds(f * plan.fn + (plan.half * k + offset) % SLOT, plan.hs, SLOT)]
                    for k in range(2)
                ]
                self.edge[side, pl.ds(f * plan.hs, plan.hs)] = jnp.where(
                    t == 0, values[0], values[1]
                ).astype(BF16)
        for link in self.links:
            link.start()


class Part:
    def __init__(self, plan, spot, span, acc, done, out, refs, sems, counter, local_sem):
        self.acc, self.done = acc, done
        self.core_out, self.core_in, out1, self.in1, out2, self.in2 = refs
        self.at, self.count, plane_first = span
        rows = pl.ds(self.at, min(self.count, plan.taps_rows - self.at))
        self.out = pltpu.make_async_copy(done.at[rows], out.at[rows], local_sem)
        link = lambda src, dst, dev: Link(src, dst, sems, counter.take(), dev, None, None)
        aligned = lambda v: pl.multiple_of(v, 16)
        half = self.count // 2
        base = aligned(self.at + spot.core * half)
        other = aligned(self.at + (1 - spot.core) * half)
        sibling = {"col": spot.c + 1 - 2 * spot.core}
        self.other = pl.ds(other, half)
        self.core = link(self.core_out, self.core_in, sibling)
        stages = (spot.plane(plan), spot.line(plan))
        if not plane_first:
            stages = stages[::-1]
        (one, ones), (two, twos) = stages
        self.big = big = half // (len(ones) + 1)
        self.small = small = big // (len(twos) + 1)
        self.own1_in = aligned(one * big)
        self.own1 = own1 = aligned(base + one * big)
        self.own2 = own2 = aligned(own1 + two * small)
        self.send1 = [
            (aligned(base + o * big), aligned(o * big), out1.at[d], link(out1.at[d], self.in1.at[d], dev))
            for d, (o, dev) in enumerate(ones)
        ]
        self.send2 = [
            (aligned(own1 + o * small), out2.at[d], link(out2.at[d], self.in2.at[d], dev))
            for d, (o, dev) in enumerate(twos)
        ]
        piece2 = done.at[pl.ds(own2, small)]
        self.gather2 = [link(piece2, piece2, dev) for _, dev in twos]
        piece1 = done.at[pl.ds(own1, big)]
        self.gather1 = [link(piece1, piece1, dev) for _, dev in ones]
        self.forward = [link(piece1, piece1, sibling)]
        for d in range(len(ones)):
            o, _ = ones[len(ones) - 1 - d]
            ref = done.at[pl.ds(aligned(base + o * big), big)]
            self.forward.append(link(ref, ref, sibling))

    def start(self):
        self.core_out[...] = self.acc[self.other].astype(BF16)
        self.core.start()

    def first(self):
        self.core.wait_recv()
        for at, inside, out, link in self.send1:
            out[...] = (
                self.acc[pl.ds(at, self.big)] + self.core_in[pl.ds(inside, self.big)].astype(F32)
            ).astype(BF16)
            link.start()

    def second(self):
        big, own1 = self.big, self.own1
        total = self.acc[pl.ds(own1, big)] + self.core_in[pl.ds(self.own1_in, big)].astype(F32)
        for d, item in enumerate(self.send1):
            item[-1].wait_recv()
            total = total + self.in1[d].astype(F32)
        self.acc[pl.ds(own1, big)] = total
        for at, out, link in self.send2:
            out[...] = self.acc[pl.ds(at, self.small)].astype(BF16)
            link.start()

    def third(self):
        total = self.acc[pl.ds(self.own2, self.small)]
        for d, item in enumerate(self.send2):
            item[-1].wait_recv()
            total = total + self.in2[d].astype(F32)
        self.done[pl.ds(self.own2, self.small)] = total.astype(BF16)
        for link in self.gather2:
            link.start()

    def fourth(self):
        for link in self.gather2:
            link.wait_recv()
        for link in self.gather1:
            link.start()
        self.forward[0].start()

    def fifth(self):
        for d, link in enumerate(self.gather1):
            link.wait_recv()
            self.forward[1 + d].start()

    def sixth(self):
        for link in self.forward:
            link.wait_recv()
        self.out.start()

    def drain(self):
        self.core.wait_send()
        for item in self.send1 + self.send2:
            item[-1].wait_send()
        for link in self.gather2 + self.gather1 + self.forward:
            link.wait_send()
        self.out.wait()


def part_scratch(plan):
    shapes = []
    for _, count, plane_first in plan.parts[0] + plan.parts[1]:
        ways = (plan.nxy, plan.nrow) if plane_first else (plan.nrow, plan.nxy)
        big = count // 2 // ways[0]
        small = big // ways[1]
        shapes += [pltpu.VMEM((count // 2, plan.c), BF16)] * 2
        for rows, k in ((big, ways[0]), (big, ways[0]), (small, ways[1]), (small, ways[1])):
            shapes.append(pltpu.VMEM((max(1, k - 1), rows, plan.c), BF16))
    return shapes


def around(value, by):
    rows = value.reshape(value.shape[0] // SLOT, SLOT, value.shape[1])
    return pltpu.roll(rows, by, axis=1).reshape(value.shape)


def convolve_split(plan, padded, weight, out, keep, future):
    c = plan.c
    for t in range(plan.frames):
        pieces, used = [], []
        for p in range(3):
            source = t + p if future else t + p - 2
            if not 0 <= source < plan.frames:
                continue
            used.append(p)
            for q in range(3):
                pieces.append(padded[pl.ds(source * plan.pn + q * SLOT, plan.fn), :])
        lhs = jnp.concatenate(pieces, axis=1)
        rhs = weight[3 * used[0] : 3 * used[-1] + 3].reshape(3 * len(used) * c, 3 * c)
        wide = jnp.dot(lhs, rhs, preferred_element_type=F32)
        total = around(wide[:, 0:c], 1) + wide[:, c : 2 * c] + around(wide[:, 2 * c :], SLOT - 1)
        out[pl.ds(t * plan.fn, plan.fn), :] = keep(total)


def place_padded(plan, ref, value, top, bot):
    for t in range(plan.frames):
        at = t * plan.pn
        ref[pl.ds(at, SLOT), :] = top[t * SLOT : (t + 1) * SLOT].astype(BF16)
        ref[pl.ds(at + SLOT, plan.fn), :] = value[t * plan.fn : (t + 1) * plan.fn].astype(BF16)
        ref[pl.ds(at + SLOT + plan.fn, SLOT), :] = bot[t * SLOT : (t + 1) * SLOT].astype(BF16)


def shifted_grad(plan, ref, value):
    c = plan.c
    for s, moved in enumerate((around(value, SLOT - 1), value, around(value, 1))):
        for t in range(plan.frames):
            ref[pl.ds(t * plan.gn, plan.fn), s * c : (s + 1) * c] = moved[
                t * plan.fn : (t + 1) * plan.fn
            ].astype(BF16)


def turned_acted(plan, padded, ref):
    c = plan.c
    for q in range(3):
        for t in range(plan.frames):
            slab = padded[pl.ds(t * plan.pn + q * SLOT, plan.gn), :]
            ref[q * c : (q + 1) * c, t * plan.gn : (t + 1) * plan.gn] = slab.T


def kernel_grad(plan, turned, moved, acc, p):
    c = plan.c
    lag = 2 - p
    count = (plan.frames - lag) * plan.gn
    term = jnp.dot(
        turned[:, 0:count], moved[pl.ds(lag * plan.gn, count), :], preferred_element_type=F32
    )
    for q in range(3):
        for s in range(3):
            acc[pl.ds((9 * p + 3 * q + s) * c, c), :] = term[
                q * c : (q + 1) * c, s * c : (s + 1) * c
            ]


def turn_weight(plan, weight, out):
    c = plan.c
    for k in range(27):
        j = 26 - k
        source = weight[j // 3, :, (j % 3) * c : (j % 3 + 1) * c]
        out[k // 3, :, (k % 3) * c : (k % 3 + 1) * c] = source.T


def split_body(plan, *refs):
    refs = list(refs)
    take = lambda k: [refs.pop(0) for _ in range(k)]
    features, cotangent, conv_one, conv_two, *norms = take(8)
    block_out, grad_input, part_one, part_two = take(4)
    w32, rows32, stage_x, stage_g = take(4)
    done_one, done_two = take(2)
    wide_h, wide_l, wide_b, unit_h = take(4)
    spread_mid, spread_top, spread_bot = take(3)
    weight_one, weight_two, turned_one, turned_two = take(4)
    pad_one, pad_two, pad_g, pad_h = take(4)
    at_one, at_two, moved_g, moved_h = take(4)
    acc_one, acc_two = take(2)
    norm_in = take(4)
    pair_x, pair_g = take(2)
    halo_refs = [take(5) for _ in range(4)]
    total_refs = [take(2) for _ in range(4)]
    sum_refs = [[take(6) for _ in parts] for parts in plan.parts]
    out_refs = [take(2) for _ in range(2)]
    sems = take(2)
    (local_sem,) = take(1)

    spot = Spot(plan)
    peers = spot.peers(plan)
    counter = Counter()
    c = plan.c

    loads = []
    cells = pl.ds(0, plan.cells)
    for k, (src, dst) in enumerate(
        [(features, stage_x.at[cells]), (cotangent, stage_g.at[cells])]
        + list(zip(norms, norm_in))
        + [(conv_one.at[:, s], weight_one.at[:, :, pl.ds(s * c, c)]) for s in range(3)]
        + [(conv_two.at[:, s], weight_two.at[:, :, pl.ds(s * c, c)]) for s in range(3)]
    ):
        loads.append(pltpu.make_async_copy(src, dst, local_sem.at[k]))
    for copy in loads[:2]:
        copy.start()

    ex_x = Reshard(plan, spot, pair_x, halo_refs[0], sems, counter)
    ex_g = Reshard(plan, spot, pair_g, halo_refs[1], sems, counter)
    ex_h = Border(plan, spot, halo_refs[2], sems, counter)
    ex_l = Border(plan, spot, halo_refs[3], sems, counter)
    totals = [Total(peers, *r, sems, counter) for r in total_refs]
    sums_two, sums_one = (
        [
            Part(plan, spot, span, acc, done, out, r, sems, counter, local_sem.at[first + k])
            for k, (span, r) in enumerate(zip(parts, group))
        ]
        for acc, done, out, parts, group, first in (
            (acc_two, done_two, part_two, plan.parts[0], sum_refs[0], 16),
            (acc_one, done_one, part_one, plan.parts[1], sum_refs[1], 16 + len(plan.parts[0])),
        )
    )
    outs = []
    for (mine, theirs) in out_refs:
        outs.append(
            Link(
                mine.at[pl.ds(plan.f * (1 - spot.t), plan.f)], theirs, sems, counter.take(),
                {"tm": 1 - spot.t}, None, None,
            )
        )
    assert counter.at <= MANY

    for ex in (ex_x, ex_g, ex_h, ex_l):
        ex.clear()
    barrier = pltpu.get_barrier_semaphore()
    for dev in peers:
        pl.semaphore_signal(barrier, inc=1, device_id=dev, device_id_type=MESH)
    for copy in loads[2:]:
        copy.start()

    per_group = c // GROUPS
    members = float(plan.n // SLOT * plan.half * 2 * plan.nrow * plan.ncol * per_group)
    lane_i = lax.broadcasted_iota(jnp.int32, (c, c), 0)
    lane_j = lax.broadcasted_iota(jnp.int32, (c, c), 1)
    same = (lax.div(lane_i, per_group) == lax.div(lane_j, per_group)).astype(F32)

    def group_means(total):
        sums = jnp.dot(total, same, preferred_element_type=F32, precision=lax.Precision.HIGHEST)
        return sums[0:1] / members, sums[1:2] / members

    def moments(total):
        average, square = group_means(total)
        return average, lax.rsqrt(square - average * average + EPSILON)

    w32[...] = jnp.zeros(w32.shape, F32)
    for stage in (stage_x, stage_g):
        spare = plan.cells_up - plan.cells
        if spare:
            stage[pl.ds(plan.cells, spare)] = jnp.zeros((spare, plan.f, c), BF16)
    loads[0].wait()
    ex_x.start(stage_x, rows32, w32)
    x = w32[...]
    first, second = column_sum(x), column_sum(x * x)
    pl.semaphore_wait(barrier, len(peers))
    ex_x.send()
    totals[0].start(first, second)
    ex_x.send_rest()
    loads[1].wait()
    ex_g.start(stage_g, rows32, w32)
    ex_g.send()
    ex_g.send_rest()
    ex_x.keep()
    ex_g.keep()

    rel = (lax.broadcasted_iota(jnp.int32, (SLOT, c), 0) - plan.half * spot.t) & (SLOT - 1)
    one = lambda cond: cond.astype(jnp.int32)
    inside = rel < plan.half
    inner = jnp.where(spot.t == 0, plan.half, SLOT - 1)
    kept = jnp.logical_or(inside, rel == inner)
    legal = jnp.where(
        inside, 1, jnp.where(rel == plan.half, one(spot.right), jnp.where(rel == SLOT - 1, one(spot.left), 0))
    )

    def masked(value, mask):
        rows = value.reshape(value.shape[0] // SLOT, SLOT, c)
        return jnp.where(mask[None], rows, 0.0).reshape(value.shape)

    interior = lambda value: masked(value, inside)

    def targets(rows, source):
        i = lax.broadcasted_iota(jnp.int32, (rows, 2 * plan.ext), 0)
        j = lax.broadcasted_iota(jnp.int32, (rows, 2 * plan.ext), 1)
        where = ((i & (SLOT - 1)) - plan.half * spot.t) & (SLOT - 1)
        code = source(i >> 4)
        aim = jnp.where(where == SLOT - 1, code, jnp.where(where == plan.half, code + plan.ext, -1))
        return (j == aim).astype(F32).astype(BF16)

    def of_group(g):
        t = 0
        for k in range(1, plan.frames):
            t = t + (g >= k * plan.h).astype(jnp.int32)
        return g + t * (plan.hs - plan.h)

    spread_mid[...] = targets(plan.n, of_group)
    spread_top[...] = targets(plan.frames * SLOT, lambda t: t * plan.hs + plan.h - 1)
    spread_bot[...] = targets(plan.frames * SLOT, lambda t: t * plan.hs)
    for ref in (pad_one, pad_two):
        ref[pl.ds(plan.frames * plan.pn, SLOT), :] = jnp.zeros((SLOT, c), BF16)
    if plan.gn > plan.fn:
        for ref in (moved_g, moved_h):
            for t in range(plan.frames):
                ref[pl.ds(t * plan.gn + plan.fn, plan.gn - plan.fn), :] = jnp.zeros(
                    (plan.gn - plan.fn, 3 * c), BF16
                )
    for ref in (wide_h, wide_l):
        ref[pl.ds(plan.n, SLOT), :] = jnp.zeros((SLOT, c), F32)
    for acc in (acc_one, acc_two):
        acc[pl.ds(plan.taps_rows, plan.sum_rows - plan.taps_rows)] = jnp.zeros(
            (plan.sum_rows - plan.taps_rows, c), F32
        )
    for copy in loads[2:]:
        copy.wait()
    gain_one, shift_one, gain_two, shift_two = (ref[...] for ref in norm_in)
    turn_weight(plan, weight_two, turned_two)

    def assemble(ex, value, mask):
        flat = lambda ref: ref[...].astype(F32).reshape(plan.frames * SLOT, c)
        spread = lambda by, k: jnp.dot(by[...], ex.ch[k], preferred_element_type=F32)
        return (
            masked(value, mask) + spread(spread_mid, 0),
            masked(flat(ex.top), mask) + spread(spread_top, 1),
            masked(flat(ex.bot), mask) + spread(spread_bot, 2),
        )

    def clip(values):
        value, top, bot = values
        return (
            masked(value, legal > 0),
            masked(top, legal * one(spot.up) > 0),
            masked(bot, legal * one(spot.down) > 0),
        )

    def flat_block(ex):
        return ex.block[...].astype(F32).reshape(plan.n, c)

    ex_x.wait()
    values_x = assemble(ex_x, flat_block(ex_x), kept)
    mean_one, scale_one = moments(totals[0].finish())

    def unit_one(v):
        return (v - mean_one) * scale_one

    place_padded(
        plan, pad_one, *clip([silu(unit_one(v) * gain_one + shift_one) for v in values_x])
    )
    convolve_split(plan, pad_one, weight_one, wide_h, interior, False)
    hidden = wide_h[pl.ds(0, plan.n)]
    totals[1].start(column_sum(hidden), column_sum(hidden * hidden))
    ex_h.start(wide_h)

    ex_g.wait()
    place_padded(plan, pad_g, *clip(assemble(ex_g, flat_block(ex_g), kept)))
    convolve_split(plan, pad_g, turned_two, wide_b, interior, True)
    shifted_grad(plan, moved_g, interior(flat_block(ex_g)))
    turned_acted(plan, pad_one, at_one)
    mean_two, scale_two = moments(totals[1].finish())

    def unit_two(v):
        return (v - mean_two) * scale_two

    unit = unit_two(wide_h[pl.ds(0, plan.n)])
    lifted = interior(wide_b[...] * slope(unit * gain_two + shift_two) * gain_two)
    wide_l[pl.ds(0, plan.n)] = lifted
    totals[2].start(column_sum(lifted), column_sum(lifted * unit))
    ex_l.start(wide_l)

    ex_h.wait()
    units = [unit_two(v) for v in assemble(ex_h, wide_h[pl.ds(0, plan.n)], inside)]
    at = 0
    for v in units:
        unit_h[pl.ds(at, v.shape[0])] = v
        at += v.shape[0]
    place_padded(plan, pad_two, *clip([silu(v * gain_two + shift_two) for v in units]))
    turned_acted(plan, pad_two, at_two)
    def starts(parts, p):
        ready = plan.taps_rows if p == 2 else (p + 1) * 9 * c
        before = p * 9 * c
        for part in parts:
            end = min(part.at + part.count, plan.taps_rows)
            if before < end <= ready:
                part.start()

    for p in range(3):
        kernel_grad(plan, at_two, moved_g, acc_two, p)
        starts(sums_two, p)
    turn_weight(plan, weight_one, turned_one)
    for part in sums_two:
        part.first()
    convolve_split(plan, pad_two, weight_two, wide_b, interior, False)
    out_refs[0][0][...] = (flat_block(ex_x) + wide_b[...]).astype(BF16).reshape(
        plan.frames, plan.fn, c
    )
    a_two, b_two = group_means(totals[2].finish())
    ex_l.wait()
    grads, at = [], 0
    for lift in assemble(ex_l, wide_l[pl.ds(0, plan.n)], inside):
        count = lift.shape[0]
        grads.append(scale_two * (lift - a_two - unit_h[pl.ds(at, count)] * b_two))
        at += count
    grads = clip(grads)
    shifted_grad(plan, moved_h, interior(grads[0]))
    for p in range(3):
        kernel_grad(plan, at_one, moved_h, acc_one, p)
        starts(sums_one, p)
    slot = lax.broadcasted_iota(jnp.int32, (plan.h, SLOT, c), 1)

    leave = [
        pltpu.make_async_copy(stage.at[cells], target, local_sem.at[14 + k])
        for k, (stage, target) in enumerate(((stage_x, block_out), (stage_g, grad_input)))
    ]

    def emit(k, stage):
        mine, theirs = out_refs[k]
        outs[k].wait_recv()
        for f in range(plan.f):
            a = mine[plan.f * spot.t + f].astype(F32).reshape(plan.h, SLOT, c)
            b = theirs[f].astype(F32).reshape(plan.h, SLOT, c)
            low = jnp.where(spot.t == 0, a, b)
            high = jnp.where(spot.t == 0, b, a)
            low = jnp.where(slot < plan.half, low, high)
            for y in range(plan.h):
                at = y * plan.w * plan.f + f
                rows32[pl.ds(at, SLOT, plan.f)] = low[y]
                rows32[pl.ds(at + SLOT * plan.f, plan.w - SLOT, plan.f)] = high[y, 0 : plan.w - SLOT]
        for at in range(0, plan.cells, 8):
            n = min(8, plan.cells - at)
            block = rows32[pl.ds(at * plan.f, n * plan.f)]
            stage[pl.ds(at, n)] = block.reshape(n, plan.f, c).astype(BF16)
        leave[k].start()

    def go(which, *steps):
        parts = dict(one=sums_one, two=sums_two)[which]
        for k, step in steps:
            if k < len(parts):
                getattr(parts[k], step)()

    go("one", (0, "first"))
    place_padded(plan, pad_h, *grads)
    convolve_split(plan, pad_h, turned_one, wide_b, interior, True)
    go("one", (1, "first"), (2, "first"))
    unit = unit_one(flat_block(ex_x))
    lifted = interior(wide_b[...] * slope(unit * gain_one + shift_one) * gain_one)
    wide_l[pl.ds(0, plan.n)] = lifted
    totals[3].start(column_sum(lifted), column_sum(lifted * unit))
    go("two", (1, "second"), (0, "second"), (2, "second"))
    outs[0].start()
    go("two", (0, "third"))
    go("one", (0, "second"), (1, "second"))
    go("two", (1, "third"))
    a_one, b_one = group_means(totals[3].finish())
    unit = unit_one(flat_block(ex_x))
    out_refs[1][0][...] = (
        flat_block(ex_g) + scale_one * (wide_l[pl.ds(0, plan.n)] - a_one - unit * b_one)
    ).astype(BF16).reshape(plan.frames, plan.fn, c)
    outs[1].start()
    go("one", (2, "second"))
    go("two", (2, "third"), (0, "fourth"))
    go("one", (0, "third"), (1, "third"))
    go("two", (1, "fourth"))
    go("one", (2, "third"))
    go("two", (2, "fourth"))
    emit(0, stage_x)
    go("one", (0, "fourth"))
    go("two", (0, "fifth"))
    emit(1, stage_g)
    go("one", (1, "fourth"), (2, "fourth"))
    go("two", (1, "fifth"), (2, "fifth"), (0, "sixth"), (1, "sixth"), (2, "sixth"))
    go("one", (0, "fifth"), (1, "fifth"), (2, "fifth"), (0, "sixth"), (1, "sixth"), (2, "sixth"))
    for item in [ex_x, ex_g, ex_h, ex_l] + totals + sums_two + sums_one:
        item.drain()
    for link in outs:
        link.wait_send()
    for copy in leave:
        copy.wait()


def split_kernel(plan, features, cotangent, kernel_one, kernel_two, *norms):
    c, n = plan.c, plan.n
    frames, fn = plan.frames, plan.fn
    vm = pltpu.VMEM
    halos = []
    for k in range(4):
        edge = plan.f * plan.hs if k < 2 else plan.ext
        halos += [
            vm((frames, fn, c), BF16),
            vm((2, edge, c), BF16),
            vm((frames, SLOT, c), BF16),
            vm((frames, SLOT, c), BF16),
            vm((3, 2 * plan.ext, c), BF16),
        ]
    count = plan.ntm * plan.nrow * plan.ncol - 1
    hbm = pl.BlockSpec(memory_space=pltpu.HBM)
    pads = plan.frames * plan.pn + SLOT
    return pl.pallas_call(
        functools.partial(split_body, plan),
        out_shape=(
            jax.ShapeDtypeStruct(features.shape, BF16),
            jax.ShapeDtypeStruct(features.shape, BF16),
            jax.ShapeDtypeStruct((plan.taps_rows, c), BF16),
            jax.ShapeDtypeStruct((plan.taps_rows, c), BF16),
        ),
        in_specs=[hbm] * 8,
        out_specs=(hbm,) * 4,
        scratch_shapes=[vm((plan.f * plan.h * plan.wide + 2 * plan.wide, c), F32)]
        + [vm((plan.cells_up * plan.f, c), F32)]
        + [vm((plan.cells_up, plan.f, c), BF16)] * 2
        + [vm((plan.sum_rows, c), BF16)] * 2
        + [vm((n + SLOT, c), F32)] * 2
        + [vm((n, c), F32)]
        + [vm((n + 2 * frames * SLOT, c), F32)]
        + [vm((n, 2 * plan.ext), BF16)]
        + [vm((frames * SLOT, 2 * plan.ext), BF16)] * 2
        + [vm((9, c, 3 * c), BF16)] * 4
        + [vm((pads, c), BF16)] * 4
        + [vm((3 * c, frames * plan.gn), BF16)] * 2
        + [vm((frames * plan.gn, 3 * c), BF16)] * 2
        + [vm((plan.sum_rows, c), F32)] * 2
        + [vm((1, c), F32)] * 4
        + [vm((2, plan.f, fn, c), BF16)] * 2
        + halos
        + [vm((8, c), F32), vm((count, 8, c), F32)] * 4
        + part_scratch(plan)
        + [vm((frames, fn, c), BF16), vm((plan.f, fn, c), BF16)] * 2
        + [pltpu.SemaphoreType.DMA((MANY,))] * 2
        + [pltpu.SemaphoreType.DMA((32,))],
        compiler_params=pltpu.CompilerParams(
            collective_id=0, has_side_effects=True, vmem_limit_bytes=VMEM_ASK
        ),
    )(features, cotangent, kernel_one, kernel_two, *norms)


def widen_body(parts, *refs):
    ins, outs, narrow, wide, held, sems = refs[:4], refs[4:8], *refs[8:]
    moves = [pltpu.make_async_copy(ins[k], held.at[k], sems.at[0, k]) for k in range(2)]
    leave = [pltpu.make_async_copy(held.at[k], outs[k], sems.at[0, 2 + k]) for k in range(2)]
    loads, stores = [], []
    for a in range(2):
        for j, (at, count) in enumerate(parts):
            rows = pl.ds(at, count)
            k = len(parts) * a + j
            loads.append(
                pltpu.make_async_copy(ins[2 + a].at[rows], narrow.at[a, rows], sems.at[1, k])
            )
            stores.append(
                pltpu.make_async_copy(wide.at[a, rows], outs[2 + a].at[rows], sems.at[2, k])
            )
    for copy in loads[: len(parts)] + moves + loads[len(parts) :]:
        copy.start()
    for a in range(2):
        for j, (at, count) in enumerate(parts):
            k = len(parts) * a + j
            loads[k].wait()
            wide[a, pl.ds(at, count)] = narrow[a, pl.ds(at, count)].astype(F32)
            stores[k].start()
        moves[a].wait()
        leave[a].start()
    for copy in stores + leave:
        copy.wait()


def widen(block_out, grad_input, part_one, part_two):
    rows, c = part_one.shape
    piece = -(-rows // 64) * 16
    parts = [(at, min(piece, rows - at)) for at in range(0, rows, piece)]
    hbm = pl.BlockSpec(memory_space=pltpu.HBM)
    shape = jax.ShapeDtypeStruct
    return pl.pallas_call(
        functools.partial(widen_body, parts),
        out_shape=(
            shape(block_out.shape, BF16),
            shape(grad_input.shape, BF16),
            shape((rows, c), F32),
            shape((rows, c), F32),
        ),
        in_specs=[hbm] * 4,
        out_specs=(hbm,) * 4,
        scratch_shapes=[
            pltpu.VMEM((2, rows, c), BF16),
            pltpu.VMEM((2, rows, c), F32),
            pltpu.VMEM((2,) + block_out.shape, BF16),
            pltpu.SemaphoreType.DMA((3, 2 * len(parts))),
        ],
        compiler_params=pltpu.CompilerParams(vmem_limit_bytes=VMEM_ASK),
    )(block_out, grad_input, part_one, part_two)


def local_split(plan, features, cotangent, conv_one, conv_two, *norms):
    c = plan.c
    norms = [v.reshape(1, c) for v in norms]
    shape = (9, 3, c, c)
    turn = lambda v: v.transpose(1, 2, 0, 3).reshape(plan.cells, plan.f, c)
    back = lambda v: v.reshape(plan.h, plan.w, plan.f, c).transpose(2, 0, 1, 3)
    block_out, grad_input, part_one, part_two = widen(
        *split_kernel(
            plan, turn(features), turn(cotangent), conv_one.reshape(shape), conv_two.reshape(shape), *norms
        )
    )
    return (
        back(block_out),
        back(grad_input),
        part_one.reshape(conv_one.shape),
        part_two.reshape(conv_two.shape),
    )


def local(features, cotangent, conv_one, conv_two, gain_one, shift_one, gain_two, shift_two):
    f, h, w, c = features.shape
    sizes = tuple(lax.axis_size(a) for a in AXES)
    if Split.fits(f, h, w, c, sizes):
        return local_split(
            Split(f, h, w, c, sizes), features, cotangent, conv_one, conv_two,
            gain_one, shift_one, gain_two, shift_two,
        )
    plan = Plan(f, h, w, c, sizes)
    norms = [v.reshape(1, c) for v in (gain_one, shift_one, gain_two, shift_two)]
    block_out, grad_input, part_one, part_two = block_kernel(
        plan, features, cotangent, conv_one.reshape(-1, c), conv_two.reshape(-1, c), *norms
    )
    return (
        block_out,
        grad_input,
        part_one.astype(F32).reshape(conv_one.shape),
        part_two.astype(F32).reshape(conv_two.shape),
    )


def solution(mesh):
    block = P("tm", "row", "col", None)
    return jax.shard_map(
        local,
        mesh=mesh,
        in_specs=(block, block) + (P(),) * 6,
        out_specs=(block, block, P(), P()),
        check_vma=False,
    )
```

```python
import functools

import jax
import jax.numpy as jnp
from jax import lax
from jax.experimental import pallas as pl
from jax.experimental.pallas import tpu as pltpu
from jax.sharding import PartitionSpec as P

GROUPS = 32
EPSILON = 1e-05
MESH = pl.DeviceIdType.MESH
F32 = jnp.float32
BF16 = jnp.bfloat16
AXES = ("tm", "row", "col")


class Plan:
    def __init__(self, f, h, w, c, sizes):
        self.f, self.h, self.w, self.c = f, h, w, c
        self.wp = 16
        while self.wp < w + 2:
            self.wp *= 2
        self.n = f * h * self.wp
        self.hp = h + 2
        self.np = (f + 2) * self.hp * self.wp
        self.cb = -(-(f * h) // 16) * 16
        self.rb = 2 * self.wp
        self.ntm, self.nrow, self.ncol = sizes
        self.na = self.nrow
        self.nb = self.ntm * self.ncol
        self.taps_rows = 27 * c
        unit = 16 * self.ntm * self.nrow * self.ncol
        units = -(-self.taps_rows // unit)
        first = -(-units // 2)
        self.sum_rows = units * unit
        self.parts = [(0, first * unit)]
        if units > first:
            self.parts.append((first * unit, (units - first) * unit))

    def stages(self, order):
        near = 2 if self.ncol % 2 == 0 else 1
        known = dict(
            near=("col", 1, near, True),
            col=("col", near, self.ncol // near, False),
            tm=("tm", 1, self.ntm, False),
            row=("row", 1, self.nrow, False),
        )
        return [known[name] for name in order if known[name][2] > 1]


class Link:
    def __init__(self, src, dst, sems, index, device, sends, receives):
        self.make = lambda: pltpu.make_async_remote_copy(
            src_ref=src,
            dst_ref=dst,
            send_sem=sems[0].at[index],
            recv_sem=sems[1].at[index],
            device_id=device,
            device_id_type=MESH,
        )
        self.sends, self.receives = sends, receives

    def start(self):
        if self.sends is None:
            self.make().start()
            return

        @pl.when(self.sends)
        def _():
            self.make().start()

    def wait_send(self):
        if self.sends is None:
            self.make().wait_send()
            return

        @pl.when(self.sends)
        def _():
            self.make().wait_send()

    def wait_recv(self):
        if self.receives is None:
            self.make().wait_recv()
            return

        @pl.when(self.receives)
        def _():
            self.make().wait_recv()


class Place:
    def __init__(self, plan):
        self.t, self.r, self.c = (lax.axis_index(a) for a in AXES)
        self.has = dict(
            left=self.c > 0,
            right=self.c < plan.ncol - 1,
            up=self.r > 0,
            down=self.r < plan.nrow - 1,
            past=self.t > 0,
            future=self.t < plan.ntm - 1,
        )
        self.dev = dict(
            left={"col": self.c - 1},
            right={"col": self.c + 1},
            up={"row": self.r - 1},
            down={"row": self.r + 1},
            past={"tm": self.t - 1},
            future={"tm": self.t + 1},
        )

    def partners(self, plan):
        rows = [{"row": lax.rem(self.r + d, plan.na)} for d in range(1, plan.na)]
        index = self.t * plan.ncol + self.c
        others = []
        for d in range(1, plan.nb):
            to = lax.rem(index + d, plan.nb)
            others.append({"tm": lax.div(to, plan.ncol), "col": lax.rem(to, plan.ncol)})
        return rows, others


class Reduce:
    def __init__(self, plan, place, refs, sems, base):
        self.own, self.slots_a, self.mid, self.slots_b = refs
        rows, others = place.partners(plan)
        self.a = [
            Link(self.own, self.slots_a.at[d], sems, base + d, dev, None, None)
            for d, dev in enumerate(rows)
        ]
        self.b = [
            Link(self.mid, self.slots_b.at[d], sems, base + len(rows) + d, dev, None, None)
            for d, dev in enumerate(others)
        ]

    def start(self, first, second):
        self.own[...] = jnp.zeros_like(self.own)
        self.own[0:1] = first
        self.own[1:2] = second
        for link in self.a:
            link.start()

    def middle(self):
        for link in self.a:
            link.wait_recv()
        total = self.own[...]
        for d in range(len(self.a)):
            total = total + self.slots_a[d]
        self.mid[...] = total
        for link in self.b:
            link.start()

    def finish(self):
        for link in self.b:
            link.wait_recv()
        total = self.mid[...]
        for d in range(len(self.b)):
            total = total + self.slots_b[d]
        return total

    def drain(self):
        for link in self.a + self.b:
            link.wait_send()


class KernelSum:
    def __init__(self, plan, place, stages, span, acc, done, outs, ins, sems, base):
        self.acc, self.done, self.outs, self.ins = acc, done, outs, ins
        self.stages = stages
        at, count = span
        self.spans, self.reduce, self.gather = [], [], []
        for k, (axis, stride, ways, wide) in enumerate(stages):
            here = dict(tm=place.t, row=place.r, col=place.c)[axis]
            mine = lax.rem(lax.div(here, stride), ways)
            piece = count // ways
            aligned = lambda v: pl.multiple_of(v, 16)
            kept = aligned(at + mine * piece)
            links, sources = [], []
            for d in range(1, ways):
                other = lax.rem(mine + d, ways)
                dev = {axis: here + (other - mine) * stride}
                sent = aligned(at + other * piece)
                if wide:
                    src = acc.at[pl.ds(sent, piece)]
                else:
                    src = outs[k].at[d - 1]
                    sources.append((d - 1, sent))
                links.append((Link(src, ins[k].at[d - 1], sems, base, dev, None, None), dev))
                base += 1
            self.reduce.append([link for link, _ in links])
            gathers = []
            for _, dev in links:
                part = done.at[pl.ds(kept, piece)]
                gathers.append(Link(part, part, sems, base, dev, None, None))
                base += 1
            self.gather.append(gathers)
            self.spans.append((kept, piece, sources))
            at, count = kept, piece
        self.base = base

    def steps(self):
        out = []
        last = len(self.stages) - 1
        for k in range(len(self.stages)):
            out.append(functools.partial(self.reduce_step, k))
        for k in range(last, -1, -1):
            out.append(functools.partial(self.gather_step, k))
        out.append(self.last_step)
        return out

    def reduce_step(self, k):
        if k:
            self.settle(k - 1)
        kept, piece, sources = self.spans[k]
        for slot, sent in sources:
            self.outs[k][slot] = self.acc[pl.ds(sent, piece)].astype(BF16)
        for link in self.reduce[k]:
            link.start()

    def settle(self, k):
        kept, piece, _ = self.spans[k]
        for link in self.reduce[k]:
            link.wait_recv()
        total = self.acc[pl.ds(kept, piece)]
        for d in range(len(self.reduce[k])):
            total = total + self.ins[k][d].astype(F32)
        if k == len(self.stages) - 1:
            self.done[pl.ds(kept, piece)] = total.astype(BF16)
        else:
            self.acc[pl.ds(kept, piece)] = total

    def gather_step(self, k):
        if k == len(self.stages) - 1:
            self.settle(k)
        else:
            for link in self.gather[k + 1]:
                link.wait_recv()
        for link in self.gather[k]:
            link.start()

    def last_step(self):
        for link in self.gather[0]:
            link.wait_recv()

    def drain(self):
        for links in self.reduce + self.gather:
            for link in links:
                link.wait_send()


ORDERS = (("near", "col", "tm", "row"), ("near", "tm", "col", "row"))


def sum_scratch(plan):
    shapes, counts = [], []
    for order, (_, count) in zip(ORDERS, plan.parts):
        outs, ins = [], []
        for axis, stride, ways, wide in plan.stages(order):
            piece = count // ways
            shape = (ways - 1, piece, plan.c)
            outs.append(pltpu.VMEM((1, 16, plan.c) if wide else shape, BF16))
            ins.append(pltpu.VMEM(shape, F32 if wide else BF16))
            count = piece
        counts.append(len(outs))
        shapes += outs + ins
    return shapes, counts


def sum_sems(plan):
    return 2 * sum(
        stage[2] - 1 for order, _ in zip(ORDERS, plan.parts) for stage in plan.stages(order)
    )


EX_SEMS = 10


class Exchange:
    def __init__(self, plan, place, refs, sems, base, directions):
        self.plan, self.place, self.directions = plan, place, directions
        self.own, self.cols_out, self.cols_in, self.rows_out, self.rows_in = refs[:5]
        has, dev = place.has, place.dev
        cb, half = plan.cb, plan.f * plan.wp
        self.cols = [
            Link(self.cols_out.at[pl.ds(0, cb)], self.cols_in.at[pl.ds(0, cb)], sems, base,
                 dev["left"], has["left"], has["right"]),
            Link(self.cols_out.at[pl.ds(cb, cb)], self.cols_in.at[pl.ds(cb, cb)], sems, base + 1,
                 dev["right"], has["right"], has["left"]),
        ]
        self.rows = [
            Link(self.rows_out.at[pl.ds(0, half)], self.rows_in.at[pl.ds(half, half)], sems,
                 base + 2, dev["up"], has["up"], has["down"]),
            Link(self.rows_out.at[pl.ds(half, half)], self.rows_in.at[pl.ds(0, half)], sems,
                 base + 3, dev["down"], has["down"], has["up"]),
        ]
        self.tm = {}
        for k, source in enumerate(directions):
            block, cols, rows = refs[5 + 3 * k : 8 + 3 * k]
            target = "future" if source == "past" else "past"
            links = [
                Link(src, dst, sems, base + 4 + 3 * k + j, dev[target], has[target], has[source])
                for j, (src, dst) in enumerate(
                    [(self.own, block), (self.cols_in, cols), (self.rows_in, rows)]
                )
            ]
            self.tm[source] = ((block, cols, rows), links)

    def clear(self):
        cb, half = self.plan.cb, self.plan.f * self.plan.wp
        has = self.place.has

        def zero(ref, part, cond):
            @pl.when(jnp.logical_not(cond))
            def _():
                ref[part] = jnp.zeros(ref.at[part].shape, ref.dtype)

        zero(self.cols_in, pl.ds(0, cb), has["right"])
        zero(self.cols_in, pl.ds(cb, cb), has["left"])
        zero(self.rows_in, pl.ds(0, half), has["up"])
        zero(self.rows_in, pl.ds(half, half), has["down"])
        for source, (refs, _) in self.tm.items():
            for ref in refs:
                zero(ref, pl.ds(0, ref.shape[0]), has[source])

    def start(self, wide, pick):
        self.own[...] = wide[...].astype(BF16)
        for source in self.directions:
            self.tm[source][1][0].start()
        self.cols_out[...] = jnp.dot(pick[...], self.own[...], preferred_element_type=F32).astype(BF16)
        for link in self.cols:
            link.start()

    def middle(self, wide, spread):
        plan = self.plan
        for link in self.cols:
            link.wait_recv()
        for source in self.directions:
            self.tm[source][1][1].start()
        ends = spread_cols(self.cols_in, spread)
        size = plan.h * plan.wp
        for f in range(plan.f):
            for k, at in enumerate((f * size, (f + 1) * size - plan.wp)):
                self.rows_out[pl.ds((k * plan.f + f) * plan.wp, plan.wp)] = (
                    wide[pl.ds(at, plan.wp)] + ends[at : at + plan.wp]
                ).astype(BF16)
        for link in self.rows:
            link.start()

    def later(self):
        for link in self.rows:
            link.wait_recv()
        for source in self.directions:
            self.tm[source][1][2].start()

    def finish(self):
        for source in self.directions:
            for link in self.tm[source][1]:
                link.wait_recv()

    def drain(self):
        for link in self.cols + self.rows:
            link.wait_send()
        for source in self.directions:
            for link in self.tm[source][1]:
                link.wait_send()

    def pieces(self, wide, spread, source):
        plan = self.plan
        size = plan.h * plan.wp
        (block, cols, rows), _ = self.tm[source]

        def of(value, border, side):
            out = []
            for f in range(plan.f):
                top = border[pl.ds(f * plan.wp, plan.wp)].astype(F32)
                low = border[pl.ds((plan.f + f) * plan.wp, plan.wp)].astype(F32)
                out.append((side, top, value[f * size : (f + 1) * size], low))
            return out

        inner = of(wide[...] + spread_cols(self.cols_in, spread), self.rows_in, None)
        outer = of(block[...].astype(F32) + spread_cols(cols, spread), rows, source)
        if source == "past":
            return outer[plan.f - 2 :] + inner
        return inner + outer[:2]


def spread_cols(cols, spread):
    return jnp.dot(spread[...], cols[...], preferred_element_type=F32)


def silu(v):
    return v / (1.0 + jnp.exp(-v))


def slope(v):
    sigm = 1.0 / (1.0 + jnp.exp(-v))
    return sigm * (1.0 + v * (1.0 - sigm))


def valid(plan, place, count, side, border):
    has = place.has
    w = lax.broadcasted_iota(jnp.int32, (count, plan.c), 0) & (plan.wp - 1)
    one = lambda cond: cond.astype(jnp.int32)
    mask = jnp.where(
        w < plan.w,
        1,
        jnp.where(
            w == plan.w,
            one(has["right"]),
            jnp.where(w == plan.wp - 1, one(has["left"]), 0),
        ),
    )
    for name in (side, border):
        if name is not None:
            mask = mask * one(has[name])
    return mask > 0


def store_shifted(plan, ref, at, value):
    count = value.shape[0]
    rows = value.reshape(count // plan.wp, plan.wp, plan.c)
    before = pltpu.roll(rows, 1, axis=1).reshape(value.shape)
    after = pltpu.roll(rows, plan.wp - 1, axis=1).reshape(value.shape)
    c = plan.c
    ref[pl.ds(at, count), 0:c] = before.astype(BF16)
    ref[pl.ds(at, count), c : 2 * c] = value.astype(BF16)
    ref[pl.ds(at, count), 2 * c : 3 * c] = after.astype(BF16)


def build(plan, ref, frames):
    for k, (top, rows, low) in enumerate(frames):
        at = k * plan.hp * plan.wp
        store_shifted(plan, ref, at, top)
        store_shifted(plan, ref, at + plan.wp, rows)
        store_shifted(plan, ref, at + (plan.h + 1) * plan.wp, low)


def convolve(plan, ref, kernel, out):
    size = plan.h * plan.wp

    def frame(f, carry):
        pieces = []
        for p in range(3):
            for q in range(3):
                at = pl.multiple_of(((f + p) * plan.hp + q) * plan.wp, plan.wp)
                pieces.append(ref[pl.ds(at, size), :])
        wide = jnp.dot(jnp.concatenate(pieces, axis=1), kernel[...], preferred_element_type=F32)
        w = lax.broadcasted_iota(jnp.int32, wide.shape, 0) & (plan.wp - 1)
        out[pl.ds(pl.multiple_of(f * size, size), size), :] = jnp.where(w < plan.w, wide, 0.0)
        return carry

    lax.fori_loop(0, plan.f, frame, 0)


def kernel_term(plan, ref, turned, part, low, high):
    size = plan.h * plan.wp

    def tap(pq, carry):
        p, q = lax.div(pq, 3), lax.rem(pq, 3)
        pieces = []
        for f in range(plan.f):
            at = pl.multiple_of(((f + p) * plan.hp + q) * plan.wp, plan.wp)
            pieces.append(ref[pl.ds(at, size), :])
        term = jnp.dot(turned, jnp.concatenate(pieces, axis=0), preferred_element_type=F32)
        part[pl.ds(pl.multiple_of(pq * 3 * plan.c, 3 * plan.c), 3 * plan.c), :] = term.T
        return carry

    lax.fori_loop(low, high, tap, 0)


def turn_kernel(plan, kernel, out):
    taps, c = 27, plan.c

    def tap(k, carry):
        source = kernel[pl.ds(pl.multiple_of((taps - 1 - k) * c, c), c), :]
        out[pl.ds(pl.multiple_of(k * c, c), c), :] = source.astype(F32).T.astype(BF16)
        return carry

    lax.fori_loop(0, taps, tap, 0)


def spaced(plan, ref, wide):
    wide[...] = jnp.zeros_like(wide)
    for f in range(plan.f):
        for y in range(plan.h):
            wide[pl.ds((f * plan.h + y) * plan.wp, plan.w)] = ref[f, y].astype(F32)


def unspaced(plan, value, ref):
    for f in range(plan.f):
        for y in range(plan.h):
            at = (f * plan.h + y) * plan.wp
            ref[f, y] = value[at : at + plan.w].astype(BF16)


def column_sum(value):
    return jnp.sum(value, axis=0, keepdims=True)


def body(plan, n_ex, *refs):
    refs = list(refs)
    take = lambda k: [refs.pop(0) for _ in range(k)]
    features, cotangent, kernel_one, kernel_two, *norms = take(8)
    block_out, grad_input, part_one, part_two = take(4)
    wide_x, wide_g, wide_h, wide_l, wide_b = take(5)
    pick, spread, turned_one, turned_two = take(4)
    x3_one, x3_two, x3_g, x3_h = take(4)
    exchange_refs = [take(k) for k in n_ex]
    reduce_refs = [take(4) for _ in range(4)]
    acc_one, acc_two, done_one, done_two = take(4)
    sum_refs = []
    for _ in range(2):
        for count in sum_scratch(plan)[1]:
            sum_refs.append((take(count), take(count)))
    sems = take(2)

    place = Place(plan)
    rows, others = place.partners(plan)
    per_reduce = len(rows) + len(others)
    exchanges = [
        Exchange(plan, place, r, sems, EX_SEMS * k, d)
        for k, (r, d) in enumerate(
            zip(exchange_refs, (("past",), ("future",), ("past", "future"), ("future",)))
        )
    ]
    ex_x, ex_g, ex_h, ex_l = exchanges
    reduces = [
        Reduce(plan, place, r, sems, EX_SEMS * 4 + per_reduce * k)
        for k, r in enumerate(reduce_refs)
    ]
    sums = []
    base = EX_SEMS * 4 + per_reduce * 4
    for acc, done in ((acc_two, done_two), (acc_one, done_one)):
        for order, span in zip(ORDERS, plan.parts):
            outs, ins = sum_refs[len(sums)]
            sums.append(
                KernelSum(plan, place, plan.stages(order), span, acc, done, outs, ins, sems, base)
            )
            base = sums[-1].base
        acc[pl.ds(plan.taps_rows, plan.sum_rows - plan.taps_rows)] = jnp.zeros(
            (plan.sum_rows - plan.taps_rows, plan.c), F32
        )
    sums_two, sums_one = sums[: len(plan.parts)], sums[len(plan.parts) :]
    steps_two = [list(group) for group in zip(*[item.steps() for item in sums_two])]

    def advance():
        if steps_two:
            for step in steps_two.pop(0):
                step()

    for ex in exchanges:
        ex.clear()

    barrier = pltpu.get_barrier_semaphore()
    for dev in rows + others:
        pl.semaphore_signal(barrier, inc=1, device_id=dev, device_id_type=MESH)

    c = plan.c
    per_group = c // GROUPS
    members = float(plan.f * plan.h * plan.w * plan.ntm * plan.nrow * plan.ncol * per_group)
    lane_i = lax.broadcasted_iota(jnp.int32, (c, c), 0)
    lane_j = lax.broadcasted_iota(jnp.int32, (c, c), 1)
    same = (lax.div(lane_i, per_group) == lax.div(lane_j, per_group)).astype(F32)

    def group_means(total):
        sums = jnp.dot(
            total, same, preferred_element_type=F32, precision=lax.Precision.HIGHEST
        )
        return sums[0:1] / members, sums[1:2] / members

    def moments(total):
        average, square = group_means(total)
        return average, lax.rsqrt(square - average * average + EPSILON)

    spaced(plan, features, wide_x)
    j = lax.broadcasted_iota(jnp.int32, (2 * plan.cb, plan.n), 0)
    at = lax.broadcasted_iota(jnp.int32, (2 * plan.cb, plan.n), 1)
    first = j < plan.cb
    pick[...] = (
        at == jnp.where(first, j * plan.wp, (j - plan.cb) * plan.wp + plan.w - 1)
    ).astype(F32).astype(BF16)
    at = lax.broadcasted_iota(jnp.int32, (plan.n, 2 * plan.cb), 0)
    j = lax.broadcasted_iota(jnp.int32, (plan.n, 2 * plan.cb), 1)
    first = j < plan.cb
    spread[...] = (
        at == jnp.where(first, j * plan.wp + plan.w, (j - plan.cb) * plan.wp + plan.wp - 1)
    ).astype(F32).astype(BF16)

    pl.semaphore_wait(barrier, per_reduce)
    gain_one, shift_one, gain_two, shift_two = (ref[...] for ref in norms)

    x = wide_x[...]
    reduces[0].start(column_sum(x), column_sum(x * x))
    ex_x.start(wide_x, pick)
    spaced(plan, cotangent, wide_g)
    ex_g.start(wide_g, pick)
    reduces[0].middle()
    ex_x.middle(wide_x, spread)
    ex_g.middle(wide_g, spread)
    turn_kernel(plan, kernel_two, turned_two)
    ex_x.later()
    ex_g.later()
    turn_kernel(plan, kernel_one, turned_one)
    mean_one, scale_one = moments(reduces[0].finish())
    ex_x.finish()

    def unit_one(v):
        return (v - mean_one) * scale_one

    def frames_of(pieces, fn):
        out = []
        for side, top, rows_, low in pieces:
            keep = lambda v, border: jnp.where(
                valid(plan, place, v.shape[0], side, border), fn(v), 0.0
            )
            out.append((keep(top, "up"), keep(rows_, None), keep(low, "down")))
        return out

    build(
        plan,
        x3_one,
        frames_of(
            ex_x.pieces(wide_x, spread, "past"),
            lambda v: silu(unit_one(v) * gain_one + shift_one),
        ),
    )
    convolve(plan, x3_one, kernel_one, wide_h)
    hidden = wide_h[...]
    reduces[1].start(column_sum(hidden), column_sum(hidden * hidden))
    ex_h.start(wide_h, pick)
    reduces[1].middle()
    ex_h.middle(wide_h, spread)
    ex_g.finish()
    build(plan, x3_g, [p[1:] for p in ex_g.pieces(wide_g, spread, "future")])
    ex_h.later()
    convolve(plan, x3_g, turned_two, wide_b)
    mean_two, scale_two = moments(reduces[1].finish())

    def unit_two(v):
        return (v - mean_two) * scale_two

    unit = unit_two(wide_h[...])
    lifted = wide_b[...] * slope(unit * gain_two + shift_two) * gain_two
    wide_l[...] = lifted
    reduces[2].start(column_sum(lifted), column_sum(lifted * unit))
    ex_l.start(wide_l, pick)
    reduces[2].middle()
    ex_l.middle(wide_l, spread)
    ex_h.finish()
    build(
        plan,
        x3_two,
        frames_of(
            ex_h.pieces(wide_h, spread, "past"),
            lambda v: silu(unit_two(v) * gain_two + shift_two),
        ),
    )
    ex_l.later()
    kernel_term(plan, x3_two, wide_g[...].T.astype(BF16), acc_two, 0, 9)
    a_two, b_two = group_means(reduces[2].finish())
    advance()
    ex_l.finish()
    frames = []
    for (side, *lifts), (_, *hids) in zip(
        ex_l.pieces(wide_l, spread, "future"), ex_h.pieces(wide_h, spread, "future")
    ):
        out = []
        for border, lift, hid in zip(("up", None, "down"), lifts, hids):
            value = scale_two * (lift - a_two - unit_two(hid) * b_two)
            out.append(jnp.where(valid(plan, place, lift.shape[0], side, border), value, 0.0))
        frames.append(tuple(out))
    build(plan, x3_h, frames)
    advance()
    w = lax.broadcasted_iota(jnp.int32, (plan.h * plan.wp, c), 0) & (plan.wp - 1)
    own = jnp.concatenate(
        [jnp.where(w < plan.w, frames[f][1], 0.0) for f in range(plan.f)], axis=0
    )
    turned = own.T.astype(BF16)
    ready = min(9, -(-plan.parts[0][1] // (3 * c)))
    kernel_term(plan, x3_one, turned, acc_one, 0, ready)
    steps_one = [item.steps() for item in sums_one]
    steps_one[0].pop(0)()
    advance()
    kernel_term(plan, x3_one, turned, acc_one, ready, 9)
    for steps in steps_one[1:]:
        steps.pop(0)()

    def advance_one():
        for steps in steps_one:
            steps.pop(0)()

    convolve(plan, x3_h, turned_one, wide_b)
    unit = unit_one(wide_x[...])
    lifted = wide_b[...] * slope(unit * gain_one + shift_one) * gain_one
    reduces[3].start(column_sum(lifted), column_sum(lifted * unit))
    wide_l[...] = lifted
    advance_one()
    advance()
    reduces[3].middle()
    convolve(plan, x3_two, kernel_two, wide_b)
    advance_one()
    advance()
    unspaced(plan, wide_x[...] + wide_b[...], block_out)
    a_one, b_one = group_means(reduces[3].finish())
    advance_one()
    advance()
    unit = unit_one(wide_x[...])
    unspaced(
        plan,
        wide_g[...] + scale_one * (wide_l[...] - a_one - unit * b_one),
        grad_input,
    )
    while steps_one[0]:
        advance_one()
        advance()
    part_two[...] = done_two[pl.ds(0, plan.taps_rows)]
    part_one[...] = done_one[pl.ds(0, plan.taps_rows)]
    for item in exchanges + reduces + sums:
        item.drain()


def block_kernel(plan, features, cotangent, kernel_one, kernel_two, *norms):
    c, n = plan.c, plan.n
    half = plan.f * plan.wp
    exchange = []
    n_ex = []
    for count in (1, 1, 2, 1):
        shapes = [(n, c), (2 * plan.cb, c), (2 * plan.cb, c), (2 * half, c), (2 * half, c)]
        shapes += [(n, c), (2 * plan.cb, c), (2 * half, c)] * count
        n_ex.append(len(shapes))
        exchange += [pltpu.VMEM(s, BF16) for s in shapes]
    reduce = [
        pltpu.VMEM((8, c), F32),
        pltpu.VMEM((max(1, plan.na - 1), 8, c), F32),
        pltpu.VMEM((8, c), F32),
        pltpu.VMEM((max(1, plan.nb - 1), 8, c), F32),
    ] * 4
    sems = 4 * EX_SEMS + 4 * (plan.na + plan.nb - 2) + 2 * sum_sems(plan)
    vmem = pl.BlockSpec(memory_space=pltpu.VMEM)
    taps = kernel_one.shape[0]
    return pl.pallas_call(
        functools.partial(body, plan, n_ex),
        out_shape=(
            jax.ShapeDtypeStruct(features.shape, BF16),
            jax.ShapeDtypeStruct(features.shape, BF16),
            jax.ShapeDtypeStruct((taps, c), BF16),
            jax.ShapeDtypeStruct((taps, c), BF16),
        ),
        in_specs=[vmem] * 8,
        out_specs=(vmem,) * 4,
        scratch_shapes=[pltpu.VMEM((n, c), F32)] * 5
        + [pltpu.VMEM((2 * plan.cb, n), BF16), pltpu.VMEM((n, 2 * plan.cb), BF16)]
        + [pltpu.VMEM((taps, c), BF16)] * 2
        + [pltpu.VMEM((plan.np, 3 * c), BF16)] * 4
        + exchange
        + reduce
        + [pltpu.VMEM((plan.sum_rows, c), F32)] * 2
        + [pltpu.VMEM((plan.sum_rows, c), BF16)] * 2
        + sum_scratch(plan)[0] * 2
        + [pltpu.SemaphoreType.DMA((sems,))] * 2,
        compiler_params=pltpu.CompilerParams(
            collective_id=0, has_side_effects=True, vmem_limit_bytes=52 * 2**20
        ),
    )(features, cotangent, kernel_one, kernel_two, *norms)


SLOT = 16
MANY = 256
SHARES = (((3, True), (2, True), (2, True)), ((2, False), (3, True), (2, True)))
VMEM_ASK = 60 * 2**20


class Split:
    def __init__(self, f, h, w, c, sizes):
        self.f, self.h, self.w, self.c = f, h, w, c
        self.ntm, self.nrow, self.ncol = sizes
        self.frames = f * self.ntm
        self.half = w // 2
        self.fn = h * SLOT
        self.pn = (h + 2) * SLOT
        self.n = self.frames * self.fn
        self.hs = -(-h // 16) * 16
        self.ext = self.frames * self.hs
        self.wide = 2 * SLOT
        self.gn = -(-self.fn // 128) * 128
        self.taps_rows = 27 * c
        self.nxy = self.ntm * (self.ncol // 2)
        unit = 32 * self.nxy * self.nrow
        units = -(-self.taps_rows // unit)
        self.sum_rows = units * unit
        self.parts = [self.cut(units, unit, shares) for shares in SHARES]
        self.cells = h * w
        self.cells_up = -(-self.cells // 8) * 8

    @staticmethod
    def cut(units, unit, shares):
        whole = sum(share for share, _ in shares)
        parts, at, taken = [], 0, 0
        for share, plane_first in shares:
            taken += share
            end = units * taken // whole
            if end > at:
                parts.append((at * unit, (end - at) * unit, plane_first))
            at = end
        return parts

    @staticmethod
    def fits(f, h, w, c, sizes):
        ntm, nrow, ncol = sizes
        return (
            ntm == 2
            and ncol % 2 == 0
            and w % 2 == 0
            and SLOT < w <= 2 * SLOT
            and w // 2 + 2 <= SLOT
            and w - SLOT <= w // 2 - 1
            and h <= 16
            and f * ntm * 16 <= 64
            and f * ntm >= 3
        )


class Spot:
    def __init__(self, plan):
        self.t, self.r, self.c = (lax.axis_index(a) for a in AXES)
        self.k = 2 * self.c + self.t
        self.left = self.k > 0
        self.right = self.k < 2 * plan.ncol - 1
        self.up = self.r > 0
        self.down = self.r < plan.nrow - 1
        self.core = lax.rem(self.c, 2)
        self.y = lax.div(self.c, 2)

    def peers(self, plan):
        offsets = [
            (dt, dr, dc)
            for dt in range(plan.ntm)
            for dr in range(plan.nrow)
            for dc in range(plan.ncol)
            if (dt, dr, dc) != (0, 0, 0)
        ]
        offsets.sort(key=lambda o: -(2 * (o[1] > 0) + o[0] + min(1, o[2])))
        out = []
        for dt, dr, dc in offsets:
            out.append(
                {
                    "tm": lax.rem(self.t + dt, plan.ntm),
                    "row": lax.rem(self.r + dr, plan.nrow),
                    "col": lax.rem(self.c + dc, plan.ncol),
                }
            )
        return out

    def plane(self, plan):
        me = self.t * (plan.ncol // 2) + self.y
        out = []
        for d in range(1, plan.nxy):
            o = lax.rem(me + d, plan.nxy)
            dev = {
                "tm": lax.div(o, plan.ncol // 2),
                "col": 2 * lax.rem(o, plan.ncol // 2) + self.core,
            }
            out.append((o, dev))
        return me, out

    def line(self, plan):
        out = []
        for d in range(1, plan.nrow):
            o = lax.rem(self.r + d, plan.nrow)
            out.append((o, {"row": o}))
        return self.r, out


class Counter:
    def __init__(self):
        self.at = 0

    def take(self):
        self.at += 1
        return self.at - 1


class Total:
    def __init__(self, peers, own, slots, sems, counter):
        self.own, self.slots, self.peers, self.sems = own, slots, peers, sems
        self.index = counter.take()

    def start(self, first, second):
        self.own[0:1] = first
        self.own[1:2] = second
        for d, dev in enumerate(self.peers):
            pltpu.make_async_remote_copy(
                src_ref=self.own.at[pl.ds(0, 2)],
                dst_ref=self.slots.at[d, pl.ds(0, 2)],
                send_sem=self.sems[0].at[self.index],
                recv_sem=self.sems[1].at[self.index],
                device_id=dev,
                device_id_type=MESH,
            ).start()

    def whole(self, k):
        part = self.slots.at[pl.ds(0, len(self.peers)), pl.ds(0, 2)]
        return pltpu.make_async_copy(part, part, self.sems[k].at[self.index])

    def finish(self):
        self.whole(1).wait()
        total = self.own[0:2]
        for d in range(len(self.peers)):
            total = total + self.slots[d, 0:2]
        return total

    def drain(self):
        self.whole(0).wait()


class Halo:
    def __init__(self, plan, spot, refs, sems, counter):
        self.plan, self.spot = plan, spot
        self.block, self.edge, self.top, self.bot, self.ch = refs
        self.sems, self.counter = sems, counter
        self.links = []

    def link(self, src, dst, dev, sends, receives):
        item = Link(src, dst, self.sems, self.counter.take(), dev, sends, receives)
        self.links.append(item)
        return item

    def rows(self):
        s = self.spot
        return ((1, s.r + 1, s.down, s.up), (2, s.r - 1, s.up, s.down))

    def lines(self):
        s = self.spot
        return ((0, None, None, None),) + self.rows()

    def clear(self):
        for ref in (self.top, self.bot, self.ch):
            ref[...] = jnp.zeros(ref.shape, BF16)

    def wait(self):
        for link in self.links:
            link.wait_recv()

    def drain(self):
        for link in self.links:
            link.wait_send()


def both(*conds):
    out = None
    for cond in conds:
        if cond is not None:
            out = cond if out is None else jnp.logical_and(out, cond)
    return out


class Reshard(Halo):
    def __init__(self, plan, spot, pair, refs, sems, counter):
        super().__init__(plan, spot, refs, sems, counter)
        self.pair = pair
        t, r, c, f = spot.t, spot.r, spot.c, plan.f
        n = plan.ncol
        self.link(pair.at[1 - t], self.block.at[pl.ds(f * t, f)], {"tm": 1 - t}, None, None)
        for which, row, sends, receives in self.rows():
            src_at = plan.fn - SLOT if which == 1 else 0
            dst = (self.top if which == 1 else self.bot).at[pl.ds(f * t, f)]
            for d in range(2):
                to = t if d == 0 else 1 - t
                self.link(pair.at[to, :, pl.ds(src_at, SLOT)], dst, {"tm": to, "row": row}, sends, receives)
        rows = f * plan.hs
        for which, row, sends, receives in self.lines():
            for d in range(2):
                dev = {"tm": t - d, "col": c + 1}
                if row is not None:
                    dev["row"] = row
                self.link(
                    self.edge.at[1], self.ch.at[which, pl.ds(rows * d, rows)], dev,
                    both(t == d, c < n - 1, sends), both(t == 0, c > 0, receives),
                )
                dev = {"tm": t - d + 1, "col": c - 1}
                if row is not None:
                    dev["row"] = row
                self.link(
                    self.edge.at[0], self.ch.at[which, pl.ds(plan.ext + rows * d, rows)], dev,
                    both(t == d, c > 0, sends), both(t == 1, c < n - 1, receives),
                )

    def start(self, stage, rows, w32):
        plan, t = self.plan, self.spot.t
        step = 8 * plan.f
        for k in range(plan.cells_up // 8):
            rows[pl.ds(step * k, step)] = stage[pl.ds(8 * k, 8)].astype(F32).reshape(step, plan.c)
        for f in range(plan.f):
            for y in range(plan.h):
                w32[pl.ds((f * plan.h + y) * plan.wide, plan.w)] = rows[
                    pl.ds(y * plan.w * plan.f + f, plan.w, plan.f)
                ]
        slot = lax.broadcasted_iota(jnp.int32, (plan.h, SLOT, plan.c), 1)
        for f in range(plan.f):
            v = w32[pl.ds(f * plan.h * plan.wide, plan.h * plan.wide)]
            v = v.reshape(plan.h, plan.wide, plan.c)
            low, high = v[:, :SLOT], v[:, SLOT:]
            second = jnp.where(slot >= plan.half - 1, low, high)
            self.pair[0, f] = low.reshape(plan.fn, plan.c).astype(BF16)
            self.pair[1, f] = second.reshape(plan.fn, plan.c).astype(BF16)
            for side, x in ((0, 0), (1, plan.w - 1)):
                at = f * plan.h * plan.wide + x
                self.edge[side, pl.ds(f * plan.hs, plan.hs)] = w32[
                    pl.ds(at, plan.hs, plan.wide)
                ].astype(BF16)

    def send(self):
        self.links[0].start()

    def send_rest(self):
        for link in self.links[1:]:
            link.start()

    def keep(self):
        self.block[pl.ds(self.plan.f * self.spot.t, self.plan.f)] = self.pair[self.spot.t]


class Border(Halo):
    def __init__(self, plan, spot, refs, sems, counter):
        super().__init__(plan, spot, refs, sems, counter)
        t, c = spot.t, spot.c
        for which, row, sends, receives in self.rows():
            at = plan.fn - SLOT if which == 1 else 0
            dst = self.top if which == 1 else self.bot
            self.link(self.block.at[:, pl.ds(at, SLOT)], dst, {"row": row}, sends, receives)
        for which, row, sends, receives in self.lines():
            dev = {"tm": 1 - t, "col": c - 1 + t}
            if row is not None:
                dev["row"] = row
            self.link(
                self.edge.at[0], self.ch.at[which, pl.ds(plan.ext, plan.ext)], dev,
                both(spot.left, sends), both(spot.right, receives),
            )
            dev = {"tm": 1 - t, "col": c + t}
            if row is not None:
                dev["row"] = row
            self.link(
                self.edge.at[1], self.ch.at[which, pl.ds(0, plan.ext)], dev,
                both(spot.right, sends), both(spot.left, receives),
            )

    def start(self, wide):
        plan, t = self.plan, self.spot.t
        for f in range(plan.frames):
            self.block[f] = wide[pl.ds(f * plan.fn, plan.fn)].astype(BF16)
            for side, offset in ((0, 0), (1, plan.half - 1)):
                values = [
                    wide[pl.ds(f * plan.fn + (plan.half * k + offset) % SLOT, plan.hs, SLOT)]
                    for k in range(2)
                ]
                self.edge[side, pl.ds(f * plan.hs, plan.hs)] = jnp.where(
                    t == 0, values[0], values[1]
                ).astype(BF16)
        for link in self.links:
            link.start()


class Part:
    def __init__(self, plan, spot, span, acc, done, out, refs, sems, counter, local_sem):
        self.acc, self.done = acc, done
        self.core_in, out1, self.in1, out2, self.in2 = refs
        self.at, self.count, plane_first = span
        rows = pl.ds(self.at, min(self.count, plan.taps_rows - self.at))
        self.out = pltpu.make_async_copy(done.at[rows], out.at[rows], local_sem)
        link = lambda src, dst, dev: Link(src, dst, sems, counter.take(), dev, None, None)
        aligned = lambda v: pl.multiple_of(v, 16)
        half = self.count // 2
        base = aligned(self.at + spot.core * half)
        other = aligned(self.at + (1 - spot.core) * half)
        sibling = {"col": spot.c + 1 - 2 * spot.core}
        self.core = link(acc.at[pl.ds(other, half)], self.core_in, sibling)
        stages = (spot.plane(plan), spot.line(plan))
        if not plane_first:
            stages = stages[::-1]
        (one, ones), (two, twos) = stages
        self.big = big = half // (len(ones) + 1)
        self.small = small = big // (len(twos) + 1)
        self.own1_in = aligned(one * big)
        self.own1 = own1 = aligned(base + one * big)
        self.own2 = own2 = aligned(own1 + two * small)
        self.send1 = [
            (aligned(base + o * big), aligned(o * big), out1.at[d], link(out1.at[d], self.in1.at[d], dev))
            for d, (o, dev) in enumerate(ones)
        ]
        self.send2 = [
            (aligned(own1 + o * small), out2.at[d], link(out2.at[d], self.in2.at[d], dev))
            for d, (o, dev) in enumerate(twos)
        ]
        piece2 = done.at[pl.ds(own2, small)]
        self.gather2 = [link(piece2, piece2, dev) for _, dev in twos]
        piece1 = done.at[pl.ds(own1, big)]
        self.gather1 = [link(piece1, piece1, dev) for _, dev in ones]
        self.forward = [link(piece1, piece1, sibling)]
        for d in range(len(ones)):
            o, _ = ones[len(ones) - 1 - d]
            ref = done.at[pl.ds(aligned(base + o * big), big)]
            self.forward.append(link(ref, ref, sibling))

    def start(self):
        self.core.start()

    def first(self):
        self.core.wait_recv()
        for at, inside, out, link in self.send1:
            out[...] = (
                self.acc[pl.ds(at, self.big)] + self.core_in[pl.ds(inside, self.big)]
            ).astype(BF16)
            link.start()

    def second(self):
        big, own1 = self.big, self.own1
        total = self.acc[pl.ds(own1, big)] + self.core_in[pl.ds(self.own1_in, big)]
        for d, item in enumerate(self.send1):
            item[-1].wait_recv()
            total = total + self.in1[d].astype(F32)
        self.acc[pl.ds(own1, big)] = total
        for at, out, link in self.send2:
            out[...] = self.acc[pl.ds(at, self.small)].astype(BF16)
            link.start()

    def third(self):
        total = self.acc[pl.ds(self.own2, self.small)]
        for d, item in enumerate(self.send2):
            item[-1].wait_recv()
            total = total + self.in2[d].astype(F32)
        self.done[pl.ds(self.own2, self.small)] = total.astype(BF16)
        for link in self.gather2:
            link.start()

    def fourth(self):
        for link in self.gather2:
            link.wait_recv()
        for link in self.gather1:
            link.start()
        self.forward[0].start()

    def fifth(self):
        for d, link in enumerate(self.gather1):
            link.wait_recv()
            self.forward[1 + d].start()

    def sixth(self):
        for link in self.forward:
            link.wait_recv()
        self.out.start()

    def drain(self):
        self.core.wait_send()
        for item in self.send1 + self.send2:
            item[-1].wait_send()
        for link in self.gather2 + self.gather1 + self.forward:
            link.wait_send()
        self.out.wait()


def part_scratch(plan):
    shapes = []
    for _, count, plane_first in plan.parts[0] + plan.parts[1]:
        ways = (plan.nxy, plan.nrow) if plane_first else (plan.nrow, plan.nxy)
        big = count // 2 // ways[0]
        small = big // ways[1]
        shapes.append(pltpu.VMEM((count // 2, plan.c), F32))
        for rows, k in ((big, ways[0]), (big, ways[0]), (small, ways[1]), (small, ways[1])):
            shapes.append(pltpu.VMEM((max(1, k - 1), rows, plan.c), BF16))
    return shapes


def around(value, by):
    rows = value.reshape(value.shape[0] // SLOT, SLOT, value.shape[1])
    return pltpu.roll(rows, by, axis=1).reshape(value.shape)


def convolve_split(plan, padded, weight, out, keep, future):
    c = plan.c
    for t in range(plan.frames):
        pieces, used = [], []
        for p in range(3):
            source = t + p if future else t + p - 2
            if not 0 <= source < plan.frames:
                continue
            used.append(p)
            for q in range(3):
                pieces.append(padded[pl.ds(source * plan.pn + q * SLOT, plan.fn), :])
        lhs = jnp.concatenate(pieces, axis=1)
        rhs = weight[3 * used[0] : 3 * used[-1] + 3].reshape(3 * len(used) * c, 3 * c)
        wide = jnp.dot(lhs, rhs, preferred_element_type=F32)
        total = around(wide[:, 0:c], 1) + wide[:, c : 2 * c] + around(wide[:, 2 * c :], SLOT - 1)
        out[pl.ds(t * plan.fn, plan.fn), :] = keep(total)


def place_padded(plan, ref, value, top, bot):
    for t in range(plan.frames):
        at = t * plan.pn
        ref[pl.ds(at, SLOT), :] = top[t * SLOT : (t + 1) * SLOT].astype(BF16)
        ref[pl.ds(at + SLOT, plan.fn), :] = value[t * plan.fn : (t + 1) * plan.fn].astype(BF16)
        ref[pl.ds(at + SLOT + plan.fn, SLOT), :] = bot[t * SLOT : (t + 1) * SLOT].astype(BF16)


def shifted_grad(plan, ref, value):
    c = plan.c
    for s, moved in enumerate((around(value, SLOT - 1), value, around(value, 1))):
        for t in range(plan.frames):
            ref[pl.ds(t * plan.gn, plan.fn), s * c : (s + 1) * c] = moved[
                t * plan.fn : (t + 1) * plan.fn
            ].astype(BF16)


def turned_acted(plan, padded, ref):
    c = plan.c
    for q in range(3):
        for t in range(plan.frames):
            slab = padded[pl.ds(t * plan.pn + q * SLOT, plan.gn), :]
            ref[q * c : (q + 1) * c, t * plan.gn : (t + 1) * plan.gn] = slab.T


def kernel_grad(plan, turned, moved, acc, p):
    c = plan.c
    lag = 2 - p
    count = (plan.frames - lag) * plan.gn
    term = jnp.dot(
        turned[:, 0:count], moved[pl.ds(lag * plan.gn, count), :], preferred_element_type=F32
    )
    for q in range(3):
        for s in range(3):
            acc[pl.ds((9 * p + 3 * q + s) * c, c), :] = term[
                q * c : (q + 1) * c, s * c : (s + 1) * c
            ]


def turn_weight(plan, weight, out):
    c = plan.c
    for k in range(27):
        j = 26 - k
        source = weight[j // 3, :, (j % 3) * c : (j % 3 + 1) * c]
        out[k // 3, :, (k % 3) * c : (k % 3 + 1) * c] = source.T


def split_body(plan, *refs):
    refs = list(refs)
    take = lambda k: [refs.pop(0) for _ in range(k)]
    features, cotangent, conv_one, conv_two, *norms = take(8)
    block_out, grad_input, part_one, part_two = take(4)
    w32, rows32, stage_x, stage_g = take(4)
    done_one, done_two = take(2)
    wide_h, wide_l, wide_b, unit_h = take(4)
    spread_mid, spread_top, spread_bot = take(3)
    weight_one, weight_two, turned_one, turned_two = take(4)
    pad_one, pad_two, pad_g, pad_h = take(4)
    at_one, at_two, moved_g, moved_h = take(4)
    acc_one, acc_two = take(2)
    norm_in = take(4)
    pair_x, pair_g = take(2)
    halo_refs = [take(5) for _ in range(4)]
    total_refs = [take(2) for _ in range(4)]
    sum_refs = [[take(5) for _ in parts] for parts in plan.parts]
    out_refs = [take(2) for _ in range(2)]
    sems = take(2)
    (local_sem,) = take(1)

    spot = Spot(plan)
    peers = spot.peers(plan)
    counter = Counter()
    c = plan.c

    loads = []
    cells = pl.ds(0, plan.cells)
    for k, (src, dst) in enumerate(
        [(features, stage_x.at[cells]), (cotangent, stage_g.at[cells])]
        + list(zip(norms, norm_in))
        + [(conv_one.at[:, s], weight_one.at[:, :, pl.ds(s * c, c)]) for s in range(3)]
        + [(conv_two.at[:, s], weight_two.at[:, :, pl.ds(s * c, c)]) for s in range(3)]
    ):
        loads.append(pltpu.make_async_copy(src, dst, local_sem.at[k]))
    for copy in loads[:2]:
        copy.start()

    ex_x = Reshard(plan, spot, pair_x, halo_refs[0], sems, counter)
    ex_g = Reshard(plan, spot, pair_g, halo_refs[1], sems, counter)
    ex_h = Border(plan, spot, halo_refs[2], sems, counter)
    ex_l = Border(plan, spot, halo_refs[3], sems, counter)
    totals = [Total(peers, *r, sems, counter) for r in total_refs]
    sums_two, sums_one = (
        [
            Part(plan, spot, span, acc, done, out, r, sems, counter, local_sem.at[first + k])
            for k, (span, r) in enumerate(zip(parts, group))
        ]
        for acc, done, out, parts, group, first in (
            (acc_two, done_two, part_two, plan.parts[0], sum_refs[0], 16),
            (acc_one, done_one, part_one, plan.parts[1], sum_refs[1], 16 + len(plan.parts[0])),
        )
    )
    outs = []
    for (mine, theirs) in out_refs:
        outs.append(
            Link(
                mine.at[pl.ds(plan.f * (1 - spot.t), plan.f)], theirs, sems, counter.take(),
                {"tm": 1 - spot.t}, None, None,
            )
        )
    assert counter.at <= MANY

    for ex in (ex_x, ex_g, ex_h, ex_l):
        ex.clear()
    barrier = pltpu.get_barrier_semaphore()
    for dev in peers:
        pl.semaphore_signal(barrier, inc=1, device_id=dev, device_id_type=MESH)
    for copy in loads[2:]:
        copy.start()

    per_group = c // GROUPS
    members = float(plan.n // SLOT * plan.half * 2 * plan.nrow * plan.ncol * per_group)
    lane_i = lax.broadcasted_iota(jnp.int32, (c, c), 0)
    lane_j = lax.broadcasted_iota(jnp.int32, (c, c), 1)
    same = (lax.div(lane_i, per_group) == lax.div(lane_j, per_group)).astype(F32)

    def group_means(total):
        sums = jnp.dot(total, same, preferred_element_type=F32, precision=lax.Precision.HIGHEST)
        return sums[0:1] / members, sums[1:2] / members

    def moments(total):
        average, square = group_means(total)
        return average, lax.rsqrt(square - average * average + EPSILON)

    w32[...] = jnp.zeros(w32.shape, F32)
    for stage in (stage_x, stage_g):
        spare = plan.cells_up - plan.cells
        if spare:
            stage[pl.ds(plan.cells, spare)] = jnp.zeros((spare, plan.f, c), BF16)
    loads[0].wait()
    ex_x.start(stage_x, rows32, w32)
    x = w32[...]
    first, second = column_sum(x), column_sum(x * x)
    pl.semaphore_wait(barrier, len(peers))
    totals[0].start(first, second)
    ex_x.send()
    ex_x.send_rest()
    loads[1].wait()
    ex_g.start(stage_g, rows32, w32)
    ex_g.send()
    ex_g.send_rest()
    ex_x.keep()
    ex_g.keep()

    rel = (lax.broadcasted_iota(jnp.int32, (SLOT, c), 0) - plan.half * spot.t) & (SLOT - 1)
    one = lambda cond: cond.astype(jnp.int32)
    inside = rel < plan.half
    inner = jnp.where(spot.t == 0, plan.half, SLOT - 1)
    kept = jnp.logical_or(inside, rel == inner)
    legal = jnp.where(
        inside, 1, jnp.where(rel == plan.half, one(spot.right), jnp.where(rel == SLOT - 1, one(spot.left), 0))
    )

    def masked(value, mask):
        rows = value.reshape(value.shape[0] // SLOT, SLOT, c)
        return jnp.where(mask[None], rows, 0.0).reshape(value.shape)

    interior = lambda value: masked(value, inside)

    def targets(rows, source):
        i = lax.broadcasted_iota(jnp.int32, (rows, 2 * plan.ext), 0)
        j = lax.broadcasted_iota(jnp.int32, (rows, 2 * plan.ext), 1)
        where = ((i & (SLOT - 1)) - plan.half * spot.t) & (SLOT - 1)
        code = source(i >> 4)
        aim = jnp.where(where == SLOT - 1, code, jnp.where(where == plan.half, code + plan.ext, -1))
        return (j == aim).astype(F32).astype(BF16)

    def of_group(g):
        t = 0
        for k in range(1, plan.frames):
            t = t + (g >= k * plan.h).astype(jnp.int32)
        return g + t * (plan.hs - plan.h)

    spread_mid[...] = targets(plan.n, of_group)
    spread_top[...] = targets(plan.frames * SLOT, lambda t: t * plan.hs + plan.h - 1)
    spread_bot[...] = targets(plan.frames * SLOT, lambda t: t * plan.hs)
    for ref in (pad_one, pad_two):
        ref[pl.ds(plan.frames * plan.pn, SLOT), :] = jnp.zeros((SLOT, c), BF16)
    if plan.gn > plan.fn:
        for ref in (moved_g, moved_h):
            for t in range(plan.frames):
                ref[pl.ds(t * plan.gn + plan.fn, plan.gn - plan.fn), :] = jnp.zeros(
                    (plan.gn - plan.fn, 3 * c), BF16
                )
    for ref in (wide_h, wide_l):
        ref[pl.ds(plan.n, SLOT), :] = jnp.zeros((SLOT, c), F32)
    for acc in (acc_one, acc_two):
        acc[pl.ds(plan.taps_rows, plan.sum_rows - plan.taps_rows)] = jnp.zeros(
            (plan.sum_rows - plan.taps_rows, c), F32
        )
    for copy in loads[2:]:
        copy.wait()
    gain_one, shift_one, gain_two, shift_two = (ref[...] for ref in norm_in)
    turn_weight(plan, weight_two, turned_two)

    def assemble(ex, value, mask):
        flat = lambda ref: ref[...].astype(F32).reshape(plan.frames * SLOT, c)
        spread = lambda by, k: jnp.dot(by[...], ex.ch[k], preferred_element_type=F32)
        return (
            masked(value, mask) + spread(spread_mid, 0),
            masked(flat(ex.top), mask) + spread(spread_top, 1),
            masked(flat(ex.bot), mask) + spread(spread_bot, 2),
        )

    def clip(values):
        value, top, bot = values
        return (
            masked(value, legal > 0),
            masked(top, legal * one(spot.up) > 0),
            masked(bot, legal * one(spot.down) > 0),
        )

    def flat_block(ex):
        return ex.block[...].astype(F32).reshape(plan.n, c)

    ex_x.wait()
    values_x = assemble(ex_x, flat_block(ex_x), kept)
    mean_one, scale_one = moments(totals[0].finish())

    def unit_one(v):
        return (v - mean_one) * scale_one

    place_padded(
        plan, pad_one, *clip([silu(unit_one(v) * gain_one + shift_one) for v in values_x])
    )
    convolve_split(plan, pad_one, weight_one, wide_h, interior, False)
    hidden = wide_h[pl.ds(0, plan.n)]
    totals[1].start(column_sum(hidden), column_sum(hidden * hidden))
    ex_h.start(wide_h)

    ex_g.wait()
    place_padded(plan, pad_g, *clip(assemble(ex_g, flat_block(ex_g), kept)))
    convolve_split(plan, pad_g, turned_two, wide_b, interior, True)
    shifted_grad(plan, moved_g, interior(flat_block(ex_g)))
    turned_acted(plan, pad_one, at_one)
    mean_two, scale_two = moments(totals[1].finish())

    def unit_two(v):
        return (v - mean_two) * scale_two

    unit = unit_two(wide_h[pl.ds(0, plan.n)])
    lifted = interior(wide_b[...] * slope(unit * gain_two + shift_two) * gain_two)
    wide_l[pl.ds(0, plan.n)] = lifted
    totals[2].start(column_sum(lifted), column_sum(lifted * unit))
    ex_l.start(wide_l)

    ex_h.wait()
    units = [unit_two(v) for v in assemble(ex_h, wide_h[pl.ds(0, plan.n)], inside)]
    at = 0
    for v in units:
        unit_h[pl.ds(at, v.shape[0])] = v
        at += v.shape[0]
    place_padded(plan, pad_two, *clip([silu(v * gain_two + shift_two) for v in units]))
    turned_acted(plan, pad_two, at_two)
    def starts(parts, p):
        ready = plan.taps_rows if p == 2 else (p + 1) * 9 * c
        before = p * 9 * c
        for part in parts:
            end = min(part.at + part.count, plan.taps_rows)
            if before < end <= ready:
                part.start()

    for p in range(3):
        kernel_grad(plan, at_two, moved_g, acc_two, p)
        starts(sums_two, p)
    turn_weight(plan, weight_one, turned_one)
    for part in sums_two:
        part.first()
    convolve_split(plan, pad_two, weight_two, wide_b, interior, False)
    out_refs[0][0][...] = (flat_block(ex_x) + wide_b[...]).astype(BF16).reshape(
        plan.frames, plan.fn, c
    )
    a_two, b_two = group_means(totals[2].finish())
    ex_l.wait()
    grads, at = [], 0
    for lift in assemble(ex_l, wide_l[pl.ds(0, plan.n)], inside):
        count = lift.shape[0]
        grads.append(scale_two * (lift - a_two - unit_h[pl.ds(at, count)] * b_two))
        at += count
    grads = clip(grads)
    shifted_grad(plan, moved_h, interior(grads[0]))
    for p in range(3):
        kernel_grad(plan, at_one, moved_h, acc_one, p)
        starts(sums_one, p)
    slot = lax.broadcasted_iota(jnp.int32, (plan.h, SLOT, c), 1)

    leave = [
        pltpu.make_async_copy(stage.at[cells], target, local_sem.at[14 + k])
        for k, (stage, target) in enumerate(((stage_x, block_out), (stage_g, grad_input)))
    ]

    def emit(k, stage):
        mine, theirs = out_refs[k]
        outs[k].wait_recv()
        for f in range(plan.f):
            a = mine[plan.f * spot.t + f].astype(F32).reshape(plan.h, SLOT, c)
            b = theirs[f].astype(F32).reshape(plan.h, SLOT, c)
            low = jnp.where(spot.t == 0, a, b)
            high = jnp.where(spot.t == 0, b, a)
            low = jnp.where(slot < plan.half, low, high)
            for y in range(plan.h):
                at = y * plan.w * plan.f + f
                rows32[pl.ds(at, SLOT, plan.f)] = low[y]
                rows32[pl.ds(at + SLOT * plan.f, plan.w - SLOT, plan.f)] = high[y, 0 : plan.w - SLOT]
        for at in range(0, plan.cells, 8):
            n = min(8, plan.cells - at)
            block = rows32[pl.ds(at * plan.f, n * plan.f)]
            stage[pl.ds(at, n)] = block.reshape(n, plan.f, c).astype(BF16)
        leave[k].start()

    def go(which, *steps):
        parts = dict(one=sums_one, two=sums_two)[which]
        for k, step in steps:
            if k < len(parts):
                getattr(parts[k], step)()

    go("one", (0, "first"))
    place_padded(plan, pad_h, *grads)
    convolve_split(plan, pad_h, turned_one, wide_b, interior, True)
    go("one", (1, "first"), (2, "first"))
    unit = unit_one(flat_block(ex_x))
    lifted = interior(wide_b[...] * slope(unit * gain_one + shift_one) * gain_one)
    wide_l[pl.ds(0, plan.n)] = lifted
    totals[3].start(column_sum(lifted), column_sum(lifted * unit))
    go("two", (1, "second"), (0, "second"), (2, "second"))
    outs[0].start()
    go("two", (0, "third"))
    go("one", (0, "second"), (1, "second"))
    go("two", (1, "third"))
    a_one, b_one = group_means(totals[3].finish())
    unit = unit_one(flat_block(ex_x))
    out_refs[1][0][...] = (
        flat_block(ex_g) + scale_one * (wide_l[pl.ds(0, plan.n)] - a_one - unit * b_one)
    ).astype(BF16).reshape(plan.frames, plan.fn, c)
    outs[1].start()
    go("one", (2, "second"))
    go("two", (2, "third"), (0, "fourth"))
    go("one", (0, "third"), (1, "third"))
    go("two", (1, "fourth"))
    go("one", (2, "third"))
    go("two", (2, "fourth"))
    emit(0, stage_x)
    go("one", (0, "fourth"))
    go("two", (0, "fifth"))
    emit(1, stage_g)
    go("one", (1, "fourth"), (2, "fourth"))
    go("two", (1, "fifth"), (2, "fifth"), (0, "sixth"), (1, "sixth"), (2, "sixth"))
    go("one", (0, "fifth"), (1, "fifth"), (2, "fifth"), (0, "sixth"), (1, "sixth"), (2, "sixth"))
    for item in [ex_x, ex_g, ex_h, ex_l] + totals + sums_two + sums_one:
        item.drain()
    for link in outs:
        link.wait_send()
    for copy in leave:
        copy.wait()


def split_kernel(plan, features, cotangent, kernel_one, kernel_two, *norms):
    c, n = plan.c, plan.n
    frames, fn = plan.frames, plan.fn
    vm = pltpu.VMEM
    halos = []
    for k in range(4):
        edge = plan.f * plan.hs if k < 2 else plan.ext
        halos += [
            vm((frames, fn, c), BF16),
            vm((2, edge, c), BF16),
            vm((frames, SLOT, c), BF16),
            vm((frames, SLOT, c), BF16),
            vm((3, 2 * plan.ext, c), BF16),
        ]
    count = plan.ntm * plan.nrow * plan.ncol - 1
    hbm = pl.BlockSpec(memory_space=pltpu.HBM)
    pads = plan.frames * plan.pn + SLOT
    return pl.pallas_call(
        functools.partial(split_body, plan),
        out_shape=(
            jax.ShapeDtypeStruct(features.shape, BF16),
            jax.ShapeDtypeStruct(features.shape, BF16),
            jax.ShapeDtypeStruct((plan.taps_rows, c), BF16),
            jax.ShapeDtypeStruct((plan.taps_rows, c), BF16),
        ),
        in_specs=[hbm] * 8,
        out_specs=(hbm,) * 4,
        scratch_shapes=[vm((plan.f * plan.h * plan.wide + 2 * plan.wide, c), F32)]
        + [vm((plan.cells_up * plan.f, c), F32)]
        + [vm((plan.cells_up, plan.f, c), BF16)] * 2
        + [vm((plan.sum_rows, c), BF16)] * 2
        + [vm((n + SLOT, c), F32)] * 2
        + [vm((n, c), F32)]
        + [vm((n + 2 * frames * SLOT, c), F32)]
        + [vm((n, 2 * plan.ext), BF16)]
        + [vm((frames * SLOT, 2 * plan.ext), BF16)] * 2
        + [vm((9, c, 3 * c), BF16)] * 4
        + [vm((pads, c), BF16)] * 4
        + [vm((3 * c, frames * plan.gn), BF16)] * 2
        + [vm((frames * plan.gn, 3 * c), BF16)] * 2
        + [vm((plan.sum_rows, c), F32)] * 2
        + [vm((1, c), F32)] * 4
        + [vm((2, plan.f, fn, c), BF16)] * 2
        + halos
        + [vm((8, c), F32), vm((count, 8, c), F32)] * 4
        + part_scratch(plan)
        + [vm((frames, fn, c), BF16), vm((plan.f, fn, c), BF16)] * 2
        + [pltpu.SemaphoreType.DMA((MANY,))] * 2
        + [pltpu.SemaphoreType.DMA((32,))],
        compiler_params=pltpu.CompilerParams(
            collective_id=0, has_side_effects=True, vmem_limit_bytes=VMEM_ASK
        ),
    )(features, cotangent, kernel_one, kernel_two, *norms)


def widen_body(parts, *refs):
    ins, outs, narrow, wide, held, sems = refs[:4], refs[4:8], *refs[8:]
    moves = [pltpu.make_async_copy(ins[k], held.at[k], sems.at[0, k]) for k in range(2)]
    leave = [pltpu.make_async_copy(held.at[k], outs[k], sems.at[0, 2 + k]) for k in range(2)]
    loads, stores = [], []
    for a in range(2):
        for j, (at, count) in enumerate(parts):
            rows = pl.ds(at, count)
            k = len(parts) * a + j
            loads.append(
                pltpu.make_async_copy(ins[2 + a].at[rows], narrow.at[a, rows], sems.at[1, k])
            )
            stores.append(
                pltpu.make_async_copy(wide.at[a, rows], outs[2 + a].at[rows], sems.at[2, k])
            )
    for copy in loads[: len(parts)] + moves + loads[len(parts) :]:
        copy.start()
    for a in range(2):
        for j, (at, count) in enumerate(parts):
            k = len(parts) * a + j
            loads[k].wait()
            wide[a, pl.ds(at, count)] = narrow[a, pl.ds(at, count)].astype(F32)
            stores[k].start()
        moves[a].wait()
        leave[a].start()
    for copy in stores + leave:
        copy.wait()


def widen(block_out, grad_input, part_one, part_two):
    rows, c = part_one.shape
    piece = -(-rows // 64) * 16
    parts = [(at, min(piece, rows - at)) for at in range(0, rows, piece)]
    hbm = pl.BlockSpec(memory_space=pltpu.HBM)
    shape = jax.ShapeDtypeStruct
    return pl.pallas_call(
        functools.partial(widen_body, parts),
        out_shape=(
            shape(block_out.shape, BF16),
            shape(grad_input.shape, BF16),
            shape((rows, c), F32),
            shape((rows, c), F32),
        ),
        in_specs=[hbm] * 4,
        out_specs=(hbm,) * 4,
        scratch_shapes=[
            pltpu.VMEM((2, rows, c), BF16),
            pltpu.VMEM((2, rows, c), F32),
            pltpu.VMEM((2,) + block_out.shape, BF16),
            pltpu.SemaphoreType.DMA((3, 2 * len(parts))),
        ],
        compiler_params=pltpu.CompilerParams(vmem_limit_bytes=VMEM_ASK),
    )(block_out, grad_input, part_one, part_two)


def local_split(plan, features, cotangent, conv_one, conv_two, *norms):
    c = plan.c
    norms = [v.reshape(1, c) for v in norms]
    shape = (9, 3, c, c)
    turn = lambda v: v.transpose(1, 2, 0, 3).reshape(plan.cells, plan.f, c)
    back = lambda v: v.reshape(plan.h, plan.w, plan.f, c).transpose(2, 0, 1, 3)
    block_out, grad_input, part_one, part_two = widen(
        *split_kernel(
            plan, turn(features), turn(cotangent), conv_one.reshape(shape), conv_two.reshape(shape), *norms
        )
    )
    return (
        back(block_out),
        back(grad_input),
        part_one.reshape(conv_one.shape),
        part_two.reshape(conv_two.shape),
    )


def local(features, cotangent, conv_one, conv_two, gain_one, shift_one, gain_two, shift_two):
    f, h, w, c = features.shape
    sizes = tuple(lax.axis_size(a) for a in AXES)
    if Split.fits(f, h, w, c, sizes):
        return local_split(
            Split(f, h, w, c, sizes), features, cotangent, conv_one, conv_two,
            gain_one, shift_one, gain_two, shift_two,
        )
    plan = Plan(f, h, w, c, sizes)
    norms = [v.reshape(1, c) for v in (gain_one, shift_one, gain_two, shift_two)]
    block_out, grad_input, part_one, part_two = block_kernel(
        plan, features, cotangent, conv_one.reshape(-1, c), conv_two.reshape(-1, c), *norms
    )
    return (
        block_out,
        grad_input,
        part_one.astype(F32).reshape(conv_one.shape),
        part_two.astype(F32).reshape(conv_two.shape),
    )


def solution(mesh):
    block = P("tm", "row", "col", None)
    return jax.shard_map(
        local,
        mesh=mesh,
        in_specs=(block, block) + (P(),) * 6,
        out_specs=(block, block, P(), P()),
        check_vma=False,
    )
```
